32 devices in a mesh: seq: 8 (over z, x), kvh: 2 (over core), batch: 2 (over y).
Axes of the slice: x: 2, y: 2, z: 4, core: 2. Of those that a mesh axis runs over, the one named last changes fastest.
Arguments:
- queries: bfloat16 [8, 512, 3584], P('batch', 'seq', 'kvh'), parts along dimension 0, may hold values from -160 to 160
- text_keys: bfloat16 [8, 512, 512], P('batch', 'seq', 'kvh'), parts along dimension 0, may hold values from -6 to 6
- text_values: bfloat16 [8, 512, 512], P('batch', 'seq', 'kvh'), parts along dimension 0, may hold values from -6 to 6
- visual_keys: bfloat16 [32, 729, 512], P(('batch', 'seq'), None, 'kvh'), parts along dimension 0, may hold values from -6 to 6
- visual_values: bfloat16 [32, 729, 512], P(('batch', 'seq'), None, 'kvh'), parts along dimension 0, may hold values from -6 to 6
- gate_weight: float32 [3584, 28], P('kvh'), may hold values from -0.1875 to 0.1875
- text_offsets: int32 [16], P('batch'), parts along dimension 0, may hold values from 0 to 448, as said below
- image_sequence: int32 [32], P('batch'), parts along dimension 0, may hold values from 0 to 3, as said below
- image_position: int32 [32], P('batch'), parts along dimension 0, may hold values from 0 to 511, as said below
Outputs:
- combined: bfloat16 [8, 512, 3584], P('batch', 'seq', 'kvh'), parts along dimension 0
The draws below stay inside these ranges and needn't reach their ends.
There are 2 independent parts, one for each index of `batch`. The reference program is written for one: setup_inputs(seed, part) draws one part's arguments, and reference() takes and returns one part's arrays. A program takes and returns all parts, laid end to end along the dimension named above; an argument that names none is the same for every part. Nothing has to cross between parts.
Inputs may be any that keep to these rules, and one draw needn't show every extreme that they name: A permutation of the multiples of 64 below 512: text block j holds the positions text_offsets[j] to text_offsets[j] + 63. `image_sequence`: each of the 4 sequences owns exactly 4 images. `image_position`: every sequence has an image at position 0.
All inputs are finite; a program needn't handle non-finite values.
Results may differ from the reference program's by a relative error of at most 0.0039.
Values may be sent and summed in bfloat16 or wider, within the bound.
A program may use at most 128 MiB of HBM per device.

```python
import jax
import jax.numpy as jnp
from jax import lax

HQ = 28
KVH = 4
DH = 128
VTOK = 729
TOK_DEV = 64
SEQS = 4
IMG_SEQ = 4
GROUP = 7
SHARDS = 8
L = 512
IMAGES = 16


def layout_order(key):
    return jax.random.permutation(jax.random.fold_in(key, 101), SHARDS).astype(jnp.int32)


def image_plan(key):
    shuffled = jax.random.permutation(jax.random.fold_in(key, 202), IMAGES).astype(jnp.int32)
    owners = (shuffled % SEQS).astype(jnp.int32)
    places = jax.random.randint(jax.random.fold_in(key, 203), (IMAGES,), 1, L, dtype=jnp.int32)
    places = jnp.where(shuffled < SEQS, 0, places).astype(jnp.int32)
    return (owners, places)


def text_key_base(key):
    return jnp.clip(jax.random.normal(jax.random.fold_in(key, 11), (SEQS, L, KVH * DH), jnp.float32), -6.0, 6.0)


def visual_key_base(key):
    return jnp.clip(jax.random.normal(jax.random.fold_in(key, 12), (IMAGES, VTOK, KVH * DH), jnp.float32), -6.0, 6.0)


def draw_text_offsets(key, part):
    return (layout_order(key) * TOK_DEV).astype(jnp.int32)


def draw_image_sequence(key, part):
    return image_plan(key)[0]


def draw_image_position(key, part):
    return image_plan(key)[1]


def draw_text_keys(key, part):
    drawn = text_key_base(key)
    return drawn.astype(jnp.bfloat16)


def draw_visual_keys(key, part):
    drawn = visual_key_base(key)
    return drawn.astype(jnp.bfloat16)


def draw_queries(key, part):
    drawn = jnp.clip(jax.random.normal(jax.random.fold_in(key, 13), (SEQS, L, HQ * DH), jnp.float32), -6.0, 6.0)
    return drawn.astype(jnp.bfloat16)


def steps_of(rng, dims, cuts, smallest, largest):
    level, own = 1.0, jax.random.fold_in(rng, 6)
    for dim, blocks in cuts:
        draws = jnp.exp(jax.random.uniform(jax.random.fold_in(own, dim), (blocks,), jnp.float32, smallest / len(cuts), largest / len(cuts)))
        level = level * jnp.repeat(draws, dims[dim] // blocks).reshape([-1 if axis == dim else 1 for axis in range(len(dims))])
    return level


def gaussian(own_key, extent, width, bound, pieces=(), kind=jnp.bfloat16):
    values = width * jax.random.normal(own_key, extent, jnp.float32)
    if pieces:
        values = values * steps_of(own_key, extent, pieces, -0.22, 0.18)
    return jnp.clip(values, -bound, bound).astype(kind)


def setup_inputs(seed: int = 0, part: int = 0) -> dict:
    arg_keys = jax.random.split(jax.random.key(seed), 10)
    part_splits = jax.random.split(jax.random.fold_in(arg_keys[9], part), 10)
    return {
        "queries": draw_queries(jax.random.fold_in(jax.random.fold_in(arg_keys[9], part), 71), part),
        "text_keys": draw_text_keys(jax.random.fold_in(jax.random.fold_in(arg_keys[9], part), 71), part),
        "text_values": gaussian(part_splits[2], (SEQS, L, KVH * DH), 1.0, 6.0, ((1, 8), (2, 2))),
        "visual_keys": draw_visual_keys(jax.random.fold_in(jax.random.fold_in(arg_keys[9], part), 71), part),
        "visual_values": gaussian(part_splits[4], (IMAGES, VTOK, KVH * DH), 1.0, 6.0, ((0, 8), (2, 2))),
        "gate_weight": gaussian(arg_keys[5], (HQ * DH, HQ), (HQ * DH // 4) ** -0.5, 0.1875, ((0, 2),), jnp.float32),
        "text_offsets": draw_text_offsets(jax.random.fold_in(jax.random.fold_in(arg_keys[9], part), 71), part),
        "image_sequence": draw_image_sequence(jax.random.fold_in(jax.random.fold_in(arg_keys[9], part), 71), part),
        "image_position": draw_image_position(jax.random.fold_in(jax.random.fold_in(arg_keys[9], part), 71), part),
    }


NEG = -1.0e30


def block_stats(query_rows, key_blocks, value_blocks, visible):
    scaling = 1.0 / (query_rows.shape[-1] ** 0.5)
    scores = jnp.einsum("tghe,bkge->tghbk", query_rows.astype(jnp.float32), key_blocks.astype(jnp.float32), precision=lax.Precision.HIGHEST) * scaling
    allowed = visible[:, None, None, :, :]
    scores = jnp.where(allowed, scores, NEG)
    block_peak = jnp.max(scores, axis=-1)
    unnormed = jnp.where(allowed, jnp.exp(scores - block_peak[..., None]), 0.0)
    block_total = jnp.sum(unnormed, axis=-1)
    rounded = lax.optimization_barrier(unnormed.astype(jnp.bfloat16)).astype(jnp.float32)
    block_sum = jnp.einsum("tghbk,bkge->tghbe", rounded, value_blocks.astype(jnp.float32), precision=lax.Precision.HIGHEST)
    return block_peak, block_total, block_sum


def finish(block_peak, block_total, block_sum):
    overall = jnp.max(block_peak, axis=-1)
    weights = jnp.exp(block_peak - overall[..., None])
    numerator = jnp.sum(weights[..., None] * block_sum, axis=-2)
    denominator = jnp.sum(weights * block_total, axis=-1)
    return numerator / denominator[..., None]


def reference(queries, text_keys, text_values, visual_keys, visual_values, gate_weight, text_offsets, image_sequence, image_position):
    length = queries.shape[1]
    shaped = queries.reshape(SEQS, length, KVH, GROUP, DH)
    rows_all = jnp.arange(length, dtype=jnp.int32)
    positions = (text_offsets[rows_all // TOK_DEV] + rows_all % TOK_DEV).astype(jnp.int32)
    gate_logits = jnp.dot(queries.astype(jnp.float32).reshape(SEQS * length, HQ * DH), gate_weight, precision=lax.Precision.HIGHEST)
    gate = jax.nn.sigmoid(gate_logits).reshape(SEQS, length, KVH, GROUP)
    key_pos = (text_offsets[:, None] + jnp.arange(TOK_DEV, dtype=jnp.int32)[None, :]).astype(jnp.int32)
    text_visible = key_pos[None, :, :] <= positions[:, None, None]
    key_blocks = text_keys.reshape(SEQS, SHARDS, TOK_DEV, KVH, DH)
    value_blocks = text_values.reshape(SEQS, SHARDS, TOK_DEV, KVH, DH)

    def text_one(members):
        query_rows, keys_here, values_here = members
        return finish(*block_stats(query_rows, keys_here, values_here, text_visible))

    text_out = lax.map(text_one, (shaped, key_blocks, value_blocks))
    order = jnp.argsort(image_sequence, stable=True).reshape(SEQS, IMG_SEQ)
    image_keys = visual_keys.reshape(IMAGES, VTOK, KVH, DH)[order]
    image_values = visual_values.reshape(IMAGES, VTOK, KVH, DH)[order]
    image_places = image_position[order]

    def visual_one(members):
        query_rows, keys_here, values_here, places_here = members
        visible = jnp.broadcast_to(places_here[None, :, None] <= positions[:, None, None], (length, IMG_SEQ, VTOK))
        return finish(*block_stats(query_rows, keys_here, values_here, visible))

    visual_out = lax.map(visual_one, (shaped, image_keys, image_values, image_places))
    mixed = (1.0 - gate)[..., None] * text_out + gate[..., None] * visual_out
    return mixed.reshape(SEQS, length, HQ * DH).astype(jnp.bfloat16)
```

```python
import functools
import math

import jax
import jax.numpy as jnp
from jax import lax
from jax.experimental import pallas as pl
from jax.experimental.pallas import tpu as pltpu
from jax.sharding import PartitionSpec as P

DH = 128
GROUP = 7
LANES = 128
HALF = LANES // 2
CHUNKS = 4
TILE = 16
NEG = -1e30
FLOOR = -1e29
FAR = 1 << 30
SCALE = 1.0 / DH ** 0.5
SCALE2 = SCALE * math.log2(math.e)


def chunks_of(tokens):
    size = -(-tokens // (CHUNKS * TILE)) * TILE
    return [pl.ds(a, min(size, tokens - a)) for a in range(0, tokens, size)]


def heads_of(ref, lead, g):
    start = pl.multiple_of(g * (GROUP * DH), DH)
    return jnp.concatenate(
        [ref[lead, :, pl.ds(start + h * DH, DH)] for h in range(GROUP)], axis=0
    )


def put_heads(ref, lead, g, stacked):
    rows = stacked.shape[0] // GROUP
    start = pl.multiple_of(g * (GROUP * DH), DH)
    for h in range(GROUP):
        ref[(*lead, slice(None), pl.ds(start + h * DH, DH))] = stacked[h * rows:(h + 1) * rows]


def pack_stats(peak, total, rows):
    lane = lax.broadcasted_iota(jnp.int32, (rows, LANES), 1)
    packed = jnp.zeros((rows, LANES), jnp.float32)
    for h in range(GROUP):
        here = slice(h * rows, (h + 1) * rows)
        packed = jnp.where(lane == h, peak[here], packed)
        packed = jnp.where(lane == HALF + h, total[here], packed)
    return packed


def totals_of(packed):
    return pltpu.roll(packed, HALF, 1)


def softmax_parts(q, keys, values, bias):
    scores = lax.dot_general(
        q, keys, (((1,), (1,)), ((), ())), preferred_element_type=jnp.float32
    )
    if bias is not None:
        rows, count = bias.shape
        scores = (scores.reshape(GROUP, rows, count) + bias[None]).reshape(GROUP * rows, count)
    peak = jnp.maximum(jnp.max(scores, axis=-1, keepdims=True), FLOOR)
    expd = jnp.exp2((scores - peak) * SCALE2)
    total = jnp.sum(expd, axis=-1, keepdims=True)
    num = jnp.dot(expd.astype(jnp.bfloat16), values, preferred_element_type=jnp.float32)
    return peak * SCALE, total, num


def attention_kernel(
    n, heads_split, seqs, rows, groups, here, per_seq,
    offsets, image_sequence, image_position,
    queries, text_keys, text_values, visual_keys, visual_values, gate_weight,
    out_ref,
    q_pair, far_tk, far_tv, far_ik, far_iv, num, stat, cat_k, cat_v,
    t_send, t_stat_send, t_recv, t_stat_recv, v_send, v_stat_send, v_recv, v_stat_recv,
    t_own, t_own_stat, gate_own, gate_recv, gate_buf, send_sems, recv_sems,
):
    me = lax.axis_index("seq")
    core = lax.axis_index("kvh")
    members = n // 4
    blocks = n // 2
    pair = me // 4 * 4 + (me + 2) % 4
    side = me // 2 * 2 + (me + 1) % 2
    others = [(me // 4 + k) % members * 4 + me % 4 for k in range(1, members)]
    twins = [(core + k) % heads_split for k in range(1, heads_split)]

    far_ids = [(me // 4 + members - k) % members * 4 + me % 4 for k in range(1, members)]
    sources = [me, side] + far_ids + [f // 2 * 2 + (f + 1) % 2 for f in far_ids]
    places = [offsets[i] for i in (me, pair, *sources)]
    image_ids = [source * here + j for source in sources for j in range(here)]
    owners = [image_sequence[i] for i in image_ids]
    positions = [image_position[i] for i in image_ids]
    at, thresholds = [], []
    for s in range(seqs):
        slot_here = [jnp.int32(0)] * per_seq
        threshold_here = [jnp.int32(FAR)] * per_seq
        found = jnp.int32(0)
        for slot, (owner, position) in enumerate(zip(owners, positions)):
            hit = owner == s
            for j in range(per_seq):
                take = hit & (found == j)
                slot_here[j] = jnp.where(take, slot, slot_here[j])
                threshold_here[j] = jnp.where(take, position, threshold_here[j])
            found = found + jnp.where(hit, 1, 0)
        at += slot_here
        thresholds += threshold_here

    barrier = pltpu.get_barrier_semaphore()
    for peer in (pair, side, *others):
        pl.semaphore_signal(
            barrier, inc=1, device_id={"seq": peer}, device_id_type=pl.DeviceIdType.MESH
        )
    for twin in twins:
        pl.semaphore_signal(
            barrier, inc=1, device_id={"kvh": twin}, device_id_type=pl.DeviceIdType.MESH
        )
    pl.semaphore_wait(barrier, 2 + len(others) + len(twins))

    copies = []
    chunks = chunks_of(visual_values.shape[1])

    def send(src, dst, peer, axis="seq"):
        copy = pltpu.make_async_remote_copy(
            src_ref=src,
            dst_ref=dst,
            send_sem=send_sems.at[len(copies)],
            recv_sem=recv_sems.at[len(copies)],
            device_id={axis: peer},
            device_id_type=pl.DeviceIdType.MESH,
        )
        copy.start()
        copies.append(copy)
        return copy

    def slot_of(kind, k=0):
        return {"side": 0, "far": k, "diag": members - 1 + k}[kind]

    q_copy = send(queries, q_pair, pair)
    text_far = []
    for k, peer in enumerate(others, 1):
        s = slot_of("far", k)
        text_far.append((send(text_keys, far_tk.at[s], peer), send(text_values, far_tv.at[s], peer)))
    text_side = (send(text_keys, far_tk.at[0], side), send(text_values, far_tv.at[0], side))
    image_far = {}
    image_side = {}
    for j in range(here):
        for k, peer in enumerate(others, 1):
            s = slot_of("far", k)
            image_far[k, j] = [send(visual_keys.at[j], far_ik.at[s, j], peer)] + [
                send(visual_values.at[j, cut], far_iv.at[s, j, cut], peer) for cut in chunks
            ]
        image_side[j] = (
            send(visual_keys.at[j], far_ik.at[0, j], side),
            send(visual_values.at[j], far_iv.at[0, j], side),
        )

    def attend(keys, values, index, sides):
        owner = owners[index]

        def step(g, carry):
            at_g = pl.ds(pl.multiple_of(g * DH, DH), DH)
            k, v = keys[:, at_g], values[:, at_g]
            for which in sides:
                q = heads_of(queries if which == 0 else q_pair, owner, g)
                peak, total, out = softmax_parts(q, k, v, None)
                put_heads(num, (index, which), g, out)
                stat[index, which, g] = pack_stats(peak, total, rows)
            return carry

        lax.fori_loop(0, groups, step, 0)

    rest = gate_weight[...]
    q_all = queries[...].reshape(seqs * rows, queries.shape[-1])
    logits = 0.0
    for _ in range(3):
        term = rest.astype(jnp.bfloat16)
        rest = rest - term.astype(jnp.float32)
        logits = logits + lax.dot_general(
            q_all, term, (((1,), (1,)), ((), ())), preferred_element_type=jnp.float32
        )
    gate_own[...] = logits.reshape(gate_own.shape)
    t_stat_send[...] = jnp.zeros_like(t_stat_send)
    v_stat_send[...] = jnp.zeros_like(v_stat_send)

    for j in range(here):
        attend(visual_keys.at[j], visual_values.at[j], j, (0,))
    gates = [send(gate_own, gate_recv.at[k], twin, "kvh") for k, twin in enumerate(twins)]

    text_diag = []
    for k, pieces in enumerate(text_far, 1):
        for piece in pieces:
            piece.wait_recv()
        s, d = slot_of("far", k), slot_of("diag", k)
        text_diag.append((
            send(far_tk.at[s], far_tk.at[d], side), send(far_tv.at[s], far_tv.at[d], side)
        ))

    q_copy.wait_recv()
    for j in range(here):
        attend(visual_keys.at[j], visual_values.at[j], j, (1,))

    for piece in (*text_side, *[p for pieces in text_diag for p in pieces]):
        piece.wait_recv()
    for b in range(blocks):
        span = pl.ds(b * rows, rows)
        cat_k[:, span, :] = text_keys[...] if b == 0 else far_tk[b - 1]
        cat_v[:, span, :] = text_values[...] if b == 0 else far_tv[b - 1]
    count = blocks * rows
    lane = lax.broadcasted_iota(jnp.int32, (rows, count), 1)
    row = lax.broadcasted_iota(jnp.int32, (rows, count), 0)
    key_pos = lane % rows
    for b in range(blocks):
        inside = (lane >= b * rows) & (lane < (b + 1) * rows)
        key_pos = key_pos + jnp.where(inside, places[2 + b], 0)
    biases = [jnp.where(key_pos <= row + places[which], 0.0, NEG) for which in (0, 1)]

    def text_step(i, carry):
        s, g = i // groups, i % groups
        at_g = pl.ds(pl.multiple_of(g * DH, DH), DH)
        k, v = cat_k[s, :, at_g], cat_v[s, :, at_g]
        peak, total, out = softmax_parts(heads_of(queries, s, g), k, v, biases[0])
        put_heads(t_own, (s,), g, out)
        t_own_stat[s, g] = pack_stats(peak, total, rows)
        peak, total, out = softmax_parts(heads_of(q_pair, s, g), k, v, biases[1])
        out = out * (1.0 / jnp.where(total > 0.0, total, 1.0))
        put_heads(t_send, (s,), g, out.astype(jnp.bfloat16))
        t_stat_send[s] = t_stat_send[s] + pltpu.roll(pack_stats(peak, total, rows), g * 8, 1)
        return carry

    lax.fori_loop(0, seqs * groups, text_step, 0)
    text_back = (send(t_send, t_recv, pair), send(t_stat_send, t_stat_recv, pair))

    image_diag = {}

    def forward(j):
        for k in range(1, members):
            s, d = slot_of("far", k), slot_of("diag", k)
            pieces = image_far[k, j]
            pieces[0].wait_recv()
            image_diag[k, j] = [send(far_ik.at[s, j], far_ik.at[d, j], side)]
            for cut, piece in zip(chunks, pieces[1:]):
                piece.wait_recv()
                image_diag[k, j].append(send(far_iv.at[s, j, cut], far_iv.at[d, j, cut], side))

    def attend_far(slot, j, sides=(1, 0)):
        attend(far_ik.at[slot, j], far_iv.at[slot, j], (slot + 1) * here + j, sides)

    for j in range(here):
        for piece in image_side[j]:
            piece.wait_recv()
        attend_far(0, j)
    for j in range(here):
        forward(j)
        for k in range(1, members):
            attend_far(slot_of("far", k), j)
        for k in range(1, members):
            for piece in image_diag[k, j]:
                piece.wait_recv()
            last = j == here - 1 and k == members - 1
            attend_far(slot_of("diag", k), j, (1,) if last else (1, 0))

    row_pos = lax.broadcasted_iota(jnp.int32, (rows, LANES), 0)

    def visual_weights(s, g, which):
        seen, packed = [], []
        for j in range(per_seq):
            seen.append(thresholds[s * per_seq + j] <= row_pos + places[which])
            packed.append(stat[at[s * per_seq + j], which, g])
        peaks = [jnp.where(a, p, NEG) for a, p in zip(seen, packed)]
        overall = functools.reduce(jnp.maximum, peaks)
        weights = [jnp.where(a, jnp.exp(p - overall), 0.0) for a, p in zip(seen, peaks)]
        total = sum(w * totals_of(p) for w, p in zip(weights, packed))
        return overall, total, weights

    def weighted(s, g, which, h, weights):
        start = pl.multiple_of(g * (GROUP * DH), DH)
        return sum(
            w[:, h:h + 1] * num[at[s * per_seq + j], which, :, pl.ds(start + h * DH, DH)]
            for j, w in enumerate(weights)
        )

    def stat_lanes(overall, total):
        lane_id = lax.broadcasted_iota(jnp.int32, (rows, LANES), 1)
        packed = jnp.where(lane_id < HALF, overall, pltpu.roll(total, HALF, 1))
        return jnp.where(lane_id % HALF < GROUP, packed, 0.0)

    visual_back = []
    for s in range(seqs):
        def pair_step(g, carry, s=s):
            overall, total, weights = visual_weights(s, g, 1)
            inverse = 1.0 / jnp.where(total > 0.0, total, 1.0)
            weights = [w * inverse for w in weights]
            start = pl.multiple_of(g * (GROUP * DH), DH)
            for h in range(GROUP):
                v_send[s, :, pl.ds(start + h * DH, DH)] = weighted(s, g, 1, h, weights).astype(
                    jnp.bfloat16
                )
            v_stat_send[s] = v_stat_send[s] + pltpu.roll(stat_lanes(overall, total), g * 8, 1)
            return carry

        lax.fori_loop(0, groups, pair_step, 0)
        visual_back.append((
            send(v_send.at[s], v_recv.at[s], pair), send(v_stat_send.at[s], v_stat_recv.at[s], pair)
        ))

    attend_far(slot_of("diag", members - 1), here - 1, (0,))

    for piece in gates:
        piece.wait_recv()
    for s in range(seqs):
        logits = gate_own[s]
        for k in range(len(twins)):
            logits = logits + gate_recv[k, s]
        heads = groups * GROUP
        mine = logits[:, :heads]
        for c in range(1, heads_split):
            mine = jnp.where(core == c, logits[:, c * heads:(c + 1) * heads], mine)
        mine = jax.nn.sigmoid(mine)
        for g in range(groups):
            gate_buf[s, g, :, :GROUP] = mine[:, g * GROUP:(g + 1) * GROUP]

    for piece in text_back:
        piece.wait_recv()

    def unpacked(packed, g):
        return pltpu.roll(packed, LANES - g * 8, 1)

    def text_merge(i, carry):
        s, g = i // groups, i % groups
        ours, theirs = t_own_stat[s, g], unpacked(t_stat_recv[s], g)
        overall = jnp.maximum(ours, theirs)
        weight_a = jnp.exp(ours - overall)
        weight_b = jnp.exp(theirs - overall) * totals_of(theirs)
        inverse = 1.0 / (weight_a * totals_of(ours) + weight_b)
        weight_a, weight_b = weight_a * inverse, weight_b * inverse
        start = pl.multiple_of(g * (GROUP * DH), DH)
        for h in range(GROUP):
            cut = pl.ds(start + h * DH, DH)
            t_own[s, :, cut] = weight_a[:, h:h + 1] * t_own[s, :, cut] + weight_b[
                :, h:h + 1
            ] * t_recv[s, :, cut].astype(jnp.float32)
        return carry

    lax.fori_loop(0, seqs * groups, text_merge, 0)

    for s in range(seqs):
        for piece in visual_back[s]:
            piece.wait_recv()

        def own_step(g, carry, s=s):
            overall, total, weights = visual_weights(s, g, 0)
            theirs = unpacked(v_stat_recv[s], g)
            joint = jnp.maximum(overall, theirs)
            weight_a = jnp.exp(overall - joint)
            weight_b = jnp.exp(theirs - joint) * totals_of(theirs)
            inverse = 1.0 / (weight_a * total + weight_b)
            weights = [w * (weight_a * inverse) for w in weights]
            weight_b = weight_b * inverse
            start = pl.multiple_of(g * (GROUP * DH), DH)
            for h in range(GROUP):
                cut = pl.ds(start + h * DH, DH)
                visual = weighted(s, g, 0, h, weights) + weight_b[:, h:h + 1] * v_recv[
                    s, :, cut
                ].astype(jnp.float32)
                gate = gate_buf[s, g, :, h:h + 1]
                out_ref[s, :, cut] = ((1.0 - gate) * t_own[s, :, cut] + gate * visual).astype(
                    jnp.bfloat16
                )
            return carry

        lax.fori_loop(0, groups, own_step, 0)

    for copy in copies:
        copy.wait_send()


def pair_plan(n, heads_split, queries, text_keys, text_values, visual_keys, visual_values,
              gate_weight, text_offsets, image_sequence, image_position):
    seqs, rows, columns = queries.shape
    groups = text_keys.shape[-1] // DH
    here, tokens, kv_columns = visual_keys.shape
    members, blocks = n // 4, n // 2
    slots = blocks * here
    per_seq = image_sequence.shape[0] // seqs
    smem = pl.BlockSpec(memory_space=pltpu.SMEM)
    vmem = pl.BlockSpec(memory_space=pltpu.VMEM)
    bf16, f32 = jnp.bfloat16, jnp.float32
    count = 1 + 4 * (members - 1) + 2 + here * (2 * (members - 1) * (1 + len(chunks_of(tokens))) + 2) + 2 + 2 * seqs + heads_split - 1
    stats = (seqs, groups, rows, LANES)
    sent_stats = (seqs, rows, LANES)
    gate_shape = (seqs, rows, gate_weight.shape[-1])
    pairs = 2 * rows * GROUP * groups * (slots * tokens + seqs * blocks * rows)
    return pl.pallas_call(
        functools.partial(attention_kernel, n, heads_split, seqs, rows, groups, here, per_seq),
        in_specs=[smem] * 3 + [vmem] * 6,
        out_specs=vmem,
        out_shape=jax.ShapeDtypeStruct(queries.shape, bf16),
        scratch_shapes=[
            pltpu.VMEM(queries.shape, bf16),
            pltpu.VMEM((blocks - 1, *text_keys.shape), bf16),
            pltpu.VMEM((blocks - 1, *text_keys.shape), bf16),
            pltpu.VMEM((blocks - 1, *visual_keys.shape), bf16),
            pltpu.VMEM((blocks - 1, *visual_keys.shape), bf16),
            pltpu.VMEM((slots, 2, rows, columns), f32),
            pltpu.VMEM((slots, 2, groups, rows, LANES), f32),
            pltpu.VMEM((seqs, blocks * rows, kv_columns), bf16),
            pltpu.VMEM((seqs, blocks * rows, kv_columns), bf16),
            pltpu.VMEM(queries.shape, bf16),
            pltpu.VMEM(sent_stats, f32),
            pltpu.VMEM(queries.shape, bf16),
            pltpu.VMEM(sent_stats, f32),
            pltpu.VMEM(queries.shape, bf16),
            pltpu.VMEM(sent_stats, f32),
            pltpu.VMEM(queries.shape, bf16),
            pltpu.VMEM(sent_stats, f32),
            pltpu.VMEM(queries.shape, f32),
            pltpu.VMEM(stats, f32),
            pltpu.VMEM(gate_shape, f32),
            pltpu.VMEM((heads_split - 1, *gate_shape), f32),
            pltpu.VMEM(stats, f32),
            pltpu.SemaphoreType.DMA((count,)),
            pltpu.SemaphoreType.DMA((count,)),
        ],
        compiler_params=pltpu.CompilerParams(
            collective_id=0, has_side_effects=True, vmem_limit_bytes=60 << 20
        ),
        cost_estimate=pl.CostEstimate(
            flops=4 * pairs * DH, bytes_accessed=16 << 20, transcendentals=pairs
        ),
    )(
        text_offsets, image_sequence, image_position,
        queries, text_keys, text_values, visual_keys, visual_values, gate_weight.T,
    )


def line_kernel(
    seqs, rows, here, per_seq, heads_split,
    offsets, image_sequence, image_position,
    queries, text_keys, text_values, visual_keys, visual_values, gate_weight,
    out_ref,
    q_own, q_mate, q_out, tkv, tkv_out, vk, vv, part, part_mate, stat, stat_mate,
    side_part, side_stat, t_own, t_send, t_recv,
    gate_own, gate_recv, gate_buf, weights, send_sems, recv_sems,
):
    me = lax.axis_index("seq")
    core = lax.axis_index("kvh")
    z, x = me // 2, me % 2
    half = z // 2
    inner = (z + 1) // 2 % 2
    side = z * 2 + 1 - x
    mate = (half * 2 + 1 - z % 2) * 2 + x
    cross = (3 - z) * 2 + x
    twins = [(core + k) % heads_split for k in range(1, heads_split)]
    width = GROUP * DH
    group = 2 * here
    slots = 4 * group
    near, outer, across, far = 0, 1, 2, 3
    mine = 1 - inner

    def chip(kind):
        place = jnp.where(kind == outer, 3 * half, 1 + half)
        place = jnp.where(kind == across, 2 - half, place)
        return jnp.where(kind == far, 3 - 3 * half, place)

    def device(kind, sub):
        return chip(kind) * 2 + (x + sub) % 2

    def image_of(slot):
        return device(slot // group, slot // here % 2) * here + slot % here

    owners = [image_sequence[image_of(jnp.int32(i))] for i in range(slots)]
    positions = [image_position[image_of(jnp.int32(i))] for i in range(slots)]
    at, thresholds = [], []
    for s in range(seqs):
        slot_here = [jnp.int32(0)] * per_seq
        threshold_here = [jnp.int32(FAR)] * per_seq
        found = jnp.int32(0)
        for slot, (owner, position) in enumerate(zip(owners, positions)):
            hit = owner == s
            for j in range(per_seq):
                take = hit & (found == j)
                slot_here[j] = jnp.where(take, slot, slot_here[j])
                threshold_here[j] = jnp.where(take, position, threshold_here[j])
            found = found + jnp.where(hit, 1, 0)
        at += slot_here
        thresholds += threshold_here

    barrier = pltpu.get_barrier_semaphore()
    for peer in (side, mate, cross):
        pl.semaphore_signal(
            barrier, inc=1, device_id={"seq": peer}, device_id_type=pl.DeviceIdType.MESH
        )
    for twin in twins:
        pl.semaphore_signal(
            barrier, inc=1, device_id={"kvh": twin}, device_id_type=pl.DeviceIdType.MESH
        )

    bases, used = {}, 0
    for name, count in (
        ("x_text", 1), ("x_q", 1), ("x_k", here), ("x_v", here), ("x_t", 1), ("x_part", slots),
        ("x_stat", slots), ("m_text", 8), ("m_q", 2), ("m_k", slots), ("m_v", slots),
        ("m_part", slots), ("m_stat", slots), ("c_text", 8), ("c_k", slots), ("c_v", slots),
        ("gate", heads_split),
    ):
        bases[name] = used
        used += count

    def copy(name, index, src, dst, peer, axis="seq"):
        return pltpu.make_async_remote_copy(
            src_ref=src,
            dst_ref=dst,
            send_sem=send_sems.at[bases[name] + index],
            recv_sem=recv_sems.at[bases[name] + index],
            device_id={axis: peer},
            device_id_type=pl.DeviceIdType.MESH,
        )

    x_text = copy("x_text", 0, tkv_out, tkv.at[mine, 1], side)
    x_q = copy("x_q", 0, q_out, q_own.at[:, 1], side)
    away = pl.multiple_of((1 - x) * DH, DH)

    def x_k(j):
        return copy("x_k", j, visual_keys.at[j, :, pl.ds(away, DH)], vk.at[mine * group + here + j], side)

    def x_v(j):
        return copy("x_v", j, visual_values.at[j, :, pl.ds(away, DH)], vv.at[mine * group + here + j], side)

    x_t = copy("x_t", 0, t_send, t_recv, side)

    def x_part(i):
        return copy("x_part", i, part.at[i, 1], side_part.at[i], side)

    def x_stat(i):
        return copy("x_stat", i, stat.at[i], side_stat.at[i], side)

    def m_text(kind, sub):
        return copy("m_text", kind * 2 + sub, tkv.at[kind, sub], tkv.at[kind, sub], mate)

    def m_q(sub):
        return copy("m_q", sub, q_own.at[:, sub], q_mate.at[:, sub], mate)

    def m_k(i):
        return copy("m_k", i, vk.at[i], vk.at[i], mate)

    def m_v(i):
        return copy("m_v", i, vv.at[i], vv.at[i], mate)

    def m_part(i):
        return copy("m_part", i, part_mate.at[i], part.at[i], mate)

    def m_stat(i):
        return copy("m_stat", i, stat_mate.at[i], stat.at[i], mate)

    def c_text(kind, sub):
        return copy("c_text", (kind + 2) * 2 + sub, tkv.at[kind, sub], tkv.at[kind + 2, sub], cross)

    def c_k(i):
        return copy("c_k", i, vk.at[i], vk.at[i + 2 * group], cross)

    def c_v(i):
        return copy("c_v", i, vv.at[i], vv.at[i + 2 * group], cross)

    home = pl.multiple_of(x * DH, DH)
    home_q = x * width
    away_q = (1 - x) * width

    def stack_q(s, carry):
        for h in range(GROUP):
            q_own[s, 0, h] = queries[s, :, pl.ds(pl.multiple_of(home_q + h * DH, DH), DH)]
            q_out[s, h] = queries[s, :, pl.ds(pl.multiple_of(away_q + h * DH, DH), DH)]
        return carry

    for kind, source in enumerate((text_keys, text_values)):
        tkv[mine, 0, kind] = source[:, :, pl.ds(home, DH)]
        tkv_out[kind] = source[:, :, pl.ds(away, DH)]
    lax.fori_loop(0, seqs, stack_q, 0)
    for j in range(here):
        vk[mine * group + j] = visual_keys[j, :, pl.ds(home, DH)]
        vv[mine * group + j] = visual_values[j, :, pl.ds(home, DH)]

    pl.semaphore_wait(barrier, 3 + len(twins))

    x_text.start()
    x_q.start()
    for j in range(here):
        x_k(j).start()
        x_v(j).start()

    @pl.when(inner == 1)
    def _():
        c_text(near, 0).start()
        m_text(near, 0).start()
        c_k(0).start()
        c_v(0).start()

    @pl.when(inner == 0)
    def _():
        m_text(outer, 0).start()

    rest = gate_weight[...]
    q_all = queries[...].reshape(seqs * rows, queries.shape[-1])
    logits = 0.0
    for _ in range(3):
        term = rest.astype(jnp.bfloat16)
        rest = rest - term.astype(jnp.float32)
        logits = logits + lax.dot_general(
            q_all, term, (((1,), (1,)), ((), ())), preferred_element_type=jnp.float32
        )
    gate_own[...] = logits.reshape(gate_own.shape)
    gates = [copy("gate", k, gate_own, gate_recv.at[k], twin, "kvh") for k, twin in enumerate(twins)]
    for piece in gates:
        piece.start()

    lane = lax.broadcasted_iota(jnp.int32, (rows, LANES), 1)

    def softmax(scores):
        peak = jnp.max(scores, axis=-1, keepdims=True)
        return peak, jnp.exp2((scores - peak) * SCALE2).astype(jnp.bfloat16)

    def scores_of(q, k):
        return lax.dot_general(q, k, (((1,), (1,)), ((), ())), preferred_element_type=jnp.float32)

    def attend(i, q_ref, part_ref, stat_ref):
        q = q_ref[image_sequence[image_of(i)]].reshape(2, GROUP * rows, DH)
        k, v = vk[i], vv[i]
        v = jnp.concatenate([v, jnp.ones_like(v)], axis=1)
        scores = [scores_of(q[0], k), scores_of(q[1], k)]
        packed = []
        for b in range(2):
            peak, expd = softmax(scores[b])
            num = jnp.dot(expd, v, preferred_element_type=jnp.float32)
            total = num[:, DH:]
            part_ref[i, b] = (num[:, :DH] * (1.0 / total)).astype(jnp.bfloat16).reshape(GROUP, rows, DH)
            peaks = jnp.zeros((rows, LANES), jnp.float32)
            totals = jnp.ones((rows, LANES), jnp.float32)
            for h in range(GROUP):
                at_h = slice(h * rows, (h + 1) * rows)
                peaks = jnp.where(lane == h, peak[at_h], peaks)
                totals = jnp.where(lane == h, total[at_h], totals)
            packed.append(peaks * SCALE + jnp.log(totals))
        stat_ref[i] = jnp.concatenate(packed, axis=0).T[:8]

    def attend_own(i):
        attend(i, q_own, part, stat)
        x_part(i).start()
        x_stat(i).start()

    def attend_mate(i):
        attend(i, q_mate, part_mate, stat_mate)
        m_part(i).start()
        m_stat(i).start()

    def loop(start, stop, body):
        def step(i, carry):
            body(i)
            return carry

        lax.fori_loop(start, stop, step, 0)

    @pl.when(inner == 1)
    def _():
        x_text.wait_recv()
        c_text(near, 1).start()
        m_text(near, 1).start()
        for j in range(here):
            m_k(j).start()
            m_v(j).start()
        for sub in range(2):
            m_text(outer, sub).wait_recv()
            c_text(outer, sub).start()
        for j in range(1, here):
            c_k(j).start()
            c_v(j).start()
        c_text(near, 0).wait_recv()
        m_text(across, 0).start()
        x_q.wait_recv()
        loop(0, here, attend_own)
        c_text(near, 1).wait_recv()
        m_text(across, 1).start()
        x_k(0).wait_recv()
        c_k(here).start()
        for sub in range(2):
            c_text(outer, sub).wait_recv()
            m_text(far, sub).start()
        x_v(0).wait_recv()
        c_v(here).start()

    @pl.when(inner == 0)
    def _():
        x_text.wait_recv()
        m_text(outer, 1).start()
        m_q(0).start()
        x_q.wait_recv()
        m_q(1).start()
        for j in range(here):
            m_k(group + j).start()
            m_v(group + j).start()
        loop(group, group + here, attend_own)
        for j in range(here):
            x_k(j).wait_recv()
            m_k(group + here + j).start()
            x_v(j).wait_recv()
            m_v(group + here + j).start()
        for kind in (near, across, far):
            for sub in range(2):
                m_text(kind, sub).wait_recv()

    count = 8 * rows
    key_lane = lax.broadcasted_iota(jnp.int32, (rows, count), 1)
    key_row = lax.broadcasted_iota(jnp.int32, (rows, count), 0)
    key_pos = key_lane % rows
    for kind in range(4):
        for sub in range(2):
            b = kind * 2 + sub
            inside = (key_lane >= b * rows) & (key_lane < (b + 1) * rows)
            key_pos = key_pos + jnp.where(inside, offsets[device(kind, sub)], 0)
    place = [offsets[me], offsets[side]]
    biases = [jnp.where(key_pos <= key_row + p, 0.0, NEG) for p in place]

    def text_step(s):
        q = q_own[s].reshape(2, GROUP * rows, DH)
        k = tkv[:, :, 0, s].reshape(count, DH)
        v = tkv[:, :, 1, s].reshape(count, DH)
        v = jnp.concatenate([v, jnp.ones_like(v)], axis=1)
        for b in range(2):
            scores = scores_of(q[b], k).reshape(GROUP, rows, count) + biases[b][None]
            peak, expd = softmax(scores.reshape(GROUP * rows, count))
            num = jnp.dot(expd, v, preferred_element_type=jnp.float32)
            out = (num[:, :DH] * (1.0 / num[:, DH:])).reshape(GROUP, rows, DH)
            if b == 0:
                t_own[s] = out
            else:
                t_send[s] = out.astype(jnp.bfloat16)

    loop(0, seqs, text_step)
    x_t.start()

    @pl.when(inner == 1)
    def _():
        for j in range(1, here):
            x_k(j).wait_recv()
            c_k(here + j).start()
            x_v(j).wait_recv()
            c_v(here + j).start()
        for sub in range(2):
            m_q(sub).wait_recv()

        def own_step(i):
            attend_mate(i)
            attend_own(i)

        loop(here, group, own_step)

        def stream_step(c):
            @pl.when((c >= here) & (c < here + group))
            def _():
                o = group + c - here
                m_k(o).wait_recv()
                c_k(o).start()
                m_v(o).wait_recv()
                c_v(o).start()
                attend_own(o)

            c_k(c).wait_recv()
            c_v(c).wait_recv()
            attend_mate(2 * group + c)
            attend_own(2 * group + c)

        loop(0, 2 * group, stream_step)

    @pl.when(inner == 0)
    def _():
        loop(group + here, 2 * group, attend_own)
        for j in range(here):
            m_k(j).wait_recv()
            m_v(j).wait_recv()
        loop(0, here, attend_own)

        def forward(i):
            m_part(i).wait_recv()
            m_stat(i).wait_recv()
            x_part(i).start()
            x_stat(i).start()

        loop(here, group, forward)
        loop(2 * group, 4 * group, forward)

    for piece in gates:
        piece.wait_recv()
    for s in range(seqs):
        logits = gate_own[s]
        for k in range(len(twins)):
            logits = logits + gate_recv[k, s]
        heads = 2 * GROUP
        mix = logits[:, :heads]
        for c in range(1, heads_split):
            mix = jnp.where(core == c, logits[:, c * heads:(c + 1) * heads], mix)
        mix = jax.nn.sigmoid(mix)
        for g in range(2):
            gate_buf[s, g, :, :GROUP] = mix[:, g * GROUP:(g + 1) * GROUP]
    x_t.wait_recv()

    def receive(i):
        x_part(i).wait_recv()
        x_stat(i).wait_recv()

    loop(0, slots, receive)

    row_pos = lax.broadcasted_iota(jnp.int32, (rows, LANES), 0) + place[0]
    limits = jnp.full((rows, LANES), FAR, jnp.int32)
    for i, threshold in enumerate(thresholds):
        limits = jnp.where(lane // 8 == i, threshold, limits)
    seen = (limits <= row_pos) & (lane % 8 < GROUP)

    def across_images(values, join):
        stride = 8
        while stride < 8 * per_seq:
            up = pltpu.roll(values, LANES - stride, 1)
            down = pltpu.roll(values, stride, 1)
            values = join(values, jnp.where(lane // stride % 2 == 0, up, down))
            stride *= 2
        return values

    at_side = [i + here * (1 - 2 * (i // here % 2)) for i in at]

    for g in range(2):
        source = (stat, side_stat)[g]
        gathered = jnp.concatenate([source[i] for i in (at, at_side)[g]], axis=0).T
        lse = jnp.where(seen, gathered[g * rows:(g + 1) * rows], NEG)
        overall = across_images(lse, jnp.maximum)
        weight = jnp.where(seen, jnp.exp(lse - overall), 0.0)
        total = across_images(weight, jnp.add)
        weights[g] = weight * (1.0 / jnp.where(total > 0.0, total, 1.0))

    for g in range(2):
        absolute = x if g == 0 else 1 - x
        for s in range(seqs):
            gate_here = gate_buf[s, absolute]
            for h in range(GROUP):
                visual = 0.0
                for j in range(per_seq):
                    i = (at, at_side)[g][s * per_seq + j]
                    piece = part[i, 0, h] if g == 0 else side_part[i, h]
                    k = (s * per_seq + j) * 8 + h
                    visual = visual + weights[g, :, k:k + 1] * piece.astype(jnp.float32)
                text = t_own[s, h] if g == 0 else t_recv[s, h].astype(jnp.float32)
                gate = gate_here[:, h:h + 1]
                cut = pl.ds(pl.multiple_of(absolute * width + h * DH, DH), DH)
                out_ref[s, :, cut] = ((1.0 - gate) * text + gate * visual).astype(jnp.bfloat16)

    def sent(piece):
        piece.wait_send()

    sent(x_text)
    sent(x_q)
    sent(x_t)
    for j in range(here):
        sent(x_k(j))
        sent(x_v(j))
    for piece in gates:
        sent(piece)

    def all_sent(i):
        sent(x_part(i))
        sent(x_stat(i))

    loop(0, slots, all_sent)

    @pl.when(inner == 1)
    def _():
        for sub in range(2):
            for kind in (near, outer):
                sent(c_text(kind, sub))
            for kind in (near, across, far):
                sent(m_text(kind, sub))
        for j in range(here):
            sent(m_k(j))
            sent(m_v(j))

        def stream_sent(i):
            sent(c_k(i))
            sent(c_v(i))

        def mate_sent(i):
            sent(m_part(i))
            sent(m_stat(i))

        loop(0, 2 * group, stream_sent)
        loop(here, group, mate_sent)
        loop(2 * group, 4 * group, mate_sent)

    @pl.when(inner == 0)
    def _():
        for sub in range(2):
            sent(m_text(outer, sub))
            sent(m_q(sub))

        def stream_sent(i):
            sent(m_k(i))
            sent(m_v(i))

        loop(group, 2 * group, stream_sent)


def line_plan(heads_split, queries, text_keys, text_values, visual_keys, visual_values,
              gate_weight, text_offsets, image_sequence, image_position):
    seqs, rows, columns = queries.shape
    here, tokens, _ = visual_keys.shape
    slots = image_sequence.shape[0]
    per_seq = slots // seqs
    smem = pl.BlockSpec(memory_space=pltpu.SMEM)
    vmem = pl.BlockSpec(memory_space=pltpu.VMEM)
    bf16, f32 = jnp.bfloat16, jnp.float32
    stacked = (seqs, 2, GROUP, rows, DH)
    one = (seqs, GROUP, rows, DH)
    gate_shape = (seqs, rows, gate_weight.shape[-1])
    count = 2 + 2 * here + 1 + 2 * slots + 10 + 4 * slots + 8 + 2 * slots + heads_split
    pairs = 2 * rows * GROUP * (2 * slots * tokens + seqs * 8 * rows)
    return pl.pallas_call(
        functools.partial(line_kernel, seqs, rows, here, per_seq, heads_split),
        in_specs=[smem] * 3 + [vmem] * 6,
        out_specs=vmem,
        out_shape=jax.ShapeDtypeStruct(queries.shape, bf16),
        scratch_shapes=[
            pltpu.VMEM(stacked, bf16),
            pltpu.VMEM(stacked, bf16),
            pltpu.VMEM(one, bf16),
            pltpu.VMEM((4, 2, 2, seqs, rows, DH), bf16),
            pltpu.VMEM((2, seqs, rows, DH), bf16),
            pltpu.VMEM((slots, tokens, DH), bf16),
            pltpu.VMEM((slots, tokens, DH), bf16),
            pltpu.VMEM((slots, 2, GROUP, rows, DH), bf16),
            pltpu.VMEM((slots, 2, GROUP, rows, DH), bf16),
            pltpu.VMEM((slots, 8, LANES), f32),
            pltpu.VMEM((slots, 8, LANES), f32),
            pltpu.VMEM((slots, GROUP, rows, DH), bf16),
            pltpu.VMEM((slots, 8, LANES), f32),
            pltpu.VMEM(one, f32),
            pltpu.VMEM(one, bf16),
            pltpu.VMEM(one, bf16),
            pltpu.VMEM(gate_shape, f32),
            pltpu.VMEM((heads_split - 1, *gate_shape), f32),
            pltpu.VMEM((seqs, 2, rows, LANES), f32),
            pltpu.VMEM((2, rows, LANES), f32),
            pltpu.SemaphoreType.DMA((count,)),
            pltpu.SemaphoreType.DMA((count,)),
        ],
        compiler_params=pltpu.CompilerParams(
            collective_id=1, has_side_effects=True, vmem_limit_bytes=60 << 20
        ),
        cost_estimate=pl.CostEstimate(
            flops=4 * pairs * DH, bytes_accessed=16 << 20, transcendentals=pairs
        ),
    )(
        text_offsets, image_sequence, image_position,
        queries, text_keys, text_values, visual_keys, visual_values, gate_weight.T,
    )


def on_device(n, heads_split, queries, text_keys, *rest):
    groups = text_keys.shape[-1] // DH
    images = rest[-2].shape[0]
    line = n // 2
    if line - 2 == 2 and groups == 2 and images * 8 == LANES and 2 * queries.shape[1] == LANES:
        return line_plan(heads_split, queries, text_keys, *rest)
    return pair_plan(n, heads_split, queries, text_keys, *rest)


def solution(mesh):
    return jax.shard_map(
        functools.partial(on_device, mesh.shape["seq"], mesh.shape["kvh"]),
        mesh=mesh,
        in_specs=(
            P("batch", "seq", "kvh"),
            P("batch", "seq", "kvh"),
            P("batch", "seq", "kvh"),
            P(("batch", "seq"), None, "kvh"),
            P(("batch", "seq"), None, "kvh"),
            P("kvh", None),
            P("batch"),
            P("batch"),
            P("batch"),
        ),
        out_specs=P("batch", "seq", "kvh"),
        check_vma=False,
    )
```

```python
import functools
import math

import jax
import jax.numpy as jnp
from jax import lax
from jax.experimental import pallas as pl
from jax.experimental.pallas import tpu as pltpu
from jax.sharding import PartitionSpec as P

DH = 128
GROUP = 7
LANES = 128
HALF = LANES // 2
CHUNKS = 4
TILE = 16
NEG = -1e30
FLOOR = -1e29
FAR = 1 << 30
SCALE = 1.0 / DH ** 0.5
SCALE2 = SCALE * math.log2(math.e)


def chunks_of(tokens):
    size = -(-tokens // (CHUNKS * TILE)) * TILE
    return [pl.ds(a, min(size, tokens - a)) for a in range(0, tokens, size)]


def heads_of(ref, lead, g):
    start = pl.multiple_of(g * (GROUP * DH), DH)
    return jnp.concatenate(
        [ref[lead, :, pl.ds(start + h * DH, DH)] for h in range(GROUP)], axis=0
    )


def put_heads(ref, lead, g, stacked):
    rows = stacked.shape[0] // GROUP
    start = pl.multiple_of(g * (GROUP * DH), DH)
    for h in range(GROUP):
        ref[(*lead, slice(None), pl.ds(start + h * DH, DH))] = stacked[h * rows:(h + 1) * rows]


def pack_stats(peak, total, rows):
    lane = lax.broadcasted_iota(jnp.int32, (rows, LANES), 1)
    packed = jnp.zeros((rows, LANES), jnp.float32)
    for h in range(GROUP):
        here = slice(h * rows, (h + 1) * rows)
        packed = jnp.where(lane == h, peak[here], packed)
        packed = jnp.where(lane == HALF + h, total[here], packed)
    return packed


def totals_of(packed):
    return pltpu.roll(packed, HALF, 1)


def softmax_parts(q, keys, values, bias):
    scores = lax.dot_general(
        q, keys, (((1,), (1,)), ((), ())), preferred_element_type=jnp.float32
    )
    if bias is not None:
        rows, count = bias.shape
        scores = (scores.reshape(GROUP, rows, count) + bias[None]).reshape(GROUP * rows, count)
    peak = jnp.maximum(jnp.max(scores, axis=-1, keepdims=True), FLOOR)
    expd = jnp.exp2((scores - peak) * SCALE2)
    total = jnp.sum(expd, axis=-1, keepdims=True)
    num = jnp.dot(expd.astype(jnp.bfloat16), values, preferred_element_type=jnp.float32)
    return peak * SCALE, total, num


def attention_kernel(
    n, heads_split, seqs, rows, groups, here, per_seq,
    offsets, image_sequence, image_position,
    queries, text_keys, text_values, visual_keys, visual_values, gate_weight,
    out_ref,
    q_pair, far_tk, far_tv, far_ik, far_iv, num, stat, cat_k, cat_v,
    t_send, t_stat_send, t_recv, t_stat_recv, v_send, v_stat_send, v_recv, v_stat_recv,
    t_own, t_own_stat, gate_own, gate_recv, gate_buf, send_sems, recv_sems,
):
    me = lax.axis_index("seq")
    core = lax.axis_index("kvh")
    members = n // 4
    blocks = n // 2
    pair = me // 4 * 4 + (me + 2) % 4
    side = me // 2 * 2 + (me + 1) % 2
    others = [(me // 4 + k) % members * 4 + me % 4 for k in range(1, members)]
    twins = [(core + k) % heads_split for k in range(1, heads_split)]

    far_ids = [(me // 4 + members - k) % members * 4 + me % 4 for k in range(1, members)]
    sources = [me, side] + far_ids + [f // 2 * 2 + (f + 1) % 2 for f in far_ids]
    places = [offsets[i] for i in (me, pair, *sources)]
    image_ids = [source * here + j for source in sources for j in range(here)]
    owners = [image_sequence[i] for i in image_ids]
    positions = [image_position[i] for i in image_ids]
    at, thresholds = [], []
    for s in range(seqs):
        slot_here = [jnp.int32(0)] * per_seq
        threshold_here = [jnp.int32(FAR)] * per_seq
        found = jnp.int32(0)
        for slot, (owner, position) in enumerate(zip(owners, positions)):
            hit = owner == s
            for j in range(per_seq):
                take = hit & (found == j)
                slot_here[j] = jnp.where(take, slot, slot_here[j])
                threshold_here[j] = jnp.where(take, position, threshold_here[j])
            found = found + jnp.where(hit, 1, 0)
        at += slot_here
        thresholds += threshold_here

    barrier = pltpu.get_barrier_semaphore()
    for peer in (pair, side, *others):
        pl.semaphore_signal(
            barrier, inc=1, device_id={"seq": peer}, device_id_type=pl.DeviceIdType.MESH
        )
    for twin in twins:
        pl.semaphore_signal(
            barrier, inc=1, device_id={"kvh": twin}, device_id_type=pl.DeviceIdType.MESH
        )
    pl.semaphore_wait(barrier, 2 + len(others) + len(twins))

    copies = []
    chunks = chunks_of(visual_values.shape[1])

    def send(src, dst, peer, axis="seq"):
        copy = pltpu.make_async_remote_copy(
            src_ref=src,
            dst_ref=dst,
            send_sem=send_sems.at[len(copies)],
            recv_sem=recv_sems.at[len(copies)],
            device_id={axis: peer},
            device_id_type=pl.DeviceIdType.MESH,
        )
        copy.start()
        copies.append(copy)
        return copy

    def slot_of(kind, k=0):
        return {"side": 0, "far": k, "diag": members - 1 + k}[kind]

    q_copy = send(queries, q_pair, pair)
    text_far = []
    for k, peer in enumerate(others, 1):
        s = slot_of("far", k)
        text_far.append((send(text_keys, far_tk.at[s], peer), send(text_values, far_tv.at[s], peer)))
    text_side = (send(text_keys, far_tk.at[0], side), send(text_values, far_tv.at[0], side))
    image_far = {}
    image_side = {}
    for j in range(here):
        for k, peer in enumerate(others, 1):
            s = slot_of("far", k)
            image_far[k, j] = [send(visual_keys.at[j], far_ik.at[s, j], peer)] + [
                send(visual_values.at[j, cut], far_iv.at[s, j, cut], peer) for cut in chunks
            ]
        image_side[j] = (
            send(visual_keys.at[j], far_ik.at[0, j], side),
            send(visual_values.at[j], far_iv.at[0, j], side),
        )

    def attend(keys, values, index, sides):
        owner = owners[index]

        def step(g, carry):
            at_g = pl.ds(pl.multiple_of(g * DH, DH), DH)
            k, v = keys[:, at_g], values[:, at_g]
            for which in sides:
                q = heads_of(queries if which == 0 else q_pair, owner, g)
                peak, total, out = softmax_parts(q, k, v, None)
                put_heads(num, (index, which), g, out)
                stat[index, which, g] = pack_stats(peak, total, rows)
            return carry

        lax.fori_loop(0, groups, step, 0)

    rest = gate_weight[...]
    q_all = queries[...].reshape(seqs * rows, queries.shape[-1])
    logits = 0.0
    for _ in range(3):
        term = rest.astype(jnp.bfloat16)
        rest = rest - term.astype(jnp.float32)
        logits = logits + lax.dot_general(
            q_all, term, (((1,), (1,)), ((), ())), preferred_element_type=jnp.float32
        )
    gate_own[...] = logits.reshape(gate_own.shape)
    t_stat_send[...] = jnp.zeros_like(t_stat_send)
    v_stat_send[...] = jnp.zeros_like(v_stat_send)

    for j in range(here):
        attend(visual_keys.at[j], visual_values.at[j], j, (0,))
    gates = [send(gate_own, gate_recv.at[k], twin, "kvh") for k, twin in enumerate(twins)]

    text_diag = []
    for k, pieces in enumerate(text_far, 1):
        for piece in pieces:
            piece.wait_recv()
        s, d = slot_of("far", k), slot_of("diag", k)
        text_diag.append((
            send(far_tk.at[s], far_tk.at[d], side), send(far_tv.at[s], far_tv.at[d], side)
        ))

    q_copy.wait_recv()
    for j in range(here):
        attend(visual_keys.at[j], visual_values.at[j], j, (1,))

    for piece in (*text_side, *[p for pieces in text_diag for p in pieces]):
        piece.wait_recv()
    for b in range(blocks):
        span = pl.ds(b * rows, rows)
        cat_k[:, span, :] = text_keys[...] if b == 0 else far_tk[b - 1]
        cat_v[:, span, :] = text_values[...] if b == 0 else far_tv[b - 1]
    count = blocks * rows
    lane = lax.broadcasted_iota(jnp.int32, (rows, count), 1)
    row = lax.broadcasted_iota(jnp.int32, (rows, count), 0)
    key_pos = lane % rows
    for b in range(blocks):
        inside = (lane >= b * rows) & (lane < (b + 1) * rows)
        key_pos = key_pos + jnp.where(inside, places[2 + b], 0)
    biases = [jnp.where(key_pos <= row + places[which], 0.0, NEG) for which in (0, 1)]

    def text_step(i, carry):
        s, g = i // groups, i % groups
        at_g = pl.ds(pl.multiple_of(g * DH, DH), DH)
        k, v = cat_k[s, :, at_g], cat_v[s, :, at_g]
        peak, total, out = softmax_parts(heads_of(queries, s, g), k, v, biases[0])
        put_heads(t_own, (s,), g, out)
        t_own_stat[s, g] = pack_stats(peak, total, rows)
        peak, total, out = softmax_parts(heads_of(q_pair, s, g), k, v, biases[1])
        out = out * (1.0 / jnp.where(total > 0.0, total, 1.0))
        put_heads(t_send, (s,), g, out.astype(jnp.bfloat16))
        t_stat_send[s] = t_stat_send[s] + pltpu.roll(pack_stats(peak, total, rows), g * 8, 1)
        return carry

    lax.fori_loop(0, seqs * groups, text_step, 0)
    text_back = (send(t_send, t_recv, pair), send(t_stat_send, t_stat_recv, pair))

    image_diag = {}

    def forward(j):
        for k in range(1, members):
            s, d = slot_of("far", k), slot_of("diag", k)
            pieces = image_far[k, j]
            pieces[0].wait_recv()
            image_diag[k, j] = [send(far_ik.at[s, j], far_ik.at[d, j], side)]
            for cut, piece in zip(chunks, pieces[1:]):
                piece.wait_recv()
                image_diag[k, j].append(send(far_iv.at[s, j, cut], far_iv.at[d, j, cut], side))

    def attend_far(slot, j, sides=(1, 0)):
        attend(far_ik.at[slot, j], far_iv.at[slot, j], (slot + 1) * here + j, sides)

    for j in range(here):
        for piece in image_side[j]:
            piece.wait_recv()
        attend_far(0, j)
    for j in range(here):
        forward(j)
        for k in range(1, members):
            attend_far(slot_of("far", k), j)
        for k in range(1, members):
            for piece in image_diag[k, j]:
                piece.wait_recv()
            last = j == here - 1 and k == members - 1
            attend_far(slot_of("diag", k), j, (1,) if last else (1, 0))

    row_pos = lax.broadcasted_iota(jnp.int32, (rows, LANES), 0)

    def visual_weights(s, g, which):
        seen, packed = [], []
        for j in range(per_seq):
            seen.append(thresholds[s * per_seq + j] <= row_pos + places[which])
            packed.append(stat[at[s * per_seq + j], which, g])
        peaks = [jnp.where(a, p, NEG) for a, p in zip(seen, packed)]
        overall = functools.reduce(jnp.maximum, peaks)
        weights = [jnp.where(a, jnp.exp(p - overall), 0.0) for a, p in zip(seen, peaks)]
        total = sum(w * totals_of(p) for w, p in zip(weights, packed))
        return overall, total, weights

    def weighted(s, g, which, h, weights):
        start = pl.multiple_of(g * (GROUP * DH), DH)
        return sum(
            w[:, h:h + 1] * num[at[s * per_seq + j], which, :, pl.ds(start + h * DH, DH)]
            for j, w in enumerate(weights)
        )

    def stat_lanes(overall, total):
        lane_id = lax.broadcasted_iota(jnp.int32, (rows, LANES), 1)
        packed = jnp.where(lane_id < HALF, overall, pltpu.roll(total, HALF, 1))
        return jnp.where(lane_id % HALF < GROUP, packed, 0.0)

    visual_back = []
    for s in range(seqs):
        def pair_step(g, carry, s=s):
            overall, total, weights = visual_weights(s, g, 1)
            inverse = 1.0 / jnp.where(total > 0.0, total, 1.0)
            weights = [w * inverse for w in weights]
            start = pl.multiple_of(g * (GROUP * DH), DH)
            for h in range(GROUP):
                v_send[s, :, pl.ds(start + h * DH, DH)] = weighted(s, g, 1, h, weights).astype(
                    jnp.bfloat16
                )
            v_stat_send[s] = v_stat_send[s] + pltpu.roll(stat_lanes(overall, total), g * 8, 1)
            return carry

        lax.fori_loop(0, groups, pair_step, 0)
        visual_back.append((
            send(v_send.at[s], v_recv.at[s], pair), send(v_stat_send.at[s], v_stat_recv.at[s], pair)
        ))

    attend_far(slot_of("diag", members - 1), here - 1, (0,))

    for piece in gates:
        piece.wait_recv()
    for s in range(seqs):
        logits = gate_own[s]
        for k in range(len(twins)):
            logits = logits + gate_recv[k, s]
        heads = groups * GROUP
        mine = logits[:, :heads]
        for c in range(1, heads_split):
            mine = jnp.where(core == c, logits[:, c * heads:(c + 1) * heads], mine)
        mine = jax.nn.sigmoid(mine)
        for g in range(groups):
            gate_buf[s, g, :, :GROUP] = mine[:, g * GROUP:(g + 1) * GROUP]

    for piece in text_back:
        piece.wait_recv()

    def unpacked(packed, g):
        return pltpu.roll(packed, LANES - g * 8, 1)

    def text_merge(i, carry):
        s, g = i // groups, i % groups
        ours, theirs = t_own_stat[s, g], unpacked(t_stat_recv[s], g)
        overall = jnp.maximum(ours, theirs)
        weight_a = jnp.exp(ours - overall)
        weight_b = jnp.exp(theirs - overall) * totals_of(theirs)
        inverse = 1.0 / (weight_a * totals_of(ours) + weight_b)
        weight_a, weight_b = weight_a * inverse, weight_b * inverse
        start = pl.multiple_of(g * (GROUP * DH), DH)
        for h in range(GROUP):
            cut = pl.ds(start + h * DH, DH)
            t_own[s, :, cut] = weight_a[:, h:h + 1] * t_own[s, :, cut] + weight_b[
                :, h:h + 1
            ] * t_recv[s, :, cut].astype(jnp.float32)
        return carry

    lax.fori_loop(0, seqs * groups, text_merge, 0)

    for s in range(seqs):
        for piece in visual_back[s]:
            piece.wait_recv()

        def own_step(g, carry, s=s):
            overall, total, weights = visual_weights(s, g, 0)
            theirs = unpacked(v_stat_recv[s], g)
            joint = jnp.maximum(overall, theirs)
            weight_a = jnp.exp(overall - joint)
            weight_b = jnp.exp(theirs - joint) * totals_of(theirs)
            inverse = 1.0 / (weight_a * total + weight_b)
            weights = [w * (weight_a * inverse) for w in weights]
            weight_b = weight_b * inverse
            start = pl.multiple_of(g * (GROUP * DH), DH)
            for h in range(GROUP):
                cut = pl.ds(start + h * DH, DH)
                visual = weighted(s, g, 0, h, weights) + weight_b[:, h:h + 1] * v_recv[
                    s, :, cut
                ].astype(jnp.float32)
                gate = gate_buf[s, g, :, h:h + 1]
                out_ref[s, :, cut] = ((1.0 - gate) * t_own[s, :, cut] + gate * visual).astype(
                    jnp.bfloat16
                )
            return carry

        lax.fori_loop(0, groups, own_step, 0)

    for copy in copies:
        copy.wait_send()


def pair_plan(n, heads_split, queries, text_keys, text_values, visual_keys, visual_values,
              gate_weight, text_offsets, image_sequence, image_position):
    seqs, rows, columns = queries.shape
    groups = text_keys.shape[-1] // DH
    here, tokens, kv_columns = visual_keys.shape
    members, blocks = n // 4, n // 2
    slots = blocks * here
    per_seq = image_sequence.shape[0] // seqs
    smem = pl.BlockSpec(memory_space=pltpu.SMEM)
    vmem = pl.BlockSpec(memory_space=pltpu.VMEM)
    bf16, f32 = jnp.bfloat16, jnp.float32
    count = 1 + 4 * (members - 1) + 2 + here * (2 * (members - 1) * (1 + len(chunks_of(tokens))) + 2) + 2 + 2 * seqs + heads_split - 1
    stats = (seqs, groups, rows, LANES)
    sent_stats = (seqs, rows, LANES)
    gate_shape = (seqs, rows, gate_weight.shape[-1])
    pairs = 2 * rows * GROUP * groups * (slots * tokens + seqs * blocks * rows)
    return pl.pallas_call(
        functools.partial(attention_kernel, n, heads_split, seqs, rows, groups, here, per_seq),
        in_specs=[smem] * 3 + [vmem] * 6,
        out_specs=vmem,
        out_shape=jax.ShapeDtypeStruct(queries.shape, bf16),
        scratch_shapes=[
            pltpu.VMEM(queries.shape, bf16),
            pltpu.VMEM((blocks - 1, *text_keys.shape), bf16),
            pltpu.VMEM((blocks - 1, *text_keys.shape), bf16),
            pltpu.VMEM((blocks - 1, *visual_keys.shape), bf16),
            pltpu.VMEM((blocks - 1, *visual_keys.shape), bf16),
            pltpu.VMEM((slots, 2, rows, columns), f32),
            pltpu.VMEM((slots, 2, groups, rows, LANES), f32),
            pltpu.VMEM((seqs, blocks * rows, kv_columns), bf16),
            pltpu.VMEM((seqs, blocks * rows, kv_columns), bf16),
            pltpu.VMEM(queries.shape, bf16),
            pltpu.VMEM(sent_stats, f32),
            pltpu.VMEM(queries.shape, bf16),
            pltpu.VMEM(sent_stats, f32),
            pltpu.VMEM(queries.shape, bf16),
            pltpu.VMEM(sent_stats, f32),
            pltpu.VMEM(queries.shape, bf16),
            pltpu.VMEM(sent_stats, f32),
            pltpu.VMEM(queries.shape, f32),
            pltpu.VMEM(stats, f32),
            pltpu.VMEM(gate_shape, f32),
            pltpu.VMEM((heads_split - 1, *gate_shape), f32),
            pltpu.VMEM(stats, f32),
            pltpu.SemaphoreType.DMA((count,)),
            pltpu.SemaphoreType.DMA((count,)),
        ],
        compiler_params=pltpu.CompilerParams(
            collective_id=0, has_side_effects=True, vmem_limit_bytes=60 << 20
        ),
        cost_estimate=pl.CostEstimate(
            flops=4 * pairs * DH, bytes_accessed=16 << 20, transcendentals=pairs
        ),
    )(
        text_offsets, image_sequence, image_position,
        queries, text_keys, text_values, visual_keys, visual_values, gate_weight.T,
    )


def line_kernel(
    seqs, rows, here, per_seq, heads_split,
    offsets, image_sequence, image_position,
    queries, text_keys, text_values, visual_keys, visual_values, gate_weight,
    out_ref,
    q_own, q_mate, q_out, tkv, tkv_out, vk, vv, k_out, v_out, part, part_mate, stat, stat_mate,
    side_part, side_stat, late_part, late_mate, late_stat, late_mate_stat, late_side, late_side_stat,
    t_own, t_send, t_recv, early, gate_own, gate_recv, gate_buf, weights, send_sems, recv_sems,
):
    me = lax.axis_index("seq")
    core = lax.axis_index("kvh")
    z, x = me // 2, me % 2
    half = z // 2
    inner = (z + 1) // 2 % 2
    side = z * 2 + 1 - x
    mate = (half * 2 + 1 - z % 2) * 2 + x
    cross = (3 - z) * 2 + x
    diag = (half * 2 + 1 - z % 2) * 2 + 1 - x
    twins = [(core + k) % heads_split for k in range(1, heads_split)]
    width = GROUP * DH
    group = 2 * here
    slots = 4 * group
    near, outer, across, far = 0, 1, 2, 3
    mine = 1 - inner

    def chip(kind):
        place = jnp.where(kind == outer, 3 * half, 1 + half)
        place = jnp.where(kind == across, 2 - half, place)
        return jnp.where(kind == far, 3 - 3 * half, place)

    def device(kind, sub):
        return chip(kind) * 2 + (x + sub) % 2

    def image_of(slot):
        return device(slot // group, slot // here % 2) * here + slot % here

    owners = [image_sequence[image_of(jnp.int32(i))] for i in range(slots)]
    positions = [image_position[image_of(jnp.int32(i))] for i in range(slots)]
    last = slots - 1
    lates = (last, last - here)

    def table(late):
        at, thresholds = [], []
        for s in range(seqs):
            slot_here = [jnp.int32(0)] * per_seq
            threshold_here = [jnp.int32(FAR)] * per_seq
            found = jnp.int32(0)
            for slot, (owner, position) in enumerate(zip(owners, positions)):
                if slot == late:
                    continue
                hit = owner == s
                for j in range(per_seq):
                    take = hit & (found == j)
                    slot_here[j] = jnp.where(take, slot, slot_here[j])
                    threshold_here[j] = jnp.where(take, position, threshold_here[j])
                found = found + jnp.where(hit, 1, 0)
            at += slot_here
            thresholds += threshold_here
        return at, thresholds

    tables = [table(late) for late in lates]

    barrier = pltpu.get_barrier_semaphore()
    for peer in (side, mate, cross, diag):
        pl.semaphore_signal(
            barrier, inc=1, device_id={"seq": peer}, device_id_type=pl.DeviceIdType.MESH
        )
    for twin in twins:
        pl.semaphore_signal(
            barrier, inc=1, device_id={"kvh": twin}, device_id_type=pl.DeviceIdType.MESH
        )

    bases, used = {}, 0
    for name, count in (
        ("x_text", 1), ("x_q", 1), ("x_k", here), ("x_v", here), ("x_t", 1), ("x_part", slots),
        ("x_stat", slots), ("late", 6), ("m_text", 8), ("m_q", 2), ("m_k", slots), ("m_v", slots),
        ("m_part", slots), ("m_stat", slots), ("c_text", 8), ("c_k", slots), ("c_v", slots),
        ("gate", heads_split),
    ):
        bases[name] = used
        used += count

    def copy(name, index, src, dst, peer, axis="seq"):
        return pltpu.make_async_remote_copy(
            src_ref=src,
            dst_ref=dst,
            send_sem=send_sems.at[bases[name] + index],
            recv_sem=recv_sems.at[bases[name] + index],
            device_id={axis: peer},
            device_id_type=pl.DeviceIdType.MESH,
        )

    x_text = copy("x_text", 0, tkv_out, tkv.at[mine, 1], side)
    x_q = copy("x_q", 0, q_out, q_own.at[:, 1], side)
    away = pl.multiple_of((1 - x) * DH, DH)

    def x_k(j):
        return copy("x_k", j, k_out.at[j], vk.at[mine * group + here + j], side)

    def x_v(j):
        return copy("x_v", j, v_out.at[j], vv.at[mine * group + here + j], side)

    x_t = copy("x_t", 0, t_send, t_recv, side)

    def x_part(i):
        return copy("x_part", i, part.at[i, 1], side_part.at[i], side)

    def x_stat(i):
        return copy("x_stat", i, stat.at[i], side_stat.at[i], side)

    def m_text(kind, sub):
        return copy("m_text", kind * 2 + sub, tkv.at[kind, sub], tkv.at[kind, sub], mate)

    def m_q(sub):
        return copy("m_q", sub, q_own.at[:, sub], q_mate.at[:, sub], mate)

    def m_k(i):
        return copy("m_k", i, vk.at[i], vk.at[i], mate)

    def m_v(i):
        return copy("m_v", i, vv.at[i], vv.at[i], mate)

    def m_part(i):
        return copy("m_part", i, part_mate.at[i], part.at[i], mate)

    def m_stat(i):
        return copy("m_stat", i, stat_mate.at[i], stat.at[i], mate)

    def c_text(kind, sub):
        return copy("c_text", (kind + 2) * 2 + sub, tkv.at[kind, sub], tkv.at[kind + 2, sub], cross)

    def c_k(i):
        return copy("c_k", i, vk.at[i], vk.at[i + 2 * group], cross)

    def c_v(i):
        return copy("c_v", i, vv.at[i], vv.at[i + 2 * group], cross)

    late_own = (
        copy("late", 0, late_part.at[1], late_side, side),
        copy("late", 1, late_stat, late_side_stat, side),
    )
    late_to_mate = (
        copy("late", 2, late_mate.at[0], late_part.at[0], mate),
        copy("late", 3, late_mate_stat, late_stat, mate),
    )
    late_to_diag = (
        copy("late", 4, late_mate.at[1], late_side, diag),
        copy("late", 5, late_mate_stat, late_side_stat, diag),
    )

    home = pl.multiple_of(x * DH, DH)
    home_q = x * width
    away_q = (1 - x) * width

    def stack_q(s, carry):
        for h in range(GROUP):
            q_own[s, 0, h] = queries[s, :, pl.ds(pl.multiple_of(home_q + h * DH, DH), DH)]
            q_out[s, h] = queries[s, :, pl.ds(pl.multiple_of(away_q + h * DH, DH), DH)]
        return carry

    for kind, source in enumerate((text_keys, text_values)):
        tkv[mine, 0, kind] = source[:, :, pl.ds(home, DH)]
        tkv_out[kind] = source[:, :, pl.ds(away, DH)]
    lax.fori_loop(0, seqs, stack_q, 0)
    def keep_home(j):
        vk[mine * group + j] = visual_keys[:, j, pl.ds(home, DH)]
        vv[mine * group + j] = visual_values[:, j, pl.ds(home, DH)]

    def keep_away(j):
        k_out[j] = visual_keys[:, j, pl.ds(away, DH)]
        v_out[j] = visual_values[:, j, pl.ds(away, DH)]

    keep_home(0)
    pl.semaphore_wait(barrier, 4 + len(twins))

    x_text.start()
    x_q.start()

    @pl.when(inner == 1)
    def _():
        c_text(near, 0).start()
        m_text(near, 0).start()
        c_k(0).start()
        c_v(0).start()

    @pl.when(inner == 0)
    def _():
        m_text(outer, 0).start()
        m_k(group).start()

    for j in range(here):
        if j:
            keep_home(j)
        keep_away(j)
        x_k(j).start()
        x_v(j).start()

    lane = lax.broadcasted_iota(jnp.int32, (rows, LANES), 1)

    def softmax(scores):
        peak = jnp.max(scores, axis=-1, keepdims=True)
        return peak, jnp.exp2((scores - peak) * SCALE2).astype(jnp.bfloat16)

    def scores_of(q, k):
        return lax.dot_general(q, k, (((1,), (1,)), ((), ())), preferred_element_type=jnp.float32)

    def attend(i, q_ref, part_ref, stat_ref):
        attend_to(i, q_ref, part_ref.at[i], stat_ref.at[i])

    def attend_to(i, q_ref, part_ref, stat_ref):
        q = q_ref[image_sequence[image_of(i)]].reshape(2, GROUP * rows, DH)
        k, v = vk[i], vv[i]
        v = jnp.concatenate([v, jnp.ones_like(v)], axis=1)
        scores = [scores_of(q[0], k), scores_of(q[1], k)]
        packed = []
        for b in range(2):
            peak, expd = softmax(scores[b])
            num = jnp.dot(expd, v, preferred_element_type=jnp.float32)
            total = num[:, DH:]
            part_ref[b] = (num[:, :DH] * (1.0 / total)).astype(jnp.bfloat16).reshape(GROUP, rows, DH)
            peaks = jnp.zeros((rows, LANES), jnp.float32)
            totals = jnp.ones((rows, LANES), jnp.float32)
            for h in range(GROUP):
                at_h = slice(h * rows, (h + 1) * rows)
                peaks = jnp.where(lane == h, peak[at_h], peaks)
                totals = jnp.where(lane == h, total[at_h], totals)
            packed.append(peaks * SCALE + jnp.log(totals))
        stat_ref[...] = jnp.concatenate(packed, axis=0).T[:8]

    def attend_own(i):
        attend(i, q_own, part, stat)
        x_part(i).start()
        x_stat(i).start()

    def attend_mate(i):
        attend(i, q_mate, part_mate, stat_mate)
        m_part(i).start()
        m_stat(i).start()

    def loop(start, stop, body):
        def step(i, carry):
            body(i)
            return carry

        lax.fori_loop(start, stop, step, 0)

    @pl.when(inner == 1)
    def _():
        x_text.wait_recv()
        c_text(near, 1).start()
        m_text(near, 1).start()
        for j in range(here):
            m_k(j).start()
            m_v(j).start()
        for sub in range(2):
            m_text(outer, sub).wait_recv()
            c_text(outer, sub).start()
        for j in range(1, here):
            c_k(j).start()
            c_v(j).start()
        c_text(near, 0).wait_recv()
        m_text(across, 0).start()

    @pl.when(inner == 0)
    def _():
        x_text.wait_recv()
        m_text(outer, 1).start()
        m_q(0).start()

    rest = gate_weight[...]
    q_all = queries[...].reshape(seqs * rows, queries.shape[-1])
    logits = 0.0
    for _ in range(3):
        term = rest.astype(jnp.bfloat16)
        rest = rest - term.astype(jnp.float32)
        logits = logits + lax.dot_general(
            q_all, term, (((1,), (1,)), ((), ())), preferred_element_type=jnp.float32
        )
    gate_own[...] = logits.reshape(gate_own.shape)
    gates = [copy("gate", k, gate_own, gate_recv.at[k], twin, "kvh") for k, twin in enumerate(twins)]
    for piece in gates:
        piece.start()


    x_q.wait_recv()

    @pl.when(inner == 1)
    def _():
        loop(0, here, attend_own)
        c_text(near, 1).wait_recv()
        m_text(across, 1).start()
        x_k(0).wait_recv()
        c_k(here).start()
        for sub in range(2):
            c_text(outer, sub).wait_recv()
            m_text(far, sub).start()
        x_v(0).wait_recv()
        c_v(here).start()

    @pl.when(inner == 0)
    def _():
        m_q(1).start()
        m_v(group).start()
        for j in range(1, here):
            m_k(group + j).start()
            m_v(group + j).start()
        loop(group, group + here, attend_own)
        for j in range(here):
            x_k(j).wait_recv()
            m_k(group + here + j).start()
            x_v(j).wait_recv()
            m_v(group + here + j).start()
        for kind in (near, across, far):
            for sub in range(2):
                m_text(kind, sub).wait_recv()

    count = 8 * rows
    key_lane = lax.broadcasted_iota(jnp.int32, (rows, count), 1)
    key_row = lax.broadcasted_iota(jnp.int32, (rows, count), 0)
    key_pos = key_lane % rows
    for kind in range(4):
        for sub in range(2):
            b = kind * 2 + sub
            inside = (key_lane >= b * rows) & (key_lane < (b + 1) * rows)
            key_pos = key_pos + jnp.where(inside, offsets[device(kind, sub)], 0)
    place = [offsets[me], offsets[side]]
    biases = [jnp.where(key_pos <= key_row + p, 0.0, NEG) for p in place]

    def text_step(s):
        q = q_own[s].reshape(2, GROUP * rows, DH)
        k = tkv[:, :, 0, s].reshape(count, DH)
        v = tkv[:, :, 1, s].reshape(count, DH)
        v = jnp.concatenate([v, jnp.ones_like(v)], axis=1)
        for b in range(2):
            scores = scores_of(q[b], k).reshape(GROUP, rows, count) + biases[b][None]
            peak, expd = softmax(scores.reshape(GROUP * rows, count))
            num = jnp.dot(expd, v, preferred_element_type=jnp.float32)
            out = (num[:, :DH] * (1.0 / num[:, DH:])).reshape(GROUP, rows, DH)
            if b == 0:
                t_own[0, s] = out
            else:
                t_send[s] = out.astype(jnp.bfloat16)

    loop(0, seqs, text_step)
    x_t.start()

    @pl.when(inner == 1)
    def _():
        for j in range(1, here):
            x_k(j).wait_recv()
            c_k(here + j).start()
            x_v(j).wait_recv()
            c_v(here + j).start()

    for piece in gates:
        piece.wait_recv()
    for s in range(seqs):
        logits = gate_own[s]
        for k in range(len(twins)):
            logits = logits + gate_recv[k, s]
        heads = 2 * GROUP
        mix = logits[:, :heads]
        for c in range(1, heads_split):
            mix = jnp.where(core == c, logits[:, c * heads:(c + 1) * heads], mix)
        mix = jax.nn.sigmoid(mix)
        for g in range(2):
            gate_buf[s, g, :, :GROUP] = mix[:, g * GROUP:(g + 1) * GROUP]


    @pl.when(inner == 1)
    def _():
        for sub in range(2):
            m_q(sub).wait_recv()

        def own_step(i):
            attend_mate(i)
            attend_own(i)

        loop(here, group, own_step)

        def stream_step(c):
            @pl.when((c >= here) & (c < here + group))
            def _():
                o = group + c - here
                m_k(o).wait_recv()
                c_k(o).start()
                m_v(o).wait_recv()
                c_v(o).start()
                attend_own(o)

            c_k(c).wait_recv()
            c_v(c).wait_recv()
            attend_mate(2 * group + c)
            attend_own(2 * group + c)

        loop(0, 2 * group - 1, stream_step)

    @pl.when(inner == 0)
    def _():
        loop(group + here, 2 * group, attend_own)
        for j in range(here):
            m_k(j).wait_recv()
            m_v(j).wait_recv()
        loop(0, here, attend_own)

        def forward(i):
            m_part(i).wait_recv()
            m_stat(i).wait_recv()
            x_part(i).start()
            x_stat(i).start()

        loop(here, group, forward)
        loop(2 * group, last, forward)


    row_pos = lax.broadcasted_iota(jnp.int32, (rows, LANES), 0) + place[0]
    real = lane % 8 < GROUP

    def spread(values, join):
        stride = 8
        while stride < 8 * per_seq:
            up = pltpu.roll(values, LANES - stride, 1)
            down = pltpu.roll(values, stride, 1)
            values = join(values, jnp.where(lane // stride % 2 == 0, up, down))
            stride *= 2
        return values

    def lanes_of(choices, size):
        limits = jnp.full((rows, LANES), FAR, jnp.int32)
        for i, threshold in enumerate(choices):
            limits = jnp.where(lane // size == i, threshold, limits)
        return (limits <= row_pos) & real

    def early_merge(g):
        absolute = x if g == 0 else 1 - x
        at, thresholds = tables[g]
        if g == 1:
            at = [i + here * (1 - 2 * (i // here % 2)) for i in at]
        seen = lanes_of(thresholds, 8)
        gathered = jnp.concatenate([(stat, side_stat)[g][i] for i in at], axis=0).T
        lse = jnp.where(seen, gathered[g * rows:(g + 1) * rows], NEG)
        overall = spread(lse, jnp.maximum)
        weight = jnp.where(seen, jnp.exp(lse - overall), 0.0)
        total = spread(weight, jnp.add)
        gate = 0.0
        for s in range(seqs):
            here_gate = jnp.where(lane < GROUP, gate_buf[s, absolute], 0.0)
            gate = gate + (pltpu.roll(here_gate, s * per_seq * 8, 1) if s else here_gate)
        gate = spread(gate, jnp.add)
        weights[g, 0] = overall
        weights[g, 1] = total
        weights[g, 2] = gate
        weights[g, 3] = weight * (gate / jnp.where(total > 0.0, total, 1.0))
        for s in range(seqs):
            for h in range(GROUP):
                visual = 0.0
                for j in range(per_seq):
                    i = at[s * per_seq + j]
                    piece = part[i, 0, h] if g == 0 else side_part[i, h]
                    k = (s * per_seq + j) * 8 + h
                    visual = visual + weights[g, 3, :, k:k + 1] * piece.astype(jnp.float32)
                early[g, s, h] = visual
                k = s * per_seq * 8 + h
                text = t_own[g, s, h] if g == 0 else t_recv[s, h].astype(jnp.float32)
                t_own[g, s, h] = (1.0 - weights[g, 2, :, k:k + 1]) * text

    def late_merge(g):
        absolute = x if g == 0 else 1 - x
        late = image_of(jnp.int32(lates[g]))
        limits = [jnp.where(image_sequence[late] == s, image_position[late], FAR) for s in range(seqs)]
        seen = lanes_of(limits, 8 * per_seq)
        source = (late_stat, late_side_stat)[g][...]
        gathered = jnp.concatenate([source] * (LANES // 8), axis=0).T
        lse = jnp.where(seen, gathered[g * rows:(g + 1) * rows], NEG)
        before = weights[g, 0]
        overall = jnp.maximum(before, lse)
        weight_a = jnp.where(weights[g, 1] > 0.0, weights[g, 1] * jnp.exp(before - overall), 0.0)
        weight_b = jnp.where(seen, jnp.exp(lse - overall), 0.0)
        total = weight_a + weight_b
        inverse = 1.0 / jnp.where(total > 0.0, total, 1.0)
        weights[g, 0] = weight_a * inverse
        weights[g, 1] = weight_b * inverse * weights[g, 2]
        for h in range(GROUP):
            piece = (late_part[0, h] if g == 0 else late_side[h]).astype(jnp.float32)
            cut = pl.ds(pl.multiple_of(absolute * width + h * DH, DH), DH)
            for s in range(seqs):
                k = s * per_seq * 8 + h
                out_ref[s, :, cut] = (
                    t_own[g, s, h] + weights[g, 0, :, k:k + 1] * early[g, s, h]
                    + weights[g, 1, :, k:k + 1] * piece
                ).astype(jnp.bfloat16)

    def receive(i):
        x_part(i).wait_recv()
        x_stat(i).wait_recv()

    early_merge(0)

    @pl.when(inner == 1)
    def _():
        c_k(2 * group - 1).wait_recv()
        c_v(2 * group - 1).wait_recv()
        attend_to(last, q_mate, late_mate, late_mate_stat)
        for piece in (*late_to_mate, *late_to_diag):
            piece.start()
        attend_to(last, q_own, late_part, late_stat)
        for piece in late_own:
            piece.start()

    loop(0, last, receive)
    x_t.wait_recv()
    early_merge(1)

    @pl.when(inner == 0)
    def _():
        for piece in late_to_mate:
            piece.wait_recv()

    late_merge(0)

    @pl.when(inner == 0)
    def _():
        for piece in late_to_diag:
            piece.wait_recv()

    @pl.when(inner == 1)
    def _():
        for piece in late_own:
            piece.wait_recv()

    late_merge(1)

    def sent(piece):
        piece.wait_send()

    sent(x_text)
    sent(x_q)
    sent(x_t)
    for j in range(here):
        sent(x_k(j))
        sent(x_v(j))
    for piece in gates:
        sent(piece)

    def all_sent(i):
        sent(x_part(i))
        sent(x_stat(i))

    loop(0, last, all_sent)

    @pl.when(inner == 1)
    def _():
        for sub in range(2):
            for kind in (near, outer):
                sent(c_text(kind, sub))
            for kind in (near, across, far):
                sent(m_text(kind, sub))
        for j in range(here):
            sent(m_k(j))
            sent(m_v(j))

        def stream_sent(i):
            sent(c_k(i))
            sent(c_v(i))

        def mate_sent(i):
            sent(m_part(i))
            sent(m_stat(i))

        loop(0, 2 * group, stream_sent)
        loop(here, group, mate_sent)
        loop(2 * group, last, mate_sent)
        for piece in (*late_to_mate, *late_to_diag, *late_own):
            sent(piece)

    @pl.when(inner == 0)
    def _():
        for sub in range(2):
            sent(m_text(outer, sub))
            sent(m_q(sub))

        def stream_sent(i):
            sent(m_k(i))
            sent(m_v(i))

        loop(group, 2 * group, stream_sent)


def line_plan(heads_split, queries, text_keys, text_values, visual_keys, visual_values,
              gate_weight, text_offsets, image_sequence, image_position):
    seqs, rows, columns = queries.shape
    here, tokens, _ = visual_keys.shape
    slots = image_sequence.shape[0]
    per_seq = slots // seqs
    smem = pl.BlockSpec(memory_space=pltpu.SMEM)
    vmem = pl.BlockSpec(memory_space=pltpu.VMEM)
    bf16, f32 = jnp.bfloat16, jnp.float32
    stacked = (seqs, 2, GROUP, rows, DH)
    one = (seqs, GROUP, rows, DH)
    gate_shape = (seqs, rows, gate_weight.shape[-1])
    count = 2 + 2 * here + 1 + 2 * slots + 6 + 10 + 4 * slots + 8 + 2 * slots + heads_split
    pairs = 2 * rows * GROUP * (2 * slots * tokens + seqs * 8 * rows)
    return pl.pallas_call(
        functools.partial(line_kernel, seqs, rows, here, per_seq, heads_split),
        in_specs=[smem] * 3 + [vmem] * 6,
        out_specs=vmem,
        out_shape=jax.ShapeDtypeStruct(queries.shape, bf16),
        scratch_shapes=[
            pltpu.VMEM(stacked, bf16),
            pltpu.VMEM(stacked, bf16),
            pltpu.VMEM(one, bf16),
            pltpu.VMEM((4, 2, 2, seqs, rows, DH), bf16),
            pltpu.VMEM((2, seqs, rows, DH), bf16),
            pltpu.VMEM((slots, tokens, DH), bf16),
            pltpu.VMEM((slots, tokens, DH), bf16),
            pltpu.VMEM((here, tokens, DH), bf16),
            pltpu.VMEM((here, tokens, DH), bf16),
            pltpu.VMEM((slots, 2, GROUP, rows, DH), bf16),
            pltpu.VMEM((slots, 2, GROUP, rows, DH), bf16),
            pltpu.VMEM((slots, 8, LANES), f32),
            pltpu.VMEM((slots, 8, LANES), f32),
            pltpu.VMEM((slots, GROUP, rows, DH), bf16),
            pltpu.VMEM((slots, 8, LANES), f32),
            pltpu.VMEM((2, GROUP, rows, DH), bf16),
            pltpu.VMEM((2, GROUP, rows, DH), bf16),
            pltpu.VMEM((8, LANES), f32),
            pltpu.VMEM((8, LANES), f32),
            pltpu.VMEM((GROUP, rows, DH), bf16),
            pltpu.VMEM((8, LANES), f32),
            pltpu.VMEM((2, *one), f32),
            pltpu.VMEM(one, bf16),
            pltpu.VMEM(one, bf16),
            pltpu.VMEM((2, *one), f32),
            pltpu.VMEM(gate_shape, f32),
            pltpu.VMEM((heads_split - 1, *gate_shape), f32),
            pltpu.VMEM((seqs, 2, rows, LANES), f32),
            pltpu.VMEM((2, 4, rows, LANES), f32),
            pltpu.SemaphoreType.DMA((count,)),
            pltpu.SemaphoreType.DMA((count,)),
        ],
        compiler_params=pltpu.CompilerParams(
            collective_id=1, has_side_effects=True, vmem_limit_bytes=60 << 20
        ),
        cost_estimate=pl.CostEstimate(
            flops=4 * pairs * DH, bytes_accessed=16 << 20, transcendentals=pairs
        ),
    )(
        text_offsets, image_sequence, image_position,
        queries, text_keys, text_values,
        visual_keys.transpose(1, 0, 2), visual_values.transpose(1, 0, 2), gate_weight.T,
    )


def on_device(n, heads_split, queries, text_keys, *rest):
    groups = text_keys.shape[-1] // DH
    images = rest[-2].shape[0]
    line = n // 2
    if line - 2 == 2 and groups == 2 and images * 8 == LANES and 2 * queries.shape[1] == LANES:
        return line_plan(heads_split, queries, text_keys, *rest)
    return pair_plan(n, heads_split, queries, text_keys, *rest)


def solution(mesh):
    return jax.shard_map(
        functools.partial(on_device, mesh.shape["seq"], mesh.shape["kvh"]),
        mesh=mesh,
        in_specs=(
            P("batch", "seq", "kvh"),
            P("batch", "seq", "kvh"),
            P("batch", "seq", "kvh"),
            P(("batch", "seq"), None, "kvh"),
            P(("batch", "seq"), None, "kvh"),
            P("kvh", None),
            P("batch"),
            P("batch"),
            P("batch"),
        ),
        out_specs=P("batch", "seq", "kvh"),
        check_vma=False,
    )
```

```python
import functools
import math

import jax
import jax.numpy as jnp
from jax import lax
from jax.experimental import pallas as pl
from jax.experimental.pallas import tpu as pltpu
from jax.sharding import PartitionSpec as P

DH = 128
GROUP = 7
LANES = 128
HALF = LANES // 2
CHUNKS = 4
TILE = 16
NEG = -1e30
FLOOR = -1e29
FAR = 1 << 30
SCALE = 1.0 / DH ** 0.5
SCALE2 = SCALE * math.log2(math.e)


def chunks_of(tokens):
    size = -(-tokens // (CHUNKS * TILE)) * TILE
    return [pl.ds(a, min(size, tokens - a)) for a in range(0, tokens, size)]


def heads_of(ref, lead, g):
    start = pl.multiple_of(g * (GROUP * DH), DH)
    return jnp.concatenate(
        [ref[lead, :, pl.ds(start + h * DH, DH)] for h in range(GROUP)], axis=0
    )


def put_heads(ref, lead, g, stacked):
    rows = stacked.shape[0] // GROUP
    start = pl.multiple_of(g * (GROUP * DH), DH)
    for h in range(GROUP):
        ref[(*lead, slice(None), pl.ds(start + h * DH, DH))] = stacked[h * rows:(h + 1) * rows]


def pack_stats(peak, total, rows):
    lane = lax.broadcasted_iota(jnp.int32, (rows, LANES), 1)
    packed = jnp.zeros((rows, LANES), jnp.float32)
    for h in range(GROUP):
        here = slice(h * rows, (h + 1) * rows)
        packed = jnp.where(lane == h, peak[here], packed)
        packed = jnp.where(lane == HALF + h, total[here], packed)
    return packed


def totals_of(packed):
    return pltpu.roll(packed, HALF, 1)


def softmax_parts(q, keys, values, bias):
    scores = lax.dot_general(
        q, keys, (((1,), (1,)), ((), ())), preferred_element_type=jnp.float32
    )
    if bias is not None:
        rows, count = bias.shape
        scores = (scores.reshape(GROUP, rows, count) + bias[None]).reshape(GROUP * rows, count)
    peak = jnp.maximum(jnp.max(scores, axis=-1, keepdims=True), FLOOR)
    expd = jnp.exp2((scores - peak) * SCALE2)
    total = jnp.sum(expd, axis=-1, keepdims=True)
    num = jnp.dot(expd.astype(jnp.bfloat16), values, preferred_element_type=jnp.float32)
    return peak * SCALE, total, num


def attention_kernel(
    n, heads_split, seqs, rows, groups, here, per_seq,
    offsets, image_sequence, image_position,
    queries, text_keys, text_values, visual_keys, visual_values, gate_weight,
    out_ref,
    q_pair, far_tk, far_tv, far_ik, far_iv, num, stat, cat_k, cat_v,
    t_send, t_stat_send, t_recv, t_stat_recv, v_send, v_stat_send, v_recv, v_stat_recv,
    t_own, t_own_stat, gate_own, gate_recv, gate_buf, send_sems, recv_sems,
):
    me = lax.axis_index("seq")
    core = lax.axis_index("kvh")
    members = n // 4
    blocks = n // 2
    pair = me // 4 * 4 + (me + 2) % 4
    side = me // 2 * 2 + (me + 1) % 2
    others = [(me // 4 + k) % members * 4 + me % 4 for k in range(1, members)]
    twins = [(core + k) % heads_split for k in range(1, heads_split)]

    far_ids = [(me // 4 + members - k) % members * 4 + me % 4 for k in range(1, members)]
    sources = [me, side] + far_ids + [f // 2 * 2 + (f + 1) % 2 for f in far_ids]
    places = [offsets[i] for i in (me, pair, *sources)]
    image_ids = [source * here + j for source in sources for j in range(here)]
    owners = [image_sequence[i] for i in image_ids]
    positions = [image_position[i] for i in image_ids]
    at, thresholds = [], []
    for s in range(seqs):
        slot_here = [jnp.int32(0)] * per_seq
        threshold_here = [jnp.int32(FAR)] * per_seq
        found = jnp.int32(0)
        for slot, (owner, position) in enumerate(zip(owners, positions)):
            hit = owner == s
            for j in range(per_seq):
                take = hit & (found == j)
                slot_here[j] = jnp.where(take, slot, slot_here[j])
                threshold_here[j] = jnp.where(take, position, threshold_here[j])
            found = found + jnp.where(hit, 1, 0)
        at += slot_here
        thresholds += threshold_here

    barrier = pltpu.get_barrier_semaphore()
    for peer in (pair, side, *others):
        pl.semaphore_signal(
            barrier, inc=1, device_id={"seq": peer}, device_id_type=pl.DeviceIdType.MESH
        )
    for twin in twins:
        pl.semaphore_signal(
            barrier, inc=1, device_id={"kvh": twin}, device_id_type=pl.DeviceIdType.MESH
        )
    pl.semaphore_wait(barrier, 2 + len(others) + len(twins))

    copies = []
    chunks = chunks_of(visual_values.shape[1])

    def send(src, dst, peer, axis="seq"):
        copy = pltpu.make_async_remote_copy(
            src_ref=src,
            dst_ref=dst,
            send_sem=send_sems.at[len(copies)],
            recv_sem=recv_sems.at[len(copies)],
            device_id={axis: peer},
            device_id_type=pl.DeviceIdType.MESH,
        )
        copy.start()
        copies.append(copy)
        return copy

    def slot_of(kind, k=0):
        return {"side": 0, "far": k, "diag": members - 1 + k}[kind]

    q_copy = send(queries, q_pair, pair)
    text_far = []
    for k, peer in enumerate(others, 1):
        s = slot_of("far", k)
        text_far.append((send(text_keys, far_tk.at[s], peer), send(text_values, far_tv.at[s], peer)))
    text_side = (send(text_keys, far_tk.at[0], side), send(text_values, far_tv.at[0], side))
    image_far = {}
    image_side = {}
    for j in range(here):
        for k, peer in enumerate(others, 1):
            s = slot_of("far", k)
            image_far[k, j] = [send(visual_keys.at[j], far_ik.at[s, j], peer)] + [
                send(visual_values.at[j, cut], far_iv.at[s, j, cut], peer) for cut in chunks
            ]
        image_side[j] = (
            send(visual_keys.at[j], far_ik.at[0, j], side),
            send(visual_values.at[j], far_iv.at[0, j], side),
        )

    def attend(keys, values, index, sides):
        owner = owners[index]

        def step(g, carry):
            at_g = pl.ds(pl.multiple_of(g * DH, DH), DH)
            k, v = keys[:, at_g], values[:, at_g]
            for which in sides:
                q = heads_of(queries if which == 0 else q_pair, owner, g)
                peak, total, out = softmax_parts(q, k, v, None)
                put_heads(num, (index, which), g, out)
                stat[index, which, g] = pack_stats(peak, total, rows)
            return carry

        lax.fori_loop(0, groups, step, 0)

    rest = gate_weight[...]
    q_all = queries[...].reshape(seqs * rows, queries.shape[-1])
    logits = 0.0
    for _ in range(3):
        term = rest.astype(jnp.bfloat16)
        rest = rest - term.astype(jnp.float32)
        logits = logits + lax.dot_general(
            q_all, term, (((1,), (1,)), ((), ())), preferred_element_type=jnp.float32
        )
    gate_own[...] = logits.reshape(gate_own.shape)
    t_stat_send[...] = jnp.zeros_like(t_stat_send)
    v_stat_send[...] = jnp.zeros_like(v_stat_send)

    for j in range(here):
        attend(visual_keys.at[j], visual_values.at[j], j, (0,))
    gates = [send(gate_own, gate_recv.at[k], twin, "kvh") for k, twin in enumerate(twins)]

    text_diag = []
    for k, pieces in enumerate(text_far, 1):
        for piece in pieces:
            piece.wait_recv()
        s, d = slot_of("far", k), slot_of("diag", k)
        text_diag.append((
            send(far_tk.at[s], far_tk.at[d], side), send(far_tv.at[s], far_tv.at[d], side)
        ))

    q_copy.wait_recv()
    for j in range(here):
        attend(visual_keys.at[j], visual_values.at[j], j, (1,))

    for piece in (*text_side, *[p for pieces in text_diag for p in pieces]):
        piece.wait_recv()
    for b in range(blocks):
        span = pl.ds(b * rows, rows)
        cat_k[:, span, :] = text_keys[...] if b == 0 else far_tk[b - 1]
        cat_v[:, span, :] = text_values[...] if b == 0 else far_tv[b - 1]
    count = blocks * rows
    lane = lax.broadcasted_iota(jnp.int32, (rows, count), 1)
    row = lax.broadcasted_iota(jnp.int32, (rows, count), 0)
    key_pos = lane % rows
    for b in range(blocks):
        inside = (lane >= b * rows) & (lane < (b + 1) * rows)
        key_pos = key_pos + jnp.where(inside, places[2 + b], 0)
    biases = [jnp.where(key_pos <= row + places[which], 0.0, NEG) for which in (0, 1)]

    def text_step(i, carry):
        s, g = i // groups, i % groups
        at_g = pl.ds(pl.multiple_of(g * DH, DH), DH)
        k, v = cat_k[s, :, at_g], cat_v[s, :, at_g]
        peak, total, out = softmax_parts(heads_of(queries, s, g), k, v, biases[0])
        put_heads(t_own, (s,), g, out)
        t_own_stat[s, g] = pack_stats(peak, total, rows)
        peak, total, out = softmax_parts(heads_of(q_pair, s, g), k, v, biases[1])
        out = out * (1.0 / jnp.where(total > 0.0, total, 1.0))
        put_heads(t_send, (s,), g, out.astype(jnp.bfloat16))
        t_stat_send[s] = t_stat_send[s] + pltpu.roll(pack_stats(peak, total, rows), g * 8, 1)
        return carry

    lax.fori_loop(0, seqs * groups, text_step, 0)
    text_back = (send(t_send, t_recv, pair), send(t_stat_send, t_stat_recv, pair))

    image_diag = {}

    def forward(j):
        for k in range(1, members):
            s, d = slot_of("far", k), slot_of("diag", k)
            pieces = image_far[k, j]
            pieces[0].wait_recv()
            image_diag[k, j] = [send(far_ik.at[s, j], far_ik.at[d, j], side)]
            for cut, piece in zip(chunks, pieces[1:]):
                piece.wait_recv()
                image_diag[k, j].append(send(far_iv.at[s, j, cut], far_iv.at[d, j, cut], side))

    def attend_far(slot, j, sides=(1, 0)):
        attend(far_ik.at[slot, j], far_iv.at[slot, j], (slot + 1) * here + j, sides)

    for j in range(here):
        for piece in image_side[j]:
            piece.wait_recv()
        attend_far(0, j)
    for j in range(here):
        forward(j)
        for k in range(1, members):
            attend_far(slot_of("far", k), j)
        for k in range(1, members):
            for piece in image_diag[k, j]:
                piece.wait_recv()
            last = j == here - 1 and k == members - 1
            attend_far(slot_of("diag", k), j, (1,) if last else (1, 0))

    row_pos = lax.broadcasted_iota(jnp.int32, (rows, LANES), 0)

    def visual_weights(s, g, which):
        seen, packed = [], []
        for j in range(per_seq):
            seen.append(thresholds[s * per_seq + j] <= row_pos + places[which])
            packed.append(stat[at[s * per_seq + j], which, g])
        peaks = [jnp.where(a, p, NEG) for a, p in zip(seen, packed)]
        overall = functools.reduce(jnp.maximum, peaks)
        weights = [jnp.where(a, jnp.exp(p - overall), 0.0) for a, p in zip(seen, peaks)]
        total = sum(w * totals_of(p) for w, p in zip(weights, packed))
        return overall, total, weights

    def weighted(s, g, which, h, weights):
        start = pl.multiple_of(g * (GROUP * DH), DH)
        return sum(
            w[:, h:h + 1] * num[at[s * per_seq + j], which, :, pl.ds(start + h * DH, DH)]
            for j, w in enumerate(weights)
        )

    def stat_lanes(overall, total):
        lane_id = lax.broadcasted_iota(jnp.int32, (rows, LANES), 1)
        packed = jnp.where(lane_id < HALF, overall, pltpu.roll(total, HALF, 1))
        return jnp.where(lane_id % HALF < GROUP, packed, 0.0)

    visual_back = []
    for s in range(seqs):
        def pair_step(g, carry, s=s):
            overall, total, weights = visual_weights(s, g, 1)
            inverse = 1.0 / jnp.where(total > 0.0, total, 1.0)
            weights = [w * inverse for w in weights]
            start = pl.multiple_of(g * (GROUP * DH), DH)
            for h in range(GROUP):
                v_send[s, :, pl.ds(start + h * DH, DH)] = weighted(s, g, 1, h, weights).astype(
                    jnp.bfloat16
                )
            v_stat_send[s] = v_stat_send[s] + pltpu.roll(stat_lanes(overall, total), g * 8, 1)
            return carry

        lax.fori_loop(0, groups, pair_step, 0)
        visual_back.append((
            send(v_send.at[s], v_recv.at[s], pair), send(v_stat_send.at[s], v_stat_recv.at[s], pair)
        ))

    attend_far(slot_of("diag", members - 1), here - 1, (0,))

    for piece in gates:
        piece.wait_recv()
    for s in range(seqs):
        logits = gate_own[s]
        for k in range(len(twins)):
            logits = logits + gate_recv[k, s]
        heads = groups * GROUP
        mine = logits[:, :heads]
        for c in range(1, heads_split):
            mine = jnp.where(core == c, logits[:, c * heads:(c + 1) * heads], mine)
        mine = jax.nn.sigmoid(mine)
        for g in range(groups):
            gate_buf[s, g, :, :GROUP] = mine[:, g * GROUP:(g + 1) * GROUP]

    for piece in text_back:
        piece.wait_recv()

    def unpacked(packed, g):
        return pltpu.roll(packed, LANES - g * 8, 1)

    def text_merge(i, carry):
        s, g = i // groups, i % groups
        ours, theirs = t_own_stat[s, g], unpacked(t_stat_recv[s], g)
        overall = jnp.maximum(ours, theirs)
        weight_a = jnp.exp(ours - overall)
        weight_b = jnp.exp(theirs - overall) * totals_of(theirs)
        inverse = 1.0 / (weight_a * totals_of(ours) + weight_b)
        weight_a, weight_b = weight_a * inverse, weight_b * inverse
        start = pl.multiple_of(g * (GROUP * DH), DH)
        for h in range(GROUP):
            cut = pl.ds(start + h * DH, DH)
            t_own[s, :, cut] = weight_a[:, h:h + 1] * t_own[s, :, cut] + weight_b[
                :, h:h + 1
            ] * t_recv[s, :, cut].astype(jnp.float32)
        return carry

    lax.fori_loop(0, seqs * groups, text_merge, 0)

    for s in range(seqs):
        for piece in visual_back[s]:
            piece.wait_recv()

        def own_step(g, carry, s=s):
            overall, total, weights = visual_weights(s, g, 0)
            theirs = unpacked(v_stat_recv[s], g)
            joint = jnp.maximum(overall, theirs)
            weight_a = jnp.exp(overall - joint)
            weight_b = jnp.exp(theirs - joint) * totals_of(theirs)
            inverse = 1.0 / (weight_a * total + weight_b)
            weights = [w * (weight_a * inverse) for w in weights]
            weight_b = weight_b * inverse
            start = pl.multiple_of(g * (GROUP * DH), DH)
            for h in range(GROUP):
                cut = pl.ds(start + h * DH, DH)
                visual = weighted(s, g, 0, h, weights) + weight_b[:, h:h + 1] * v_recv[
                    s, :, cut
                ].astype(jnp.float32)
                gate = gate_buf[s, g, :, h:h + 1]
                out_ref[s, :, cut] = ((1.0 - gate) * t_own[s, :, cut] + gate * visual).astype(
                    jnp.bfloat16
                )
            return carry

        lax.fori_loop(0, groups, own_step, 0)

    for copy in copies:
        copy.wait_send()


def pair_plan(n, heads_split, queries, text_keys, text_values, visual_keys, visual_values,
              gate_weight, text_offsets, image_sequence, image_position):
    seqs, rows, columns = queries.shape
    groups = text_keys.shape[-1] // DH
    here, tokens, kv_columns = visual_keys.shape
    members, blocks = n // 4, n // 2
    slots = blocks * here
    per_seq = image_sequence.shape[0] // seqs
    smem = pl.BlockSpec(memory_space=pltpu.SMEM)
    vmem = pl.BlockSpec(memory_space=pltpu.VMEM)
    bf16, f32 = jnp.bfloat16, jnp.float32
    count = 1 + 4 * (members - 1) + 2 + here * (2 * (members - 1) * (1 + len(chunks_of(tokens))) + 2) + 2 + 2 * seqs + heads_split - 1
    stats = (seqs, groups, rows, LANES)
    sent_stats = (seqs, rows, LANES)
    gate_shape = (seqs, rows, gate_weight.shape[-1])
    pairs = 2 * rows * GROUP * groups * (slots * tokens + seqs * blocks * rows)
    return pl.pallas_call(
        functools.partial(attention_kernel, n, heads_split, seqs, rows, groups, here, per_seq),
        in_specs=[smem] * 3 + [vmem] * 6,
        out_specs=vmem,
        out_shape=jax.ShapeDtypeStruct(queries.shape, bf16),
        scratch_shapes=[
            pltpu.VMEM(queries.shape, bf16),
            pltpu.VMEM((blocks - 1, *text_keys.shape), bf16),
            pltpu.VMEM((blocks - 1, *text_keys.shape), bf16),
            pltpu.VMEM((blocks - 1, *visual_keys.shape), bf16),
            pltpu.VMEM((blocks - 1, *visual_keys.shape), bf16),
            pltpu.VMEM((slots, 2, rows, columns), f32),
            pltpu.VMEM((slots, 2, groups, rows, LANES), f32),
            pltpu.VMEM((seqs, blocks * rows, kv_columns), bf16),
            pltpu.VMEM((seqs, blocks * rows, kv_columns), bf16),
            pltpu.VMEM(queries.shape, bf16),
            pltpu.VMEM(sent_stats, f32),
            pltpu.VMEM(queries.shape, bf16),
            pltpu.VMEM(sent_stats, f32),
            pltpu.VMEM(queries.shape, bf16),
            pltpu.VMEM(sent_stats, f32),
            pltpu.VMEM(queries.shape, bf16),
            pltpu.VMEM(sent_stats, f32),
            pltpu.VMEM(queries.shape, f32),
            pltpu.VMEM(stats, f32),
            pltpu.VMEM(gate_shape, f32),
            pltpu.VMEM((heads_split - 1, *gate_shape), f32),
            pltpu.VMEM(stats, f32),
            pltpu.SemaphoreType.DMA((count,)),
            pltpu.SemaphoreType.DMA((count,)),
        ],
        compiler_params=pltpu.CompilerParams(
            collective_id=0, has_side_effects=True, vmem_limit_bytes=60 << 20
        ),
        cost_estimate=pl.CostEstimate(
            flops=4 * pairs * DH, bytes_accessed=16 << 20, transcendentals=pairs
        ),
    )(
        text_offsets, image_sequence, image_position,
        queries, text_keys, text_values, visual_keys, visual_values, gate_weight.T,
    )


def line_kernel(
    seqs, rows, here, per_seq, heads_split,
    offsets, image_sequence, image_position,
    queries, text_keys, text_values, visual_keys, visual_values, gate_weight,
    out_ref,
    q_own, q_mate, q_out, tkv, tkv_out, vk, vv, k_out, v_out, part, part_mate, stat, stat_mate,
    side_part, side_stat, late_part, late_mate, late_stat, late_mate_stat, late_side, late_side_stat,
    t_own, t_send, t_recv, early, gate_own, gate_recv, gate_buf, weights, send_sems, recv_sems,
):
    me = lax.axis_index("seq")
    core = lax.axis_index("kvh")
    z, x = me // 2, me % 2
    half = z // 2
    inner = (z + 1) // 2 % 2
    side = z * 2 + 1 - x
    mate = (half * 2 + 1 - z % 2) * 2 + x
    cross = (3 - z) * 2 + x
    diag = (half * 2 + 1 - z % 2) * 2 + 1 - x
    twins = [(core + k) % heads_split for k in range(1, heads_split)]
    width = GROUP * DH
    group = 2 * here
    slots = 4 * group
    near, outer, across, far = 0, 1, 2, 3
    mine = 1 - inner

    def chip(kind):
        place = jnp.where(kind == outer, 3 * half, 1 + half)
        place = jnp.where(kind == across, 2 - half, place)
        return jnp.where(kind == far, 3 - 3 * half, place)

    def device(kind, sub):
        return chip(kind) * 2 + (x + sub) % 2

    def image_of(slot):
        return device(slot // group, slot // here % 2) * here + slot % here

    owners = [image_sequence[image_of(jnp.int32(i))] for i in range(slots)]
    positions = [image_position[image_of(jnp.int32(i))] for i in range(slots)]
    last = slots - 1
    lates = (last, last - here)

    def table(late):
        at, thresholds = [], []
        for s in range(seqs):
            slot_here = [jnp.int32(0)] * per_seq
            threshold_here = [jnp.int32(FAR)] * per_seq
            found = jnp.int32(0)
            for slot, (owner, position) in enumerate(zip(owners, positions)):
                if slot == late:
                    continue
                hit = owner == s
                for j in range(per_seq):
                    take = hit & (found == j)
                    slot_here[j] = jnp.where(take, slot, slot_here[j])
                    threshold_here[j] = jnp.where(take, position, threshold_here[j])
                found = found + jnp.where(hit, 1, 0)
            at += slot_here
            thresholds += threshold_here
        return at, thresholds

    tables = [table(late) for late in lates]

    barrier = pltpu.get_barrier_semaphore()
    for peer in (side, mate, cross, diag):
        pl.semaphore_signal(
            barrier, inc=1, device_id={"seq": peer}, device_id_type=pl.DeviceIdType.MESH
        )
    for twin in twins:
        pl.semaphore_signal(
            barrier, inc=1, device_id={"kvh": twin}, device_id_type=pl.DeviceIdType.MESH
        )

    bases, used = {}, 0
    for name, count in (
        ("x_text", 1), ("x_q", 1), ("x_k", here), ("x_v", here), ("x_t", 1), ("x_part", slots),
        ("x_stat", slots), ("late", 6), ("edge", 3), ("m_text", 8), ("m_q", 2), ("m_k", slots), ("m_v", slots),
        ("m_part", slots), ("m_stat", slots), ("c_text", 8), ("c_k", slots), ("c_v", slots),
        ("gate", heads_split),
    ):
        bases[name] = used
        used += count

    def copy(name, index, src, dst, peer, axis="seq"):
        return pltpu.make_async_remote_copy(
            src_ref=src,
            dst_ref=dst,
            send_sem=send_sems.at[bases[name] + index],
            recv_sem=recv_sems.at[bases[name] + index],
            device_id={axis: peer},
            device_id_type=pl.DeviceIdType.MESH,
        )

    x_text = copy("x_text", 0, tkv_out, tkv.at[mine, 1], side)
    x_q = copy("x_q", 0, q_out, q_own.at[:, 1], side)
    away = pl.multiple_of((1 - x) * DH, DH)

    def x_k(j):
        return copy("x_k", j, k_out.at[j], vk.at[mine * group + here + j], side)

    def x_v(j):
        return copy("x_v", j, v_out.at[j], vv.at[mine * group + here + j], side)

    x_t = copy("x_t", 0, t_send, t_recv, side)

    def x_part(i):
        return copy("x_part", i, part.at[i, 1], side_part.at[i], side)

    def x_stat(i):
        return copy("x_stat", i, stat.at[i], side_stat.at[i], side)

    def m_text(kind, sub):
        return copy("m_text", kind * 2 + sub, tkv.at[kind, sub], tkv.at[kind, sub], mate)

    def m_q(sub):
        return copy("m_q", sub, q_own.at[:, sub], q_mate.at[:, sub], mate)

    def m_k(i):
        return copy("m_k", i, vk.at[i], vk.at[i], mate)

    def m_v(i):
        return copy("m_v", i, vv.at[i], vv.at[i], mate)

    def m_part(i):
        return copy("m_part", i, part_mate.at[i], part.at[i], mate)

    def m_stat(i):
        return copy("m_stat", i, stat_mate.at[i], stat.at[i], mate)

    def c_text(kind, sub):
        return copy("c_text", (kind + 2) * 2 + sub, tkv.at[kind, sub], tkv.at[kind + 2, sub], cross)

    def c_k(i):
        return copy("c_k", i, vk.at[i], vk.at[i + 2 * group], cross)

    def c_v(i):
        return copy("c_v", i, vv.at[i], vv.at[i + 2 * group], cross)

    late_own = (
        copy("late", 1, late_stat, late_side_stat, side),
        copy("late", 0, late_part.at[1], late_side, side),
    )
    late_to_mate = (
        copy("late", 3, late_mate_stat, late_stat, mate),
        copy("late", 2, late_mate.at[0], late_part.at[0], mate),
    )
    late_to_diag = (
        copy("late", 5, late_mate_stat, late_side_stat, diag),
        copy("late", 4, late_mate.at[1], late_side, diag),
    )

    edge = last - 1
    edge_to_mate = (
        copy("edge", 0, part_mate.at[edge, 0], part.at[edge, 0], mate),
        copy("m_stat", edge, stat_mate.at[edge], stat.at[edge], mate),
    )
    edge_to_diag = (
        copy("edge", 1, part_mate.at[edge, 1], side_part.at[edge], diag),
        copy("edge", 2, stat_mate.at[edge], side_stat.at[edge], diag),
    )

    home = pl.multiple_of(x * DH, DH)
    home_q = x * width
    away_q = (1 - x) * width

    def stack_q(s, carry):
        for h in range(GROUP):
            q_own[s, 0, h] = queries[s, :, pl.ds(pl.multiple_of(home_q + h * DH, DH), DH)]
            q_out[s, h] = queries[s, :, pl.ds(pl.multiple_of(away_q + h * DH, DH), DH)]
        return carry

    for kind, source in enumerate((text_keys, text_values)):
        tkv[mine, 0, kind] = source[:, :, pl.ds(home, DH)]
        tkv_out[kind] = source[:, :, pl.ds(away, DH)]
    lax.fori_loop(0, seqs, stack_q, 0)
    def keep_home(j):
        vk[mine * group + j] = visual_keys[:, j, pl.ds(home, DH)]
        vv[mine * group + j] = visual_values[:, j, pl.ds(home, DH)]

    def keep_away(j):
        k_out[j] = visual_keys[:, j, pl.ds(away, DH)]
        v_out[j] = visual_values[:, j, pl.ds(away, DH)]

    keep_home(0)
    pl.semaphore_wait(barrier, 4 + len(twins))

    x_text.start()
    x_q.start()

    @pl.when(inner == 1)
    def _():
        c_text(near, 0).start()
        m_text(near, 0).start()
        c_k(0).start()
        c_v(0).start()
        m_k(0).start()
        m_v(0).start()

    @pl.when(inner == 0)
    def _():
        m_text(outer, 0).start()
        m_k(group).start()

    for j in range(here):
        if j:
            keep_home(j)
        keep_away(j)
        x_k(j).start()
        x_v(j).start()

    lane = lax.broadcasted_iota(jnp.int32, (rows, LANES), 1)

    def softmax(scores):
        peak = jnp.max(scores, axis=-1, keepdims=True)
        return peak, jnp.exp2((scores - peak) * SCALE2).astype(jnp.bfloat16)

    def scores_of(q, k):
        return lax.dot_general(q, k, (((1,), (1,)), ((), ())), preferred_element_type=jnp.float32)

    def attend(i, q_ref, part_ref, stat_ref):
        attend_to(i, q_ref, part_ref.at[i], stat_ref.at[i])

    def attend_to(i, q_ref, part_ref, stat_ref):
        q = q_ref[image_sequence[image_of(i)]].reshape(2, GROUP * rows, DH)
        k, v = vk[i], vv[i]
        v = jnp.concatenate([v, jnp.ones_like(v)], axis=1)
        scores = [scores_of(q[0], k), scores_of(q[1], k)]
        packed = []
        for b in range(2):
            peak, expd = softmax(scores[b])
            num = jnp.dot(expd, v, preferred_element_type=jnp.float32)
            total = num[:, DH:]
            part_ref[b] = (num[:, :DH] * (1.0 / total)).astype(jnp.bfloat16).reshape(GROUP, rows, DH)
            peaks = jnp.zeros((rows, LANES), jnp.float32)
            totals = jnp.ones((rows, LANES), jnp.float32)
            for h in range(GROUP):
                at_h = slice(h * rows, (h + 1) * rows)
                peaks = jnp.where(lane == h, peak[at_h], peaks)
                totals = jnp.where(lane == h, total[at_h], totals)
            packed.append(peaks * SCALE + jnp.log(totals))
        stat_ref[...] = jnp.concatenate(packed, axis=0).T[:8]

    def attend_own(i):
        attend(i, q_own, part, stat)
        x_part(i).start()
        x_stat(i).start()

    def attend_mate(i):
        attend(i, q_mate, part_mate, stat_mate)

        @pl.when(i != edge)
        def _():
            m_part(i).start()
            m_stat(i).start()

        @pl.when(i == edge)
        def _():
            for piece in (*edge_to_mate, *edge_to_diag):
                piece.start()

    def loop(start, stop, body):
        def step(i, carry):
            body(i)
            return carry

        lax.fori_loop(start, stop, step, 0)

    @pl.when(inner == 1)
    def _():
        x_text.wait_recv()
        c_text(near, 1).start()
        m_text(near, 1).start()
        for j in range(1, here):
            m_k(j).start()
            m_v(j).start()
        for sub in range(2):
            m_text(outer, sub).wait_recv()
            c_text(outer, sub).start()
        for j in range(1, here):
            c_k(j).start()
            c_v(j).start()
        c_text(near, 0).wait_recv()
        m_text(across, 0).start()

    @pl.when(inner == 0)
    def _():
        x_text.wait_recv()
        m_text(outer, 1).start()
        m_q(0).start()

    rest = gate_weight[...]
    q_all = queries[...].reshape(seqs * rows, queries.shape[-1])
    logits = 0.0
    for _ in range(3):
        term = rest.astype(jnp.bfloat16)
        rest = rest - term.astype(jnp.float32)
        logits = logits + lax.dot_general(
            q_all, term, (((1,), (1,)), ((), ())), preferred_element_type=jnp.float32
        )
    gate_own[...] = logits.reshape(gate_own.shape)
    gates = [copy("gate", k, gate_own, gate_recv.at[k], twin, "kvh") for k, twin in enumerate(twins)]
    for piece in gates:
        piece.start()


    x_q.wait_recv()

    @pl.when(inner == 1)
    def _():
        loop(0, here, attend_own)
        c_text(near, 1).wait_recv()
        m_text(across, 1).start()
        x_k(0).wait_recv()
        c_k(here).start()
        for sub in range(2):
            c_text(outer, sub).wait_recv()
            m_text(far, sub).start()
        x_v(0).wait_recv()
        c_v(here).start()

    @pl.when(inner == 0)
    def _():
        m_q(1).start()
        m_v(group).start()
        for j in range(1, here):
            m_k(group + j).start()
            m_v(group + j).start()
        loop(group, group + here, attend_own)
        for j in range(here):
            x_k(j).wait_recv()
            m_k(group + here + j).start()
            x_v(j).wait_recv()
            m_v(group + here + j).start()
        for kind in (near, across, far):
            for sub in range(2):
                m_text(kind, sub).wait_recv()

    count = 8 * rows
    key_lane = lax.broadcasted_iota(jnp.int32, (rows, count), 1)
    key_row = lax.broadcasted_iota(jnp.int32, (rows, count), 0)
    key_pos = key_lane % rows
    for kind in range(4):
        for sub in range(2):
            b = kind * 2 + sub
            inside = (key_lane >= b * rows) & (key_lane < (b + 1) * rows)
            key_pos = key_pos + jnp.where(inside, offsets[device(kind, sub)], 0)
    place = [offsets[me], offsets[side]]
    biases = [jnp.where(key_pos <= key_row + p, 0.0, NEG) for p in place]

    def text_step(s):
        q = q_own[s].reshape(2, GROUP * rows, DH)
        k = tkv[:, :, 0, s].reshape(count, DH)
        v = tkv[:, :, 1, s].reshape(count, DH)
        v = jnp.concatenate([v, jnp.ones_like(v)], axis=1)
        for b in range(2):
            scores = scores_of(q[b], k).reshape(GROUP, rows, count) + biases[b][None]
            peak, expd = softmax(scores.reshape(GROUP * rows, count))
            num = jnp.dot(expd, v, preferred_element_type=jnp.float32)
            out = (num[:, :DH] * (1.0 / num[:, DH:])).reshape(GROUP, rows, DH)
            if b == 0:
                t_own[0, s] = out
            else:
                t_send[s] = out.astype(jnp.bfloat16)

    loop(0, seqs, text_step)
    x_t.start()

    @pl.when(inner == 1)
    def _():
        for j in range(1, here):
            x_k(j).wait_recv()
            c_k(here + j).start()
            x_v(j).wait_recv()
            c_v(here + j).start()

    for piece in gates:
        piece.wait_recv()
    for s in range(seqs):
        logits = gate_own[s]
        for k in range(len(twins)):
            logits = logits + gate_recv[k, s]
        heads = 2 * GROUP
        mix = logits[:, :heads]
        for c in range(1, heads_split):
            mix = jnp.where(core == c, logits[:, c * heads:(c + 1) * heads], mix)
        mix = jax.nn.sigmoid(mix)
        for g in range(2):
            gate_buf[s, g, :, :GROUP] = mix[:, g * GROUP:(g + 1) * GROUP]


    @pl.when(inner == 1)
    def _():
        for sub in range(2):
            m_q(sub).wait_recv()

        def own_step(i):
            attend_mate(i)
            attend_own(i)

        loop(here, group, own_step)

        def stream_step(c):
            @pl.when((c >= here) & (c < here + group))
            def _():
                o = group + c - here
                m_k(o).wait_recv()
                c_k(o).start()
                m_v(o).wait_recv()
                c_v(o).start()
                attend_own(o)

            c_k(c).wait_recv()
            c_v(c).wait_recv()
            attend_mate(2 * group + c)
            attend_own(2 * group + c)

        loop(0, 2 * group - 1, stream_step)

    @pl.when(inner == 0)
    def _():
        loop(group + here, 2 * group, attend_own)
        for j in range(here):
            m_k(j).wait_recv()
            m_v(j).wait_recv()
        loop(0, here, attend_own)

        def forward(i):
            m_part(i).wait_recv()
            m_stat(i).wait_recv()
            x_part(i).start()
            x_stat(i).start()

        loop(here, group, forward)
        loop(2 * group, edge, forward)
        for piece in edge_to_mate:
            piece.wait_recv()


    row_pos = lax.broadcasted_iota(jnp.int32, (rows, LANES), 0) + place[0]
    real = lane % 8 < GROUP

    def spread(values, join):
        stride = 8
        while stride < 8 * per_seq:
            up = pltpu.roll(values, LANES - stride, 1)
            down = pltpu.roll(values, stride, 1)
            values = join(values, jnp.where(lane // stride % 2 == 0, up, down))
            stride *= 2
        return values

    def lanes_of(choices, size):
        limits = jnp.full((rows, LANES), FAR, jnp.int32)
        for i, threshold in enumerate(choices):
            limits = jnp.where(lane // size == i, threshold, limits)
        return (limits <= row_pos) & real

    def early_merge(g):
        absolute = x if g == 0 else 1 - x
        at, thresholds = tables[g]
        if g == 1:
            at = [i + here * (1 - 2 * (i // here % 2)) for i in at]
        seen = lanes_of(thresholds, 8)
        gathered = jnp.concatenate([(stat, side_stat)[g][i] for i in at], axis=0).T
        lse = jnp.where(seen, gathered[g * rows:(g + 1) * rows], NEG)
        overall = spread(lse, jnp.maximum)
        weight = jnp.where(seen, jnp.exp(lse - overall), 0.0)
        total = spread(weight, jnp.add)
        gate = 0.0
        for s in range(seqs):
            here_gate = jnp.where(lane < GROUP, gate_buf[s, absolute], 0.0)
            gate = gate + (pltpu.roll(here_gate, s * per_seq * 8, 1) if s else here_gate)
        gate = spread(gate, jnp.add)
        weights[g, 0] = overall
        weights[g, 1] = total
        weights[g, 2] = gate
        weights[g, 3] = weight * (gate / jnp.where(total > 0.0, total, 1.0))
        for s in range(seqs):
            for h in range(GROUP):
                visual = 0.0
                for j in range(per_seq):
                    i = at[s * per_seq + j]
                    piece = part[i, 0, h] if g == 0 else side_part[i, h]
                    k = (s * per_seq + j) * 8 + h
                    visual = visual + weights[g, 3, :, k:k + 1] * piece.astype(jnp.float32)
                early[g, s, h] = visual
                k = s * per_seq * 8 + h
                text = t_own[g, s, h] if g == 0 else t_recv[s, h].astype(jnp.float32)
                t_own[g, s, h] = (1.0 - weights[g, 2, :, k:k + 1]) * text

    def late_weights(g):
        late = image_of(jnp.int32(lates[g]))
        limits = [jnp.where(image_sequence[late] == s, image_position[late], FAR) for s in range(seqs)]
        seen = lanes_of(limits, 8 * per_seq)
        source = (late_stat, late_side_stat)[g][...]
        gathered = jnp.concatenate([source] * (LANES // 8), axis=0).T
        lse = jnp.where(seen, gathered[g * rows:(g + 1) * rows], NEG)
        before = weights[g, 0]
        overall = jnp.maximum(before, lse)
        weight_a = jnp.where(weights[g, 1] > 0.0, weights[g, 1] * jnp.exp(before - overall), 0.0)
        weight_b = jnp.where(seen, jnp.exp(lse - overall), 0.0)
        total = weight_a + weight_b
        inverse = 1.0 / jnp.where(total > 0.0, total, 1.0)
        weights[g, 0] = weight_a * inverse
        weights[g, 1] = weight_b * inverse * weights[g, 2]
        for s in range(seqs):
            for h in range(GROUP):
                k = s * per_seq * 8 + h
                early[g, s, h] = t_own[g, s, h] + weights[g, 0, :, k:k + 1] * early[g, s, h]

    def late_apply(g):
        absolute = x if g == 0 else 1 - x
        for h in range(GROUP):
            piece = (late_part[0, h] if g == 0 else late_side[h]).astype(jnp.float32)
            cut = pl.ds(pl.multiple_of(absolute * width + h * DH, DH), DH)
            for s in range(seqs):
                k = s * per_seq * 8 + h
                out_ref[s, :, cut] = (
                    early[g, s, h] + weights[g, 1, :, k:k + 1] * piece
                ).astype(jnp.bfloat16)

    def receive(i):
        x_part(i).wait_recv()
        x_stat(i).wait_recv()

    early_merge(0)

    @pl.when(inner == 1)
    def _():
        c_k(2 * group - 1).wait_recv()
        c_v(2 * group - 1).wait_recv()
        attend_to(last, q_mate, late_mate, late_mate_stat)
        for piece in (late_to_mate[0], late_to_diag[0], late_to_mate[1], late_to_diag[1]):
            piece.start()
        attend_to(last, q_own, late_part, late_stat)
        for piece in late_own:
            piece.start()

    loop(0, edge, receive)

    @pl.when(inner == 1)
    def _():
        receive(edge)

    @pl.when(inner == 0)
    def _():
        for piece in edge_to_diag:
            piece.wait_recv()

    x_t.wait_recv()
    early_merge(1)

    def arrive(index):
        @pl.when(inner == 0)
        def _():
            late_to_diag[index].wait_recv()

        @pl.when(inner == 1)
        def _():
            late_own[index].wait_recv()

    @pl.when(inner == 0)
    def _():
        late_to_mate[0].wait_recv()

    late_weights(0)
    arrive(0)
    late_weights(1)

    @pl.when(inner == 0)
    def _():
        late_to_mate[1].wait_recv()

    late_apply(0)
    arrive(1)
    late_apply(1)

    def sent(piece):
        piece.wait_send()

    sent(x_text)
    sent(x_q)
    sent(x_t)
    for j in range(here):
        sent(x_k(j))
        sent(x_v(j))
    for piece in gates:
        sent(piece)

    def all_sent(i):
        sent(x_part(i))
        sent(x_stat(i))

    loop(0, edge, all_sent)

    @pl.when(inner == 1)
    def _():
        for sub in range(2):
            for kind in (near, outer):
                sent(c_text(kind, sub))
            for kind in (near, across, far):
                sent(m_text(kind, sub))
        for j in range(here):
            sent(m_k(j))
            sent(m_v(j))

        def stream_sent(i):
            sent(c_k(i))
            sent(c_v(i))

        def mate_sent(i):
            sent(m_part(i))
            sent(m_stat(i))

        loop(0, 2 * group, stream_sent)
        loop(here, group, mate_sent)
        loop(2 * group, edge, mate_sent)
        all_sent(edge)
        for piece in (*edge_to_mate, *edge_to_diag, *late_to_mate, *late_to_diag, *late_own):
            sent(piece)

    @pl.when(inner == 0)
    def _():
        for sub in range(2):
            sent(m_text(outer, sub))
            sent(m_q(sub))

        def stream_sent(i):
            sent(m_k(i))
            sent(m_v(i))

        loop(group, 2 * group, stream_sent)


def line_plan(heads_split, queries, text_keys, text_values, visual_keys, visual_values,
              gate_weight, text_offsets, image_sequence, image_position):
    seqs, rows, columns = queries.shape
    here, tokens, _ = visual_keys.shape
    slots = image_sequence.shape[0]
    per_seq = slots // seqs
    smem = pl.BlockSpec(memory_space=pltpu.SMEM)
    vmem = pl.BlockSpec(memory_space=pltpu.VMEM)
    bf16, f32 = jnp.bfloat16, jnp.float32
    stacked = (seqs, 2, GROUP, rows, DH)
    one = (seqs, GROUP, rows, DH)
    gate_shape = (seqs, rows, gate_weight.shape[-1])
    count = 2 + 2 * here + 1 + 2 * slots + 6 + 3 + 10 + 4 * slots + 8 + 2 * slots + heads_split
    pairs = 2 * rows * GROUP * (2 * slots * tokens + seqs * 8 * rows)
    return pl.pallas_call(
        functools.partial(line_kernel, seqs, rows, here, per_seq, heads_split),
        in_specs=[smem] * 3 + [vmem] * 6,
        out_specs=vmem,
        out_shape=jax.ShapeDtypeStruct(queries.shape, bf16),
        scratch_shapes=[
            pltpu.VMEM(stacked, bf16),
            pltpu.VMEM(stacked, bf16),
            pltpu.VMEM(one, bf16),
            pltpu.VMEM((4, 2, 2, seqs, rows, DH), bf16),
            pltpu.VMEM((2, seqs, rows, DH), bf16),
            pltpu.VMEM((slots, tokens, DH), bf16),
            pltpu.VMEM((slots, tokens, DH), bf16),
            pltpu.VMEM((here, tokens, DH), bf16),
            pltpu.VMEM((here, tokens, DH), bf16),
            pltpu.VMEM((slots, 2, GROUP, rows, DH), bf16),
            pltpu.VMEM((slots, 2, GROUP, rows, DH), bf16),
            pltpu.VMEM((slots, 8, LANES), f32),
            pltpu.VMEM((slots, 8, LANES), f32),
            pltpu.VMEM((slots, GROUP, rows, DH), bf16),
            pltpu.VMEM((slots, 8, LANES), f32),
            pltpu.VMEM((2, GROUP, rows, DH), bf16),
            pltpu.VMEM((2, GROUP, rows, DH), bf16),
            pltpu.VMEM((8, LANES), f32),
            pltpu.VMEM((8, LANES), f32),
            pltpu.VMEM((GROUP, rows, DH), bf16),
            pltpu.VMEM((8, LANES), f32),
            pltpu.VMEM((2, *one), f32),
            pltpu.VMEM(one, bf16),
            pltpu.VMEM(one, bf16),
            pltpu.VMEM((2, *one), f32),
            pltpu.VMEM(gate_shape, f32),
            pltpu.VMEM((heads_split - 1, *gate_shape), f32),
            pltpu.VMEM((seqs, 2, rows, LANES), f32),
            pltpu.VMEM((2, 4, rows, LANES), f32),
            pltpu.SemaphoreType.DMA((count,)),
            pltpu.SemaphoreType.DMA((count,)),
        ],
        compiler_params=pltpu.CompilerParams(
            collective_id=1, has_side_effects=True, vmem_limit_bytes=60 << 20
        ),
        cost_estimate=pl.CostEstimate(
            flops=4 * pairs * DH, bytes_accessed=16 << 20, transcendentals=pairs
        ),
    )(
        text_offsets, image_sequence, image_position,
        queries, text_keys, text_values,
        visual_keys.transpose(1, 0, 2), visual_values.transpose(1, 0, 2), gate_weight.T,
    )


def on_device(n, heads_split, queries, text_keys, *rest):
    groups = text_keys.shape[-1] // DH
    images = rest[-2].shape[0]
    line = n // 2
    if line - 2 == 2 and groups == 2 and images * 8 == LANES and 2 * queries.shape[1] == LANES:
        return line_plan(heads_split, queries, text_keys, *rest)
    return pair_plan(n, heads_split, queries, text_keys, *rest)


def solution(mesh):
    return jax.shard_map(
        functools.partial(on_device, mesh.shape["seq"], mesh.shape["kvh"]),
        mesh=mesh,
        in_specs=(
            P("batch", "seq", "kvh"),
            P("batch", "seq", "kvh"),
            P("batch", "seq", "kvh"),
            P(("batch", "seq"), None, "kvh"),
            P(("batch", "seq"), None, "kvh"),
            P("kvh", None),
            P("batch"),
            P("batch"),
            P("batch"),
        ),
        out_specs=P("batch", "seq", "kvh"),
        check_vma=False,
    )
```

```python
import functools
import math

import jax
import jax.numpy as jnp
from jax import lax
from jax.experimental import pallas as pl
from jax.experimental.pallas import tpu as pltpu
from jax.sharding import PartitionSpec as P

DH = 128
GROUP = 7
LANES = 128
HALF = LANES // 2
CHUNKS = 4
TILE = 16
NEG = -1e30
FLOOR = -1e29
FAR = 1 << 30
SCALE = 1.0 / DH ** 0.5
SCALE2 = SCALE * math.log2(math.e)


def chunks_of(tokens):
    size = -(-tokens // (CHUNKS * TILE)) * TILE
    return [pl.ds(a, min(size, tokens - a)) for a in range(0, tokens, size)]


def heads_of(ref, lead, g):
    start = pl.multiple_of(g * (GROUP * DH), DH)
    return jnp.concatenate(
        [ref[lead, :, pl.ds(start + h * DH, DH)] for h in range(GROUP)], axis=0
    )


def put_heads(ref, lead, g, stacked):
    rows = stacked.shape[0] // GROUP
    start = pl.multiple_of(g * (GROUP * DH), DH)
    for h in range(GROUP):
        ref[(*lead, slice(None), pl.ds(start + h * DH, DH))] = stacked[h * rows:(h + 1) * rows]


def pack_stats(peak, total, rows):
    lane = lax.broadcasted_iota(jnp.int32, (rows, LANES), 1)
    packed = jnp.zeros((rows, LANES), jnp.float32)
    for h in range(GROUP):
        here = slice(h * rows, (h + 1) * rows)
        packed = jnp.where(lane == h, peak[here], packed)
        packed = jnp.where(lane == HALF + h, total[here], packed)
    return packed


def totals_of(packed):
    return pltpu.roll(packed, HALF, 1)


def softmax_parts(q, keys, values, bias):
    scores = lax.dot_general(
        q, keys, (((1,), (1,)), ((), ())), preferred_element_type=jnp.float32
    )
    if bias is not None:
        rows, count = bias.shape
        scores = (scores.reshape(GROUP, rows, count) + bias[None]).reshape(GROUP * rows, count)
    peak = jnp.maximum(jnp.max(scores, axis=-1, keepdims=True), FLOOR)
    expd = jnp.exp2((scores - peak) * SCALE2)
    total = jnp.sum(expd, axis=-1, keepdims=True)
    num = jnp.dot(expd.astype(jnp.bfloat16), values, preferred_element_type=jnp.float32)
    return peak * SCALE, total, num


def attention_kernel(
    n, heads_split, seqs, rows, groups, here, per_seq,
    offsets, image_sequence, image_position,
    queries, text_keys, text_values, visual_keys, visual_values, gate_weight,
    out_ref,
    q_pair, far_tk, far_tv, far_ik, far_iv, num, stat, cat_k, cat_v,
    t_send, t_stat_send, t_recv, t_stat_recv, v_send, v_stat_send, v_recv, v_stat_recv,
    t_own, t_own_stat, gate_own, gate_recv, gate_buf, send_sems, recv_sems,
):
    me = lax.axis_index("seq")
    core = lax.axis_index("kvh")
    members = n // 4
    blocks = n // 2
    pair = me // 4 * 4 + (me + 2) % 4
    side = me // 2 * 2 + (me + 1) % 2
    others = [(me // 4 + k) % members * 4 + me % 4 for k in range(1, members)]
    twins = [(core + k) % heads_split for k in range(1, heads_split)]

    far_ids = [(me // 4 + members - k) % members * 4 + me % 4 for k in range(1, members)]
    sources = [me, side] + far_ids + [f // 2 * 2 + (f + 1) % 2 for f in far_ids]
    places = [offsets[i] for i in (me, pair, *sources)]
    image_ids = [source * here + j for source in sources for j in range(here)]
    owners = [image_sequence[i] for i in image_ids]
    positions = [image_position[i] for i in image_ids]
    at, thresholds = [], []
    for s in range(seqs):
        slot_here = [jnp.int32(0)] * per_seq
        threshold_here = [jnp.int32(FAR)] * per_seq
        found = jnp.int32(0)
        for slot, (owner, position) in enumerate(zip(owners, positions)):
            hit = owner == s
            for j in range(per_seq):
                take = hit & (found == j)
                slot_here[j] = jnp.where(take, slot, slot_here[j])
                threshold_here[j] = jnp.where(take, position, threshold_here[j])
            found = found + jnp.where(hit, 1, 0)
        at += slot_here
        thresholds += threshold_here

    barrier = pltpu.get_barrier_semaphore()
    for peer in (pair, side, *others):
        pl.semaphore_signal(
            barrier, inc=1, device_id={"seq": peer}, device_id_type=pl.DeviceIdType.MESH
        )
    for twin in twins:
        pl.semaphore_signal(
            barrier, inc=1, device_id={"kvh": twin}, device_id_type=pl.DeviceIdType.MESH
        )
    pl.semaphore_wait(barrier, 2 + len(others) + len(twins))

    copies = []
    chunks = chunks_of(visual_values.shape[1])

    def send(src, dst, peer, axis="seq"):
        copy = pltpu.make_async_remote_copy(
            src_ref=src,
            dst_ref=dst,
            send_sem=send_sems.at[len(copies)],
            recv_sem=recv_sems.at[len(copies)],
            device_id={axis: peer},
            device_id_type=pl.DeviceIdType.MESH,
        )
        copy.start()
        copies.append(copy)
        return copy

    def slot_of(kind, k=0):
        return {"side": 0, "far": k, "diag": members - 1 + k}[kind]

    q_copy = send(queries, q_pair, pair)
    text_far = []
    for k, peer in enumerate(others, 1):
        s = slot_of("far", k)
        text_far.append((send(text_keys, far_tk.at[s], peer), send(text_values, far_tv.at[s], peer)))
    text_side = (send(text_keys, far_tk.at[0], side), send(text_values, far_tv.at[0], side))
    image_far = {}
    image_side = {}
    for j in range(here):
        for k, peer in enumerate(others, 1):
            s = slot_of("far", k)
            image_far[k, j] = [send(visual_keys.at[j], far_ik.at[s, j], peer)] + [
                send(visual_values.at[j, cut], far_iv.at[s, j, cut], peer) for cut in chunks
            ]
        image_side[j] = (
            send(visual_keys.at[j], far_ik.at[0, j], side),
            send(visual_values.at[j], far_iv.at[0, j], side),
        )

    def attend(keys, values, index, sides):
        owner = owners[index]

        def step(g, carry):
            at_g = pl.ds(pl.multiple_of(g * DH, DH), DH)
            k, v = keys[:, at_g], values[:, at_g]
            for which in sides:
                q = heads_of(queries if which == 0 else q_pair, owner, g)
                peak, total, out = softmax_parts(q, k, v, None)
                put_heads(num, (index, which), g, out)
                stat[index, which, g] = pack_stats(peak, total, rows)
            return carry

        lax.fori_loop(0, groups, step, 0)

    rest = gate_weight[...]
    q_all = queries[...].reshape(seqs * rows, queries.shape[-1])
    logits = 0.0
    for _ in range(3):
        term = rest.astype(jnp.bfloat16)
        rest = rest - term.astype(jnp.float32)
        logits = logits + lax.dot_general(
            q_all, term, (((1,), (1,)), ((), ())), preferred_element_type=jnp.float32
        )
    gate_own[...] = logits.reshape(gate_own.shape)
    t_stat_send[...] = jnp.zeros_like(t_stat_send)
    v_stat_send[...] = jnp.zeros_like(v_stat_send)

    for j in range(here):
        attend(visual_keys.at[j], visual_values.at[j], j, (0,))
    gates = [send(gate_own, gate_recv.at[k], twin, "kvh") for k, twin in enumerate(twins)]

    text_diag = []
    for k, pieces in enumerate(text_far, 1):
        for piece in pieces:
            piece.wait_recv()
        s, d = slot_of("far", k), slot_of("diag", k)
        text_diag.append((
            send(far_tk.at[s], far_tk.at[d], side), send(far_tv.at[s], far_tv.at[d], side)
        ))

    q_copy.wait_recv()
    for j in range(here):
        attend(visual_keys.at[j], visual_values.at[j], j, (1,))

    for piece in (*text_side, *[p for pieces in text_diag for p in pieces]):
        piece.wait_recv()
    for b in range(blocks):
        span = pl.ds(b * rows, rows)
        cat_k[:, span, :] = text_keys[...] if b == 0 else far_tk[b - 1]
        cat_v[:, span, :] = text_values[...] if b == 0 else far_tv[b - 1]
    count = blocks * rows
    lane = lax.broadcasted_iota(jnp.int32, (rows, count), 1)
    row = lax.broadcasted_iota(jnp.int32, (rows, count), 0)
    key_pos = lane % rows
    for b in range(blocks):
        inside = (lane >= b * rows) & (lane < (b + 1) * rows)
        key_pos = key_pos + jnp.where(inside, places[2 + b], 0)
    biases = [jnp.where(key_pos <= row + places[which], 0.0, NEG) for which in (0, 1)]

    def text_step(i, carry):
        s, g = i // groups, i % groups
        at_g = pl.ds(pl.multiple_of(g * DH, DH), DH)
        k, v = cat_k[s, :, at_g], cat_v[s, :, at_g]
        peak, total, out = softmax_parts(heads_of(queries, s, g), k, v, biases[0])
        put_heads(t_own, (s,), g, out)
        t_own_stat[s, g] = pack_stats(peak, total, rows)
        peak, total, out = softmax_parts(heads_of(q_pair, s, g), k, v, biases[1])
        out = out * (1.0 / jnp.where(total > 0.0, total, 1.0))
        put_heads(t_send, (s,), g, out.astype(jnp.bfloat16))
        t_stat_send[s] = t_stat_send[s] + pltpu.roll(pack_stats(peak, total, rows), g * 8, 1)
        return carry

    lax.fori_loop(0, seqs * groups, text_step, 0)
    text_back = (send(t_send, t_recv, pair), send(t_stat_send, t_stat_recv, pair))

    image_diag = {}

    def forward(j):
        for k in range(1, members):
            s, d = slot_of("far", k), slot_of("diag", k)
            pieces = image_far[k, j]
            pieces[0].wait_recv()
            image_diag[k, j] = [send(far_ik.at[s, j], far_ik.at[d, j], side)]
            for cut, piece in zip(chunks, pieces[1:]):
                piece.wait_recv()
                image_diag[k, j].append(send(far_iv.at[s, j, cut], far_iv.at[d, j, cut], side))

    def attend_far(slot, j, sides=(1, 0)):
        attend(far_ik.at[slot, j], far_iv.at[slot, j], (slot + 1) * here + j, sides)

    for j in range(here):
        for piece in image_side[j]:
            piece.wait_recv()
        attend_far(0, j)
    for j in range(here):
        forward(j)
        for k in range(1, members):
            attend_far(slot_of("far", k), j)
        for k in range(1, members):
            for piece in image_diag[k, j]:
                piece.wait_recv()
            last = j == here - 1 and k == members - 1
            attend_far(slot_of("diag", k), j, (1,) if last else (1, 0))

    row_pos = lax.broadcasted_iota(jnp.int32, (rows, LANES), 0)

    def visual_weights(s, g, which):
        seen, packed = [], []
        for j in range(per_seq):
            seen.append(thresholds[s * per_seq + j] <= row_pos + places[which])
            packed.append(stat[at[s * per_seq + j], which, g])
        peaks = [jnp.where(a, p, NEG) for a, p in zip(seen, packed)]
        overall = functools.reduce(jnp.maximum, peaks)
        weights = [jnp.where(a, jnp.exp(p - overall), 0.0) for a, p in zip(seen, peaks)]
        total = sum(w * totals_of(p) for w, p in zip(weights, packed))
        return overall, total, weights

    def weighted(s, g, which, h, weights):
        start = pl.multiple_of(g * (GROUP * DH), DH)
        return sum(
            w[:, h:h + 1] * num[at[s * per_seq + j], which, :, pl.ds(start + h * DH, DH)]
            for j, w in enumerate(weights)
        )

    def stat_lanes(overall, total):
        lane_id = lax.broadcasted_iota(jnp.int32, (rows, LANES), 1)
        packed = jnp.where(lane_id < HALF, overall, pltpu.roll(total, HALF, 1))
        return jnp.where(lane_id % HALF < GROUP, packed, 0.0)

    visual_back = []
    for s in range(seqs):
        def pair_step(g, carry, s=s):
            overall, total, weights = visual_weights(s, g, 1)
            inverse = 1.0 / jnp.where(total > 0.0, total, 1.0)
            weights = [w * inverse for w in weights]
            start = pl.multiple_of(g * (GROUP * DH), DH)
            for h in range(GROUP):
                v_send[s, :, pl.ds(start + h * DH, DH)] = weighted(s, g, 1, h, weights).astype(
                    jnp.bfloat16
                )
            v_stat_send[s] = v_stat_send[s] + pltpu.roll(stat_lanes(overall, total), g * 8, 1)
            return carry

        lax.fori_loop(0, groups, pair_step, 0)
        visual_back.append((
            send(v_send.at[s], v_recv.at[s], pair), send(v_stat_send.at[s], v_stat_recv.at[s], pair)
        ))

    attend_far(slot_of("diag", members - 1), here - 1, (0,))

    for piece in gates:
        piece.wait_recv()
    for s in range(seqs):
        logits = gate_own[s]
        for k in range(len(twins)):
            logits = logits + gate_recv[k, s]
        heads = groups * GROUP
        mine = logits[:, :heads]
        for c in range(1, heads_split):
            mine = jnp.where(core == c, logits[:, c * heads:(c + 1) * heads], mine)
        mine = jax.nn.sigmoid(mine)
        for g in range(groups):
            gate_buf[s, g, :, :GROUP] = mine[:, g * GROUP:(g + 1) * GROUP]

    for piece in text_back:
        piece.wait_recv()

    def unpacked(packed, g):
        return pltpu.roll(packed, LANES - g * 8, 1)

    def text_merge(i, carry):
        s, g = i // groups, i % groups
        ours, theirs = t_own_stat[s, g], unpacked(t_stat_recv[s], g)
        overall = jnp.maximum(ours, theirs)
        weight_a = jnp.exp(ours - overall)
        weight_b = jnp.exp(theirs - overall) * totals_of(theirs)
        inverse = 1.0 / (weight_a * totals_of(ours) + weight_b)
        weight_a, weight_b = weight_a * inverse, weight_b * inverse
        start = pl.multiple_of(g * (GROUP * DH), DH)
        for h in range(GROUP):
            cut = pl.ds(start + h * DH, DH)
            t_own[s, :, cut] = weight_a[:, h:h + 1] * t_own[s, :, cut] + weight_b[
                :, h:h + 1
            ] * t_recv[s, :, cut].astype(jnp.float32)
        return carry

    lax.fori_loop(0, seqs * groups, text_merge, 0)

    for s in range(seqs):
        for piece in visual_back[s]:
            piece.wait_recv()

        def own_step(g, carry, s=s):
            overall, total, weights = visual_weights(s, g, 0)
            theirs = unpacked(v_stat_recv[s], g)
            joint = jnp.maximum(overall, theirs)
            weight_a = jnp.exp(overall - joint)
            weight_b = jnp.exp(theirs - joint) * totals_of(theirs)
            inverse = 1.0 / (weight_a * total + weight_b)
            weights = [w * (weight_a * inverse) for w in weights]
            weight_b = weight_b * inverse
            start = pl.multiple_of(g * (GROUP * DH), DH)
            for h in range(GROUP):
                cut = pl.ds(start + h * DH, DH)
                visual = weighted(s, g, 0, h, weights) + weight_b[:, h:h + 1] * v_recv[
                    s, :, cut
                ].astype(jnp.float32)
                gate = gate_buf[s, g, :, h:h + 1]
                out_ref[s, :, cut] = ((1.0 - gate) * t_own[s, :, cut] + gate * visual).astype(
                    jnp.bfloat16
                )
            return carry

        lax.fori_loop(0, groups, own_step, 0)

    for copy in copies:
        copy.wait_send()


def pair_plan(n, heads_split, queries, text_keys, text_values, visual_keys, visual_values,
              gate_weight, text_offsets, image_sequence, image_position):
    seqs, rows, columns = queries.shape
    groups = text_keys.shape[-1] // DH
    here, tokens, kv_columns = visual_keys.shape
    members, blocks = n // 4, n // 2
    slots = blocks * here
    per_seq = image_sequence.shape[0] // seqs
    smem = pl.BlockSpec(memory_space=pltpu.SMEM)
    vmem = pl.BlockSpec(memory_space=pltpu.VMEM)
    bf16, f32 = jnp.bfloat16, jnp.float32
    count = 1 + 4 * (members - 1) + 2 + here * (2 * (members - 1) * (1 + len(chunks_of(tokens))) + 2) + 2 + 2 * seqs + heads_split - 1
    stats = (seqs, groups, rows, LANES)
    sent_stats = (seqs, rows, LANES)
    gate_shape = (seqs, rows, gate_weight.shape[-1])
    pairs = 2 * rows * GROUP * groups * (slots * tokens + seqs * blocks * rows)
    return pl.pallas_call(
        functools.partial(attention_kernel, n, heads_split, seqs, rows, groups, here, per_seq),
        in_specs=[smem] * 3 + [vmem] * 6,
        out_specs=vmem,
        out_shape=jax.ShapeDtypeStruct(queries.shape, bf16),
        scratch_shapes=[
            pltpu.VMEM(queries.shape, bf16),
            pltpu.VMEM((blocks - 1, *text_keys.shape), bf16),
            pltpu.VMEM((blocks - 1, *text_keys.shape), bf16),
            pltpu.VMEM((blocks - 1, *visual_keys.shape), bf16),
            pltpu.VMEM((blocks - 1, *visual_keys.shape), bf16),
            pltpu.VMEM((slots, 2, rows, columns), f32),
            pltpu.VMEM((slots, 2, groups, rows, LANES), f32),
            pltpu.VMEM((seqs, blocks * rows, kv_columns), bf16),
            pltpu.VMEM((seqs, blocks * rows, kv_columns), bf16),
            pltpu.VMEM(queries.shape, bf16),
            pltpu.VMEM(sent_stats, f32),
            pltpu.VMEM(queries.shape, bf16),
            pltpu.VMEM(sent_stats, f32),
            pltpu.VMEM(queries.shape, bf16),
            pltpu.VMEM(sent_stats, f32),
            pltpu.VMEM(queries.shape, bf16),
            pltpu.VMEM(sent_stats, f32),
            pltpu.VMEM(queries.shape, f32),
            pltpu.VMEM(stats, f32),
            pltpu.VMEM(gate_shape, f32),
            pltpu.VMEM((heads_split - 1, *gate_shape), f32),
            pltpu.VMEM(stats, f32),
            pltpu.SemaphoreType.DMA((count,)),
            pltpu.SemaphoreType.DMA((count,)),
        ],
        compiler_params=pltpu.CompilerParams(
            collective_id=0, has_side_effects=True, vmem_limit_bytes=60 << 20
        ),
        cost_estimate=pl.CostEstimate(
            flops=4 * pairs * DH, bytes_accessed=16 << 20, transcendentals=pairs
        ),
    )(
        text_offsets, image_sequence, image_position,
        queries, text_keys, text_values, visual_keys, visual_values, gate_weight.T,
    )


def line_kernel(
    seqs, rows, here, per_seq, heads_split,
    offsets, image_sequence, image_position,
    queries, text_keys, text_values, visual_keys, visual_values, gate_weight,
    out_ref,
    q_own, q_mate, q_out, tkv, tkv_out, vk, vv, k_out, v_out, part, part_mate, stat, stat_mate,
    side_part, side_stat, late_part, late_mate, late_stat, late_mate_stat, late_side, late_side_stat,
    t_own, t_send, t_recv, early, gate_own, gate_recv, gate_buf, weights, send_sems, recv_sems,
):
    me = lax.axis_index("seq")
    core = lax.axis_index("kvh")
    z, x = me // 2, me % 2
    half = z // 2
    inner = (z + 1) // 2 % 2
    side = z * 2 + 1 - x
    mate = (half * 2 + 1 - z % 2) * 2 + x
    cross = (3 - z) * 2 + x
    diag = (half * 2 + 1 - z % 2) * 2 + 1 - x
    twins = [(core + k) % heads_split for k in range(1, heads_split)]
    width = GROUP * DH
    group = 2 * here
    slots = 4 * group
    near, outer, across, far = 0, 1, 2, 3
    mine = 1 - inner

    def chip(kind):
        place = jnp.where(kind == outer, 3 * half, 1 + half)
        place = jnp.where(kind == across, 2 - half, place)
        return jnp.where(kind == far, 3 - 3 * half, place)

    def device(kind, sub):
        return chip(kind) * 2 + (x + sub) % 2

    def image_of(slot):
        return device(slot // group, slot // here % 2) * here + slot % here

    last = slots - 1
    lates = (last, last - here)

    barrier = pltpu.get_barrier_semaphore()
    for peer in (side, mate, cross, diag):
        pl.semaphore_signal(
            barrier, inc=1, device_id={"seq": peer}, device_id_type=pl.DeviceIdType.MESH
        )
    for twin in twins:
        pl.semaphore_signal(
            barrier, inc=1, device_id={"kvh": twin}, device_id_type=pl.DeviceIdType.MESH
        )

    bases, used = {}, 0
    for name, count in (
        ("x_text", 1), ("x_q", 1), ("x_k", here), ("x_v", here), ("x_t", 1), ("x_part", slots),
        ("x_stat", slots), ("late", 6), ("edge", 3), ("m_text", 8), ("m_q", 2), ("m_k", slots), ("m_v", slots),
        ("m_part", slots), ("m_stat", slots), ("c_text", 8), ("c_k", slots), ("c_v", slots),
        ("gate", heads_split),
    ):
        bases[name] = used
        used += count

    def copy(name, index, src, dst, peer, axis="seq"):
        return pltpu.make_async_remote_copy(
            src_ref=src,
            dst_ref=dst,
            send_sem=send_sems.at[bases[name] + index],
            recv_sem=recv_sems.at[bases[name] + index],
            device_id={axis: peer},
            device_id_type=pl.DeviceIdType.MESH,
        )

    x_text = copy("x_text", 0, tkv_out, tkv.at[mine, 1], side)
    x_q = copy("x_q", 0, q_out, q_own.at[:, 1], side)
    away = pl.multiple_of((1 - x) * DH, DH)

    def x_k(j):
        return copy("x_k", j, k_out.at[j], vk.at[mine * group + here + j], side)

    def x_v(j):
        return copy("x_v", j, v_out.at[j], vv.at[mine * group + here + j], side)

    x_t = copy("x_t", 0, t_send, t_recv, side)

    def x_part(i):
        return copy("x_part", i, part.at[i, 1], side_part.at[i], side)

    def x_stat(i):
        return copy("x_stat", i, stat.at[i], side_stat.at[i], side)

    def m_text(kind, sub):
        return copy("m_text", kind * 2 + sub, tkv.at[kind, sub], tkv.at[kind, sub], mate)

    def m_q(sub):
        return copy("m_q", sub, q_own.at[:, sub], q_mate.at[:, sub], mate)

    def m_k(i):
        return copy("m_k", i, vk.at[i], vk.at[i], mate)

    def m_v(i):
        return copy("m_v", i, vv.at[i], vv.at[i], mate)

    def m_part(i):
        return copy("m_part", i, part_mate.at[i], part.at[i], mate)

    def m_stat(i):
        return copy("m_stat", i, stat_mate.at[i], stat.at[i], mate)

    def c_text(kind, sub):
        return copy("c_text", (kind + 2) * 2 + sub, tkv.at[kind, sub], tkv.at[kind + 2, sub], cross)

    def c_k(i):
        return copy("c_k", i, vk.at[i], vk.at[i + 2 * group], cross)

    def c_v(i):
        return copy("c_v", i, vv.at[i], vv.at[i + 2 * group], cross)

    late_own = (
        copy("late", 1, late_stat, late_side_stat, side),
        copy("late", 0, late_part.at[1], late_side, side),
    )
    late_to_mate = (
        copy("late", 3, late_mate_stat, late_stat, mate),
        copy("late", 2, late_mate.at[0], late_part.at[0], mate),
    )
    late_to_diag = (
        copy("late", 5, late_mate_stat, late_side_stat, diag),
        copy("late", 4, late_mate.at[1], late_side, diag),
    )

    edge = last - 1
    edge_to_mate = (
        copy("edge", 0, part_mate.at[edge, 0], part.at[edge, 0], mate),
        copy("m_stat", edge, stat_mate.at[edge], stat.at[edge], mate),
    )
    edge_to_diag = (
        copy("edge", 1, part_mate.at[edge, 1], side_part.at[edge], diag),
        copy("edge", 2, stat_mate.at[edge], side_stat.at[edge], diag),
    )

    home = pl.multiple_of(x * DH, DH)
    home_q = x * width
    away_q = (1 - x) * width

    def stack_q(s, carry):
        for h in range(GROUP):
            q_own[s, 0, h] = queries[s, :, pl.ds(pl.multiple_of(home_q + h * DH, DH), DH)]
            q_out[s, h] = queries[s, :, pl.ds(pl.multiple_of(away_q + h * DH, DH), DH)]
        return carry

    for kind, source in enumerate((text_keys, text_values)):
        tkv[mine, 0, kind] = source[:, :, pl.ds(home, DH)]
        tkv_out[kind] = source[:, :, pl.ds(away, DH)]
    lax.fori_loop(0, seqs, stack_q, 0)
    def keep_home(j):
        vk[mine * group + j] = visual_keys[:, j, pl.ds(home, DH)]
        vv[mine * group + j] = visual_values[:, j, pl.ds(home, DH)]

    def keep_away(j):
        k_out[j] = visual_keys[:, j, pl.ds(away, DH)]
        v_out[j] = visual_values[:, j, pl.ds(away, DH)]

    keep_home(0)
    pl.semaphore_wait(barrier, 4 + len(twins))

    x_text.start()
    x_q.start()

    @pl.when(inner == 1)
    def _():
        c_text(near, 0).start()
        m_text(near, 0).start()
        c_k(0).start()
        c_v(0).start()
        m_k(0).start()
        m_v(0).start()

    @pl.when(inner == 0)
    def _():
        m_text(outer, 0).start()
        m_k(group).start()

    for j in range(here):
        if j:
            keep_home(j)
        keep_away(j)
        x_k(j).start()
        x_v(j).start()

    lane = lax.broadcasted_iota(jnp.int32, (rows, LANES), 1)

    def softmax(scores):
        peak = jnp.max(scores, axis=-1, keepdims=True)
        return peak, jnp.exp2((scores - peak) * SCALE2).astype(jnp.bfloat16)

    def scores_of(q, k):
        return lax.dot_general(q, k, (((1,), (1,)), ((), ())), preferred_element_type=jnp.float32)

    def attend(i, q_ref, part_ref, stat_ref):
        attend_to(i, q_ref, part_ref.at[i], stat_ref.at[i])

    def attend_to(i, q_ref, part_ref, stat_ref):
        apply_values(i, apply_keys(i, q_ref), part_ref, stat_ref)

    def apply_keys(i, q_ref):
        q = q_ref[image_sequence[image_of(i)]].reshape(2, GROUP * rows, DH)
        k = vk[i]
        scores = [scores_of(q[0], k), scores_of(q[1], k)]
        return [softmax(scores[0]), softmax(scores[1])]

    def apply_values(i, halves, part_ref, stat_ref):
        v = vv[i]
        v = jnp.concatenate([v, jnp.ones_like(v)], axis=1)
        packed = []
        for b in range(2):
            peak, expd = halves[b]
            num = jnp.dot(expd, v, preferred_element_type=jnp.float32)
            total = num[:, DH:]
            part_ref[b] = (num[:, :DH] * (1.0 / total)).astype(jnp.bfloat16).reshape(GROUP, rows, DH)
            peaks = jnp.zeros((rows, LANES), jnp.float32)
            totals = jnp.ones((rows, LANES), jnp.float32)
            for h in range(GROUP):
                at_h = slice(h * rows, (h + 1) * rows)
                peaks = jnp.where(lane == h, peak[at_h], peaks)
                totals = jnp.where(lane == h, total[at_h], totals)
            packed.append(peaks * SCALE + jnp.log(totals))
        stat_ref[...] = jnp.concatenate(packed, axis=0).T[:8]

    def attend_own(i):
        attend(i, q_own, part, stat)
        x_part(i).start()
        x_stat(i).start()

    def attend_mate(i):
        attend(i, q_mate, part_mate, stat_mate)

        @pl.when(i != edge)
        def _():
            m_part(i).start()
            m_stat(i).start()

        @pl.when(i == edge)
        def _():
            for piece in (*edge_to_mate, *edge_to_diag):
                piece.start()

    def loop(start, stop, body):
        def step(i, carry):
            body(i)
            return carry

        lax.fori_loop(start, stop, step, 0)

    @pl.when(inner == 1)
    def _():
        x_text.wait_recv()
        c_text(near, 1).start()
        m_text(near, 1).start()
        for j in range(1, here):
            m_k(j).start()
            m_v(j).start()
        for sub in range(2):
            m_text(outer, sub).wait_recv()
            c_text(outer, sub).start()
        for j in range(1, here):
            c_k(j).start()
            c_v(j).start()
        c_text(near, 0).wait_recv()
        m_text(across, 0).start()

    @pl.when(inner == 0)
    def _():
        x_text.wait_recv()
        m_text(outer, 1).start()
        m_q(0).start()

    rest = gate_weight[...]
    q_all = queries[...].reshape(seqs * rows, queries.shape[-1])
    logits = 0.0
    for _ in range(3):
        term = rest.astype(jnp.bfloat16)
        rest = rest - term.astype(jnp.float32)
        logits = logits + lax.dot_general(
            q_all, term, (((1,), (1,)), ((), ())), preferred_element_type=jnp.float32
        )
    gate_own[...] = logits.reshape(gate_own.shape)
    gates = [copy("gate", k, gate_own, gate_recv.at[k], twin, "kvh") for k, twin in enumerate(twins)]
    for piece in gates:
        piece.start()


    x_q.wait_recv()

    @pl.when(inner == 1)
    def _():
        loop(0, here, attend_own)
        c_text(near, 1).wait_recv()
        m_text(across, 1).start()
        x_k(0).wait_recv()
        c_k(here).start()
        for sub in range(2):
            c_text(outer, sub).wait_recv()
            m_text(far, sub).start()
        x_v(0).wait_recv()
        c_v(here).start()

    @pl.when(inner == 0)
    def _():
        m_q(1).start()
        m_v(group).start()
        for j in range(1, here):
            m_k(group + j).start()
            m_v(group + j).start()
        loop(group, group + here, attend_own)
        for j in range(here):
            x_k(j).wait_recv()
            m_k(group + here + j).start()
            x_v(j).wait_recv()
            m_v(group + here + j).start()
        for kind in (near, across, far):
            for sub in range(2):
                m_text(kind, sub).wait_recv()

    count = 8 * rows
    key_lane = lax.broadcasted_iota(jnp.int32, (rows, count), 1)
    key_row = lax.broadcasted_iota(jnp.int32, (rows, count), 0)
    key_pos = key_lane % rows
    for kind in range(4):
        for sub in range(2):
            b = kind * 2 + sub
            inside = (key_lane >= b * rows) & (key_lane < (b + 1) * rows)
            key_pos = key_pos + jnp.where(inside, offsets[device(kind, sub)], 0)
    place = [offsets[me], offsets[side]]
    biases = [jnp.where(key_pos <= key_row + p, 0.0, NEG) for p in place]

    def text_step(s):
        q = q_own[s].reshape(2, GROUP * rows, DH)
        k = tkv[:, :, 0, s].reshape(count, DH)
        v = tkv[:, :, 1, s].reshape(count, DH)
        v = jnp.concatenate([v, jnp.ones_like(v)], axis=1)
        for b in range(2):
            scores = scores_of(q[b], k).reshape(GROUP, rows, count) + biases[b][None]
            peak, expd = softmax(scores.reshape(GROUP * rows, count))
            num = jnp.dot(expd, v, preferred_element_type=jnp.float32)
            out = (num[:, :DH] * (1.0 / num[:, DH:])).reshape(GROUP, rows, DH)
            if b == 0:
                t_own[0, s] = out
            else:
                t_send[s] = out.astype(jnp.bfloat16)

    loop(0, seqs, text_step)
    x_t.start()

    @pl.when(inner == 1)
    def _():
        for j in range(1, here):
            x_k(j).wait_recv()
            c_k(here + j).start()
            x_v(j).wait_recv()
            c_v(here + j).start()

    for piece in gates:
        piece.wait_recv()
    for s in range(seqs):
        logits = gate_own[s]
        for k in range(len(twins)):
            logits = logits + gate_recv[k, s]
        heads = 2 * GROUP
        mix = logits[:, :heads]
        for c in range(1, heads_split):
            mix = jnp.where(core == c, logits[:, c * heads:(c + 1) * heads], mix)
        mix = jax.nn.sigmoid(mix)
        for g in range(2):
            gate_buf[s, g, :, :GROUP] = mix[:, g * GROUP:(g + 1) * GROUP]

    owners = [image_sequence[image_of(jnp.int32(i))] for i in range(slots)]
    positions = [image_position[image_of(jnp.int32(i))] for i in range(slots)]

    def table(late):
        at, thresholds = [], []
        for s in range(seqs):
            slot_here = [jnp.int32(0)] * per_seq
            threshold_here = [jnp.int32(FAR)] * per_seq
            found = jnp.int32(0)
            for slot, (owner, position) in enumerate(zip(owners, positions)):
                if slot == late:
                    continue
                hit = owner == s
                for j in range(per_seq):
                    take = hit & (found == j)
                    slot_here[j] = jnp.where(take, slot, slot_here[j])
                    threshold_here[j] = jnp.where(take, position, threshold_here[j])
                found = found + jnp.where(hit, 1, 0)
            at += slot_here
            thresholds += threshold_here
        return at, thresholds

    tables = [table(late) for late in lates]

    @pl.when(inner == 1)
    def _():
        for sub in range(2):
            m_q(sub).wait_recv()

        def own_step(i):
            attend_mate(i)
            attend_own(i)

        loop(here, group, own_step)

        def stream_step(c):
            @pl.when((c >= here) & (c < here + group))
            def _():
                o = group + c - here
                m_k(o).wait_recv()
                c_k(o).start()
                m_v(o).wait_recv()
                c_v(o).start()
                attend_own(o)

            c_k(c).wait_recv()
            c_v(c).wait_recv()
            attend_mate(2 * group + c)
            attend_own(2 * group + c)

        loop(0, 2 * group - 1, stream_step)

    @pl.when(inner == 0)
    def _():
        loop(group + here, 2 * group, attend_own)
        for j in range(here):
            m_k(j).wait_recv()
            m_v(j).wait_recv()
        loop(0, here, attend_own)

        def forward(i):
            m_part(i).wait_recv()
            m_stat(i).wait_recv()
            x_part(i).start()
            x_stat(i).start()

        loop(here, group, forward)
        loop(2 * group, edge, forward)
        for piece in edge_to_mate:
            piece.wait_recv()


    row_pos = lax.broadcasted_iota(jnp.int32, (rows, LANES), 0) + place[0]
    real = lane % 8 < GROUP

    def spread(values, join):
        stride = 8
        while stride < 8 * per_seq:
            up = pltpu.roll(values, LANES - stride, 1)
            down = pltpu.roll(values, stride, 1)
            values = join(values, jnp.where(lane // stride % 2 == 0, up, down))
            stride *= 2
        return values

    def lanes_of(choices, size):
        limits = jnp.full((rows, LANES), FAR, jnp.int32)
        for i, threshold in enumerate(choices):
            limits = jnp.where(lane // size == i, threshold, limits)
        return (limits <= row_pos) & real

    def early_merge(g):
        absolute = x if g == 0 else 1 - x
        at, thresholds = tables[g]
        if g == 1:
            at = [i + here * (1 - 2 * (i // here % 2)) for i in at]
        seen = lanes_of(thresholds, 8)
        gathered = jnp.concatenate([(stat, side_stat)[g][i] for i in at], axis=0).T
        lse = jnp.where(seen, gathered[g * rows:(g + 1) * rows], NEG)
        overall = spread(lse, jnp.maximum)
        weight = jnp.where(seen, jnp.exp(lse - overall), 0.0)
        total = spread(weight, jnp.add)
        gate = 0.0
        for s in range(seqs):
            here_gate = jnp.where(lane < GROUP, gate_buf[s, absolute], 0.0)
            gate = gate + (pltpu.roll(here_gate, s * per_seq * 8, 1) if s else here_gate)
        gate = spread(gate, jnp.add)
        weights[g, 0] = overall
        weights[g, 1] = total
        weights[g, 2] = gate
        weights[g, 3] = weight * (gate / jnp.where(total > 0.0, total, 1.0))
        for s in range(seqs):
            for h in range(GROUP):
                visual = 0.0
                for j in range(per_seq):
                    i = at[s * per_seq + j]
                    piece = part[i, 0, h] if g == 0 else side_part[i, h]
                    k = (s * per_seq + j) * 8 + h
                    visual = visual + weights[g, 3, :, k:k + 1] * piece.astype(jnp.float32)
                early[g, s, h] = visual
                k = s * per_seq * 8 + h
                text = t_own[g, s, h] if g == 0 else t_recv[s, h].astype(jnp.float32)
                t_own[g, s, h] = (1.0 - weights[g, 2, :, k:k + 1]) * text

    def late_weights(g):
        late = image_of(jnp.int32(lates[g]))
        limits = [jnp.where(image_sequence[late] == s, image_position[late], FAR) for s in range(seqs)]
        seen = lanes_of(limits, 8 * per_seq)
        source = (late_stat, late_side_stat)[g][...]
        gathered = jnp.concatenate([source] * (LANES // 8), axis=0).T
        lse = jnp.where(seen, gathered[g * rows:(g + 1) * rows], NEG)
        before = weights[g, 0]
        overall = jnp.maximum(before, lse)
        weight_a = jnp.where(weights[g, 1] > 0.0, weights[g, 1] * jnp.exp(before - overall), 0.0)
        weight_b = jnp.where(seen, jnp.exp(lse - overall), 0.0)
        total = weight_a + weight_b
        inverse = 1.0 / jnp.where(total > 0.0, total, 1.0)
        weights[g, 0] = weight_a * inverse
        weights[g, 1] = weight_b * inverse * weights[g, 2]
        for s in range(seqs):
            for h in range(GROUP):
                k = s * per_seq * 8 + h
                early[g, s, h] = t_own[g, s, h] + weights[g, 0, :, k:k + 1] * early[g, s, h]

    def late_apply(g):
        absolute = x if g == 0 else 1 - x
        for h in range(GROUP):
            piece = (late_part[0, h] if g == 0 else late_side[h]).astype(jnp.float32)
            cut = pl.ds(pl.multiple_of(absolute * width + h * DH, DH), DH)
            for s in range(seqs):
                k = s * per_seq * 8 + h
                out_ref[s, :, cut] = (
                    early[g, s, h] + weights[g, 1, :, k:k + 1] * piece
                ).astype(jnp.bfloat16)

    def receive(i):
        x_part(i).wait_recv()
        x_stat(i).wait_recv()

    early_merge(0)

    @pl.when(inner == 1)
    def _():
        c_k(2 * group - 1).wait_recv()
        mate_halves = apply_keys(last, q_mate)
        own_halves = apply_keys(last, q_own)
        c_v(2 * group - 1).wait_recv()
        apply_values(last, mate_halves, late_mate, late_mate_stat)
        for piece in (late_to_mate[0], late_to_diag[0], late_to_mate[1], late_to_diag[1]):
            piece.start()
        apply_values(last, own_halves, late_part, late_stat)
        for piece in late_own:
            piece.start()

    loop(0, edge, receive)

    @pl.when(inner == 1)
    def _():
        receive(edge)

    @pl.when(inner == 0)
    def _():
        for piece in edge_to_diag:
            piece.wait_recv()

    x_t.wait_recv()
    early_merge(1)

    def arrive(index):
        @pl.when(inner == 0)
        def _():
            late_to_diag[index].wait_recv()

        @pl.when(inner == 1)
        def _():
            late_own[index].wait_recv()

    @pl.when(inner == 0)
    def _():
        late_to_mate[0].wait_recv()

    late_weights(0)
    arrive(0)
    late_weights(1)

    @pl.when(inner == 0)
    def _():
        late_to_mate[1].wait_recv()

    late_apply(0)
    arrive(1)
    late_apply(1)

    def sent(piece):
        piece.wait_send()

    sent(x_text)
    sent(x_q)
    sent(x_t)
    for j in range(here):
        sent(x_k(j))
        sent(x_v(j))
    for piece in gates:
        sent(piece)

    def all_sent(i):
        sent(x_part(i))
        sent(x_stat(i))

    loop(0, edge, all_sent)

    @pl.when(inner == 1)
    def _():
        for sub in range(2):
            for kind in (near, outer):
                sent(c_text(kind, sub))
            for kind in (near, across, far):
                sent(m_text(kind, sub))
        for j in range(here):
            sent(m_k(j))
            sent(m_v(j))

        def stream_sent(i):
            sent(c_k(i))
            sent(c_v(i))

        def mate_sent(i):
            sent(m_part(i))
            sent(m_stat(i))

        loop(0, 2 * group, stream_sent)
        loop(here, group, mate_sent)
        loop(2 * group, edge, mate_sent)
        all_sent(edge)
        for piece in (*edge_to_mate, *edge_to_diag, *late_to_mate, *late_to_diag, *late_own):
            sent(piece)

    @pl.when(inner == 0)
    def _():
        for sub in range(2):
            sent(m_text(outer, sub))
            sent(m_q(sub))

        def stream_sent(i):
            sent(m_k(i))
            sent(m_v(i))

        loop(group, 2 * group, stream_sent)


def line_plan(heads_split, queries, text_keys, text_values, visual_keys, visual_values,
              gate_weight, text_offsets, image_sequence, image_position):
    seqs, rows, columns = queries.shape
    here, tokens, _ = visual_keys.shape
    slots = image_sequence.shape[0]
    per_seq = slots // seqs
    smem = pl.BlockSpec(memory_space=pltpu.SMEM)
    vmem = pl.BlockSpec(memory_space=pltpu.VMEM)
    bf16, f32 = jnp.bfloat16, jnp.float32
    stacked = (seqs, 2, GROUP, rows, DH)
    one = (seqs, GROUP, rows, DH)
    gate_shape = (seqs, rows, gate_weight.shape[-1])
    count = 2 + 2 * here + 1 + 2 * slots + 6 + 3 + 10 + 4 * slots + 8 + 2 * slots + heads_split
    pairs = 2 * rows * GROUP * (2 * slots * tokens + seqs * 8 * rows)
    return pl.pallas_call(
        functools.partial(line_kernel, seqs, rows, here, per_seq, heads_split),
        in_specs=[smem] * 3 + [vmem] * 6,
        out_specs=vmem,
        out_shape=jax.ShapeDtypeStruct(queries.shape, bf16),
        scratch_shapes=[
            pltpu.VMEM(stacked, bf16),
            pltpu.VMEM(stacked, bf16),
            pltpu.VMEM(one, bf16),
            pltpu.VMEM((4, 2, 2, seqs, rows, DH), bf16),
            pltpu.VMEM((2, seqs, rows, DH), bf16),
            pltpu.VMEM((slots, tokens, DH), bf16),
            pltpu.VMEM((slots, tokens, DH), bf16),
            pltpu.VMEM((here, tokens, DH), bf16),
            pltpu.VMEM((here, tokens, DH), bf16),
            pltpu.VMEM((slots, 2, GROUP, rows, DH), bf16),
            pltpu.VMEM((slots, 2, GROUP, rows, DH), bf16),
            pltpu.VMEM((slots, 8, LANES), f32),
            pltpu.VMEM((slots, 8, LANES), f32),
            pltpu.VMEM((slots, GROUP, rows, DH), bf16),
            pltpu.VMEM((slots, 8, LANES), f32),
            pltpu.VMEM((2, GROUP, rows, DH), bf16),
            pltpu.VMEM((2, GROUP, rows, DH), bf16),
            pltpu.VMEM((8, LANES), f32),
            pltpu.VMEM((8, LANES), f32),
            pltpu.VMEM((GROUP, rows, DH), bf16),
            pltpu.VMEM((8, LANES), f32),
            pltpu.VMEM((2, *one), f32),
            pltpu.VMEM(one, bf16),
            pltpu.VMEM(one, bf16),
            pltpu.VMEM((2, *one), f32),
            pltpu.VMEM(gate_shape, f32),
            pltpu.VMEM((heads_split - 1, *gate_shape), f32),
            pltpu.VMEM((seqs, 2, rows, LANES), f32),
            pltpu.VMEM((2, 4, rows, LANES), f32),
            pltpu.SemaphoreType.DMA((count,)),
            pltpu.SemaphoreType.DMA((count,)),
        ],
        compiler_params=pltpu.CompilerParams(
            collective_id=1, has_side_effects=True, vmem_limit_bytes=60 << 20
        ),
        cost_estimate=pl.CostEstimate(
            flops=4 * pairs * DH, bytes_accessed=16 << 20, transcendentals=pairs
        ),
    )(
        text_offsets, image_sequence, image_position,
        queries, text_keys, text_values,
        visual_keys.transpose(1, 0, 2), visual_values.transpose(1, 0, 2), gate_weight.T,
    )


def on_device(n, heads_split, queries, text_keys, *rest):
    groups = text_keys.shape[-1] // DH
    images = rest[-2].shape[0]
    line = n // 2
    if line - 2 == 2 and groups == 2 and images * 8 == LANES and 2 * queries.shape[1] == LANES:
        return line_plan(heads_split, queries, text_keys, *rest)
    return pair_plan(n, heads_split, queries, text_keys, *rest)


def solution(mesh):
    return jax.shard_map(
        functools.partial(on_device, mesh.shape["seq"], mesh.shape["kvh"]),
        mesh=mesh,
        in_specs=(
            P("batch", "seq", "kvh"),
            P("batch", "seq", "kvh"),
            P("batch", "seq", "kvh"),
            P(("batch", "seq"), None, "kvh"),
            P(("batch", "seq"), None, "kvh"),
            P("kvh", None),
            P("batch"),
            P("batch"),
            P("batch"),
        ),
        out_specs=P("batch", "seq", "kvh"),
        check_vma=False,
    )
```

```python
import functools
import math

import jax
import jax.numpy as jnp
from jax import lax
from jax.experimental import pallas as pl
from jax.experimental.pallas import tpu as pltpu
from jax.sharding import PartitionSpec as P

DH = 128
GROUP = 7
LANES = 128
HALF = LANES // 2
CHUNKS = 4
TILE = 16
NEG = -1e30
FLOOR = -1e29
FAR = 1 << 30
SCALE = 1.0 / DH ** 0.5
SCALE2 = SCALE * math.log2(math.e)


def chunks_of(tokens):
    size = -(-tokens // (CHUNKS * TILE)) * TILE
    return [pl.ds(a, min(size, tokens - a)) for a in range(0, tokens, size)]


def heads_of(ref, lead, g):
    start = pl.multiple_of(g * (GROUP * DH), DH)
    return jnp.concatenate(
        [ref[lead, :, pl.ds(start + h * DH, DH)] for h in range(GROUP)], axis=0
    )


def put_heads(ref, lead, g, stacked):
    rows = stacked.shape[0] // GROUP
    start = pl.multiple_of(g * (GROUP * DH), DH)
    for h in range(GROUP):
        ref[(*lead, slice(None), pl.ds(start + h * DH, DH))] = stacked[h * rows:(h + 1) * rows]


def pack_stats(peak, total, rows):
    lane = lax.broadcasted_iota(jnp.int32, (rows, LANES), 1)
    packed = jnp.zeros((rows, LANES), jnp.float32)
    for h in range(GROUP):
        here = slice(h * rows, (h + 1) * rows)
        packed = jnp.where(lane == h, peak[here], packed)
        packed = jnp.where(lane == HALF + h, total[here], packed)
    return packed


def totals_of(packed):
    return pltpu.roll(packed, HALF, 1)


def softmax_parts(q, keys, values, bias):
    scores = lax.dot_general(
        q, keys, (((1,), (1,)), ((), ())), preferred_element_type=jnp.float32
    )
    if bias is not None:
        rows, count = bias.shape
        scores = (scores.reshape(GROUP, rows, count) + bias[None]).reshape(GROUP * rows, count)
    peak = jnp.maximum(jnp.max(scores, axis=-1, keepdims=True), FLOOR)
    expd = jnp.exp2((scores - peak) * SCALE2)
    total = jnp.sum(expd, axis=-1, keepdims=True)
    num = jnp.dot(expd.astype(jnp.bfloat16), values, preferred_element_type=jnp.float32)
    return peak * SCALE, total, num


def attention_kernel(
    n, heads_split, seqs, rows, groups, here, per_seq,
    offsets, image_sequence, image_position,
    queries, text_keys, text_values, visual_keys, visual_values, gate_weight,
    out_ref,
    q_pair, far_tk, far_tv, far_ik, far_iv, num, stat, cat_k, cat_v,
    t_send, t_stat_send, t_recv, t_stat_recv, v_send, v_stat_send, v_recv, v_stat_recv,
    t_own, t_own_stat, gate_own, gate_recv, gate_buf, send_sems, recv_sems,
):
    me = lax.axis_index("seq")
    core = lax.axis_index("kvh")
    members = n // 4
    blocks = n // 2
    pair = me // 4 * 4 + (me + 2) % 4
    side = me // 2 * 2 + (me + 1) % 2
    others = [(me // 4 + k) % members * 4 + me % 4 for k in range(1, members)]
    twins = [(core + k) % heads_split for k in range(1, heads_split)]

    far_ids = [(me // 4 + members - k) % members * 4 + me % 4 for k in range(1, members)]
    sources = [me, side] + far_ids + [f // 2 * 2 + (f + 1) % 2 for f in far_ids]
    places = [offsets[i] for i in (me, pair, *sources)]
    image_ids = [source * here + j for source in sources for j in range(here)]
    owners = [image_sequence[i] for i in image_ids]
    positions = [image_position[i] for i in image_ids]
    at, thresholds = [], []
    for s in range(seqs):
        slot_here = [jnp.int32(0)] * per_seq
        threshold_here = [jnp.int32(FAR)] * per_seq
        found = jnp.int32(0)
        for slot, (owner, position) in enumerate(zip(owners, positions)):
            hit = owner == s
            for j in range(per_seq):
                take = hit & (found == j)
                slot_here[j] = jnp.where(take, slot, slot_here[j])
                threshold_here[j] = jnp.where(take, position, threshold_here[j])
            found = found + jnp.where(hit, 1, 0)
        at += slot_here
        thresholds += threshold_here

    barrier = pltpu.get_barrier_semaphore()
    for peer in (pair, side, *others):
        pl.semaphore_signal(
            barrier, inc=1, device_id={"seq": peer}, device_id_type=pl.DeviceIdType.MESH
        )
    for twin in twins:
        pl.semaphore_signal(
            barrier, inc=1, device_id={"kvh": twin}, device_id_type=pl.DeviceIdType.MESH
        )
    pl.semaphore_wait(barrier, 2 + len(others) + len(twins))

    copies = []
    chunks = chunks_of(visual_values.shape[1])

    def send(src, dst, peer, axis="seq"):
        copy = pltpu.make_async_remote_copy(
            src_ref=src,
            dst_ref=dst,
            send_sem=send_sems.at[len(copies)],
            recv_sem=recv_sems.at[len(copies)],
            device_id={axis: peer},
            device_id_type=pl.DeviceIdType.MESH,
        )
        copy.start()
        copies.append(copy)
        return copy

    def slot_of(kind, k=0):
        return {"side": 0, "far": k, "diag": members - 1 + k}[kind]

    q_copy = send(queries, q_pair, pair)
    text_far = []
    for k, peer in enumerate(others, 1):
        s = slot_of("far", k)
        text_far.append((send(text_keys, far_tk.at[s], peer), send(text_values, far_tv.at[s], peer)))
    text_side = (send(text_keys, far_tk.at[0], side), send(text_values, far_tv.at[0], side))
    image_far = {}
    image_side = {}
    for j in range(here):
        for k, peer in enumerate(others, 1):
            s = slot_of("far", k)
            image_far[k, j] = [send(visual_keys.at[j], far_ik.at[s, j], peer)] + [
                send(visual_values.at[j, cut], far_iv.at[s, j, cut], peer) for cut in chunks
            ]
        image_side[j] = (
            send(visual_keys.at[j], far_ik.at[0, j], side),
            send(visual_values.at[j], far_iv.at[0, j], side),
        )

    def attend(keys, values, index, sides):
        owner = owners[index]

        def step(g, carry):
            at_g = pl.ds(pl.multiple_of(g * DH, DH), DH)
            k, v = keys[:, at_g], values[:, at_g]
            for which in sides:
                q = heads_of(queries if which == 0 else q_pair, owner, g)
                peak, total, out = softmax_parts(q, k, v, None)
                put_heads(num, (index, which), g, out)
                stat[index, which, g] = pack_stats(peak, total, rows)
            return carry

        lax.fori_loop(0, groups, step, 0)

    rest = gate_weight[...]
    q_all = queries[...].reshape(seqs * rows, queries.shape[-1])
    logits = 0.0
    for _ in range(3):
        term = rest.astype(jnp.bfloat16)
        rest = rest - term.astype(jnp.float32)
        logits = logits + lax.dot_general(
            q_all, term, (((1,), (1,)), ((), ())), preferred_element_type=jnp.float32
        )
    gate_own[...] = logits.reshape(gate_own.shape)
    t_stat_send[...] = jnp.zeros_like(t_stat_send)
    v_stat_send[...] = jnp.zeros_like(v_stat_send)

    for j in range(here):
        attend(visual_keys.at[j], visual_values.at[j], j, (0,))
    gates = [send(gate_own, gate_recv.at[k], twin, "kvh") for k, twin in enumerate(twins)]

    text_diag = []
    for k, pieces in enumerate(text_far, 1):
        for piece in pieces:
            piece.wait_recv()
        s, d = slot_of("far", k), slot_of("diag", k)
        text_diag.append((
            send(far_tk.at[s], far_tk.at[d], side), send(far_tv.at[s], far_tv.at[d], side)
        ))

    q_copy.wait_recv()
    for j in range(here):
        attend(visual_keys.at[j], visual_values.at[j], j, (1,))

    for piece in (*text_side, *[p for pieces in text_diag for p in pieces]):
        piece.wait_recv()
    for b in range(blocks):
        span = pl.ds(b * rows, rows)
        cat_k[:, span, :] = text_keys[...] if b == 0 else far_tk[b - 1]
        cat_v[:, span, :] = text_values[...] if b == 0 else far_tv[b - 1]
    count = blocks * rows
    lane = lax.broadcasted_iota(jnp.int32, (rows, count), 1)
    row = lax.broadcasted_iota(jnp.int32, (rows, count), 0)
    key_pos = lane % rows
    for b in range(blocks):
        inside = (lane >= b * rows) & (lane < (b + 1) * rows)
        key_pos = key_pos + jnp.where(inside, places[2 + b], 0)
    biases = [jnp.where(key_pos <= row + places[which], 0.0, NEG) for which in (0, 1)]

    def text_step(i, carry):
        s, g = i // groups, i % groups
        at_g = pl.ds(pl.multiple_of(g * DH, DH), DH)
        k, v = cat_k[s, :, at_g], cat_v[s, :, at_g]
        peak, total, out = softmax_parts(heads_of(queries, s, g), k, v, biases[0])
        put_heads(t_own, (s,), g, out)
        t_own_stat[s, g] = pack_stats(peak, total, rows)
        peak, total, out = softmax_parts(heads_of(q_pair, s, g), k, v, biases[1])
        out = out * (1.0 / jnp.where(total > 0.0, total, 1.0))
        put_heads(t_send, (s,), g, out.astype(jnp.bfloat16))
        t_stat_send[s] = t_stat_send[s] + pltpu.roll(pack_stats(peak, total, rows), g * 8, 1)
        return carry

    lax.fori_loop(0, seqs * groups, text_step, 0)
    text_back = (send(t_send, t_recv, pair), send(t_stat_send, t_stat_recv, pair))

    image_diag = {}

    def forward(j):
        for k in range(1, members):
            s, d = slot_of("far", k), slot_of("diag", k)
            pieces = image_far[k, j]
            pieces[0].wait_recv()
            image_diag[k, j] = [send(far_ik.at[s, j], far_ik.at[d, j], side)]
            for cut, piece in zip(chunks, pieces[1:]):
                piece.wait_recv()
                image_diag[k, j].append(send(far_iv.at[s, j, cut], far_iv.at[d, j, cut], side))

    def attend_far(slot, j, sides=(1, 0)):
        attend(far_ik.at[slot, j], far_iv.at[slot, j], (slot + 1) * here + j, sides)

    for j in range(here):
        for piece in image_side[j]:
            piece.wait_recv()
        attend_far(0, j)
    for j in range(here):
        forward(j)
        for k in range(1, members):
            attend_far(slot_of("far", k), j)
        for k in range(1, members):
            for piece in image_diag[k, j]:
                piece.wait_recv()
            last = j == here - 1 and k == members - 1
            attend_far(slot_of("diag", k), j, (1,) if last else (1, 0))

    row_pos = lax.broadcasted_iota(jnp.int32, (rows, LANES), 0)

    def visual_weights(s, g, which):
        seen, packed = [], []
        for j in range(per_seq):
            seen.append(thresholds[s * per_seq + j] <= row_pos + places[which])
            packed.append(stat[at[s * per_seq + j], which, g])
        peaks = [jnp.where(a, p, NEG) for a, p in zip(seen, packed)]
        overall = functools.reduce(jnp.maximum, peaks)
        weights = [jnp.where(a, jnp.exp(p - overall), 0.0) for a, p in zip(seen, peaks)]
        total = sum(w * totals_of(p) for w, p in zip(weights, packed))
        return overall, total, weights

    def weighted(s, g, which, h, weights):
        start = pl.multiple_of(g * (GROUP * DH), DH)
        return sum(
            w[:, h:h + 1] * num[at[s * per_seq + j], which, :, pl.ds(start + h * DH, DH)]
            for j, w in enumerate(weights)
        )

    def stat_lanes(overall, total):
        lane_id = lax.broadcasted_iota(jnp.int32, (rows, LANES), 1)
        packed = jnp.where(lane_id < HALF, overall, pltpu.roll(total, HALF, 1))
        return jnp.where(lane_id % HALF < GROUP, packed, 0.0)

    visual_back = []
    for s in range(seqs):
        def pair_step(g, carry, s=s):
            overall, total, weights = visual_weights(s, g, 1)
            inverse = 1.0 / jnp.where(total > 0.0, total, 1.0)
            weights = [w * inverse for w in weights]
            start = pl.multiple_of(g * (GROUP * DH), DH)
            for h in range(GROUP):
                v_send[s, :, pl.ds(start + h * DH, DH)] = weighted(s, g, 1, h, weights).astype(
                    jnp.bfloat16
                )
            v_stat_send[s] = v_stat_send[s] + pltpu.roll(stat_lanes(overall, total), g * 8, 1)
            return carry

        lax.fori_loop(0, groups, pair_step, 0)
        visual_back.append((
            send(v_send.at[s], v_recv.at[s], pair), send(v_stat_send.at[s], v_stat_recv.at[s], pair)
        ))

    attend_far(slot_of("diag", members - 1), here - 1, (0,))

    for piece in gates:
        piece.wait_recv()
    for s in range(seqs):
        logits = gate_own[s]
        for k in range(len(twins)):
            logits = logits + gate_recv[k, s]
        heads = groups * GROUP
        mine = logits[:, :heads]
        for c in range(1, heads_split):
            mine = jnp.where(core == c, logits[:, c * heads:(c + 1) * heads], mine)
        mine = jax.nn.sigmoid(mine)
        for g in range(groups):
            gate_buf[s, g, :, :GROUP] = mine[:, g * GROUP:(g + 1) * GROUP]

    for piece in text_back:
        piece.wait_recv()

    def unpacked(packed, g):
        return pltpu.roll(packed, LANES - g * 8, 1)

    def text_merge(i, carry):
        s, g = i // groups, i % groups
        ours, theirs = t_own_stat[s, g], unpacked(t_stat_recv[s], g)
        overall = jnp.maximum(ours, theirs)
        weight_a = jnp.exp(ours - overall)
        weight_b = jnp.exp(theirs - overall) * totals_of(theirs)
        inverse = 1.0 / (weight_a * totals_of(ours) + weight_b)
        weight_a, weight_b = weight_a * inverse, weight_b * inverse
        start = pl.multiple_of(g * (GROUP * DH), DH)
        for h in range(GROUP):
            cut = pl.ds(start + h * DH, DH)
            t_own[s, :, cut] = weight_a[:, h:h + 1] * t_own[s, :, cut] + weight_b[
                :, h:h + 1
            ] * t_recv[s, :, cut].astype(jnp.float32)
        return carry

    lax.fori_loop(0, seqs * groups, text_merge, 0)

    for s in range(seqs):
        for piece in visual_back[s]:
            piece.wait_recv()

        def own_step(g, carry, s=s):
            overall, total, weights = visual_weights(s, g, 0)
            theirs = unpacked(v_stat_recv[s], g)
            joint = jnp.maximum(overall, theirs)
            weight_a = jnp.exp(overall - joint)
            weight_b = jnp.exp(theirs - joint) * totals_of(theirs)
            inverse = 1.0 / (weight_a * total + weight_b)
            weights = [w * (weight_a * inverse) for w in weights]
            weight_b = weight_b * inverse
            start = pl.multiple_of(g * (GROUP * DH), DH)
            for h in range(GROUP):
                cut = pl.ds(start + h * DH, DH)
                visual = weighted(s, g, 0, h, weights) + weight_b[:, h:h + 1] * v_recv[
                    s, :, cut
                ].astype(jnp.float32)
                gate = gate_buf[s, g, :, h:h + 1]
                out_ref[s, :, cut] = ((1.0 - gate) * t_own[s, :, cut] + gate * visual).astype(
                    jnp.bfloat16
                )
            return carry

        lax.fori_loop(0, groups, own_step, 0)

    for copy in copies:
        copy.wait_send()


def pair_plan(n, heads_split, queries, text_keys, text_values, visual_keys, visual_values,
              gate_weight, text_offsets, image_sequence, image_position):
    seqs, rows, columns = queries.shape
    groups = text_keys.shape[-1] // DH
    here, tokens, kv_columns = visual_keys.shape
    members, blocks = n // 4, n // 2
    slots = blocks * here
    per_seq = image_sequence.shape[0] // seqs
    smem = pl.BlockSpec(memory_space=pltpu.SMEM)
    vmem = pl.BlockSpec(memory_space=pltpu.VMEM)
    bf16, f32 = jnp.bfloat16, jnp.float32
    count = 1 + 4 * (members - 1) + 2 + here * (2 * (members - 1) * (1 + len(chunks_of(tokens))) + 2) + 2 + 2 * seqs + heads_split - 1
    stats = (seqs, groups, rows, LANES)
    sent_stats = (seqs, rows, LANES)
    gate_shape = (seqs, rows, gate_weight.shape[-1])
    pairs = 2 * rows * GROUP * groups * (slots * tokens + seqs * blocks * rows)
    return pl.pallas_call(
        functools.partial(attention_kernel, n, heads_split, seqs, rows, groups, here, per_seq),
        in_specs=[smem] * 3 + [vmem] * 6,
        out_specs=vmem,
        out_shape=jax.ShapeDtypeStruct(queries.shape, bf16),
        scratch_shapes=[
            pltpu.VMEM(queries.shape, bf16),
            pltpu.VMEM((blocks - 1, *text_keys.shape), bf16),
            pltpu.VMEM((blocks - 1, *text_keys.shape), bf16),
            pltpu.VMEM((blocks - 1, *visual_keys.shape), bf16),
            pltpu.VMEM((blocks - 1, *visual_keys.shape), bf16),
            pltpu.VMEM((slots, 2, rows, columns), f32),
            pltpu.VMEM((slots, 2, groups, rows, LANES), f32),
            pltpu.VMEM((seqs, blocks * rows, kv_columns), bf16),
            pltpu.VMEM((seqs, blocks * rows, kv_columns), bf16),
            pltpu.VMEM(queries.shape, bf16),
            pltpu.VMEM(sent_stats, f32),
            pltpu.VMEM(queries.shape, bf16),
            pltpu.VMEM(sent_stats, f32),
            pltpu.VMEM(queries.shape, bf16),
            pltpu.VMEM(sent_stats, f32),
            pltpu.VMEM(queries.shape, bf16),
            pltpu.VMEM(sent_stats, f32),
            pltpu.VMEM(queries.shape, f32),
            pltpu.VMEM(stats, f32),
            pltpu.VMEM(gate_shape, f32),
            pltpu.VMEM((heads_split - 1, *gate_shape), f32),
            pltpu.VMEM(stats, f32),
            pltpu.SemaphoreType.DMA((count,)),
            pltpu.SemaphoreType.DMA((count,)),
        ],
        compiler_params=pltpu.CompilerParams(
            collective_id=0, has_side_effects=True, vmem_limit_bytes=60 << 20
        ),
        cost_estimate=pl.CostEstimate(
            flops=4 * pairs * DH, bytes_accessed=16 << 20, transcendentals=pairs
        ),
    )(
        text_offsets, image_sequence, image_position,
        queries, text_keys, text_values, visual_keys, visual_values, gate_weight.T,
    )


def line_kernel(
    seqs, rows, here, per_seq, heads_split,
    offsets, image_sequence, image_position,
    queries, text_keys, text_values, visual_keys, visual_values, gate_weight,
    out_ref,
    q_own, q_mate, q_out, tkv, tkv_out, vk, vv, k_out, v_out, part, part_mate, stat, stat_mate,
    side_part, side_stat, late_part, late_mate, late_stat, late_mate_stat, late_side, late_side_stat,
    t_own, t_send, t_recv, early, gate_own, gate_recv, gate_buf, weights, send_sems, recv_sems,
):
    me = lax.axis_index("seq")
    core = lax.axis_index("kvh")
    z, x = me // 2, me % 2
    half = z // 2
    inner = (z + 1) // 2 % 2
    side = z * 2 + 1 - x
    mate = (half * 2 + 1 - z % 2) * 2 + x
    cross = (3 - z) * 2 + x
    diag = (half * 2 + 1 - z % 2) * 2 + 1 - x
    twins = [(core + k) % heads_split for k in range(1, heads_split)]
    width = GROUP * DH
    group = 2 * here
    slots = 4 * group
    near, outer, across, far = 0, 1, 2, 3
    mine = 1 - inner

    def chip(kind):
        place = jnp.where(kind == outer, 3 * half, 1 + half)
        place = jnp.where(kind == across, 2 - half, place)
        return jnp.where(kind == far, 3 - 3 * half, place)

    def device(kind, sub):
        return chip(kind) * 2 + (x + sub) % 2

    def image_of(slot):
        return device(slot // group, slot // here % 2) * here + slot % here

    last = slots - 1
    lates = (last, last - here)

    barrier = pltpu.get_barrier_semaphore()
    for peer in (side, mate, cross, diag):
        pl.semaphore_signal(
            barrier, inc=1, device_id={"seq": peer}, device_id_type=pl.DeviceIdType.MESH
        )
    for twin in twins:
        pl.semaphore_signal(
            barrier, inc=1, device_id={"kvh": twin}, device_id_type=pl.DeviceIdType.MESH
        )

    bases, used = {}, 0
    for name, count in (
        ("x_text", 1), ("x_q", 1), ("x_k", here), ("x_v", here), ("x_t", 1), ("x_part", slots),
        ("x_stat", slots), ("late", 6), ("edge", 3), ("m_text", 8), ("m_q", 2), ("m_k", slots), ("m_v", slots),
        ("m_part", slots), ("m_stat", slots), ("c_text", 8), ("c_k", slots), ("c_v", slots),
        ("gate", heads_split),
    ):
        bases[name] = used
        used += count

    def copy(name, index, src, dst, peer, axis="seq"):
        return pltpu.make_async_remote_copy(
            src_ref=src,
            dst_ref=dst,
            send_sem=send_sems.at[bases[name] + index],
            recv_sem=recv_sems.at[bases[name] + index],
            device_id={axis: peer},
            device_id_type=pl.DeviceIdType.MESH,
        )

    x_text = copy("x_text", 0, tkv_out, tkv.at[mine, 1], side)
    x_q = copy("x_q", 0, q_out, q_own.at[:, 1], side)
    away = pl.multiple_of((1 - x) * DH, DH)

    def x_k(j):
        return copy("x_k", j, k_out.at[j], vk.at[mine * group + here + j], side)

    def x_v(j):
        return copy("x_v", j, v_out.at[j], vv.at[mine * group + here + j], side)

    x_t = copy("x_t", 0, t_send, t_recv, side)

    def x_part(i):
        return copy("x_part", i, part.at[i, 1], side_part.at[i], side)

    def x_stat(i):
        return copy("x_stat", i, stat.at[i], side_stat.at[i], side)

    def m_text(kind, sub):
        return copy("m_text", kind * 2 + sub, tkv.at[kind, sub], tkv.at[kind, sub], mate)

    def m_q(sub):
        return copy("m_q", sub, q_own.at[:, sub], q_mate.at[:, sub], mate)

    def m_k(i):
        return copy("m_k", i, vk.at[i], vk.at[i], mate)

    def m_v(i):
        return copy("m_v", i, vv.at[i], vv.at[i], mate)

    def m_part(i):
        return copy("m_part", i, part_mate.at[i], part.at[i], mate)

    def m_stat(i):
        return copy("m_stat", i, stat_mate.at[i], stat.at[i], mate)

    def c_text(kind, sub):
        return copy("c_text", (kind + 2) * 2 + sub, tkv.at[kind, sub], tkv.at[kind + 2, sub], cross)

    def c_k(i):
        return copy("c_k", i, vk.at[i], vk.at[i + 2 * group], cross)

    def c_v(i):
        return copy("c_v", i, vv.at[i], vv.at[i + 2 * group], cross)

    late_own = (
        copy("late", 1, late_stat, late_side_stat, side),
        copy("late", 0, late_part.at[1], late_side, side),
    )
    late_to_mate = (
        copy("late", 3, late_mate_stat, late_stat, mate),
        copy("late", 2, late_mate.at[0], late_part.at[0], mate),
    )
    late_to_diag = (
        copy("late", 5, late_mate_stat, late_side_stat, diag),
        copy("late", 4, late_mate.at[1], late_side, diag),
    )

    edge = last - 1
    edge_to_mate = (
        copy("edge", 0, part_mate.at[edge, 0], part.at[edge, 0], mate),
        copy("m_stat", edge, stat_mate.at[edge], stat.at[edge], mate),
    )
    edge_to_diag = (
        copy("edge", 1, part_mate.at[edge, 1], side_part.at[edge], diag),
        copy("edge", 2, stat_mate.at[edge], side_stat.at[edge], diag),
    )

    home = pl.multiple_of(x * DH, DH)
    home_q = x * width
    away_q = (1 - x) * width

    def stack_q(s, carry):
        for h in range(GROUP):
            q_own[s, 0, h] = queries[s, :, pl.ds(pl.multiple_of(home_q + h * DH, DH), DH)]
            q_out[s, h] = queries[s, :, pl.ds(pl.multiple_of(away_q + h * DH, DH), DH)]
        return carry

    for kind, source in enumerate((text_keys, text_values)):
        tkv[mine, 0, kind] = source[:, :, pl.ds(home, DH)]
        tkv_out[kind] = source[:, :, pl.ds(away, DH)]
    lax.fori_loop(0, seqs, stack_q, 0)
    def keep_home(j):
        vk[mine * group + j] = visual_keys[:, j, pl.ds(home, DH)]
        vv[mine * group + j] = visual_values[:, j, pl.ds(home, DH)]

    def keep_away(j):
        k_out[j] = visual_keys[:, j, pl.ds(away, DH)]
        v_out[j] = visual_values[:, j, pl.ds(away, DH)]

    keep_home(0)
    pl.semaphore_wait(barrier, 4 + len(twins))

    x_text.start()
    x_q.start()

    @pl.when(inner == 1)
    def _():
        c_text(near, 0).start()
        m_text(near, 0).start()
        c_k(0).start()
        c_v(0).start()
        m_k(0).start()
        m_v(0).start()

    @pl.when(inner == 0)
    def _():
        m_text(outer, 0).start()
        m_k(group).start()

    for j in range(here):
        if j:
            keep_home(j)
        keep_away(j)
        x_k(j).start()
        x_v(j).start()

    lane = lax.broadcasted_iota(jnp.int32, (rows, LANES), 1)

    def softmax(scores):
        peak = jnp.max(scores, axis=-1, keepdims=True)
        return peak, jnp.exp2((scores - peak) * SCALE2).astype(jnp.bfloat16)

    def scores_of(q, k):
        return lax.dot_general(q, k, (((1,), (1,)), ((), ())), preferred_element_type=jnp.float32)

    def attend(i, q_ref, part_ref, stat_ref):
        attend_to(i, q_ref, part_ref.at[i], stat_ref.at[i])

    def attend_to(i, q_ref, part_ref, stat_ref):
        apply_values(i, apply_keys(i, q_ref), part_ref, stat_ref)

    def apply_keys(i, q_ref):
        q = q_ref[image_sequence[image_of(i)]].reshape(2, GROUP * rows, DH)
        k = vk[i]
        scores = [scores_of(q[0], k), scores_of(q[1], k)]
        return [softmax(scores[0]), softmax(scores[1])]

    def apply_values(i, halves, part_ref, stat_ref):
        v = vv[i]
        v = jnp.concatenate([v, jnp.ones_like(v)], axis=1)
        packed = []
        for b in range(2):
            peak, expd = halves[b]
            num = jnp.dot(expd, v, preferred_element_type=jnp.float32)
            total = num[:, DH:]
            part_ref[b] = (num[:, :DH] * (1.0 / total)).astype(jnp.bfloat16).reshape(GROUP, rows, DH)
            peaks = jnp.zeros((rows, LANES), jnp.float32)
            totals = jnp.ones((rows, LANES), jnp.float32)
            for h in range(GROUP):
                at_h = slice(h * rows, (h + 1) * rows)
                peaks = jnp.where(lane == h, peak[at_h], peaks)
                totals = jnp.where(lane == h, total[at_h], totals)
            packed.append(peaks * SCALE + jnp.log(totals))
        stat_ref[...] = jnp.concatenate(packed, axis=0).T[:8]

    def attend_own(i):
        attend(i, q_own, part, stat)
        x_part(i).start()
        x_stat(i).start()

    def attend_mate(i):
        attend(i, q_mate, part_mate, stat_mate)

        @pl.when(i != edge)
        def _():
            m_part(i).start()
            m_stat(i).start()

        @pl.when(i == edge)
        def _():
            for piece in (*edge_to_mate, *edge_to_diag):
                piece.start()

    def loop(start, stop, body):
        def step(i, carry):
            body(i)
            return carry

        lax.fori_loop(start, stop, step, 0)

    @pl.when(inner == 1)
    def _():
        x_text.wait_recv()
        c_text(near, 1).start()
        m_text(near, 1).start()
        for j in range(1, here):
            m_k(j).start()
            m_v(j).start()
        for sub in range(2):
            m_text(outer, sub).wait_recv()
            c_text(outer, sub).start()
        for j in range(1, here):
            c_k(j).start()
            c_v(j).start()
        c_text(near, 0).wait_recv()
        m_text(across, 0).start()

    @pl.when(inner == 0)
    def _():
        x_text.wait_recv()
        m_text(outer, 1).start()
        m_q(0).start()

    rest = gate_weight[...]
    q_all = queries[...].reshape(seqs * rows, queries.shape[-1])
    logits = 0.0
    for _ in range(3):
        term = rest.astype(jnp.bfloat16)
        rest = rest - term.astype(jnp.float32)
        logits = logits + lax.dot_general(
            q_all, term, (((1,), (1,)), ((), ())), preferred_element_type=jnp.float32
        )
    gate_own[...] = logits.reshape(gate_own.shape)
    gates = [copy("gate", k, gate_own, gate_recv.at[k], twin, "kvh") for k, twin in enumerate(twins)]
    for piece in gates:
        piece.start()


    x_q.wait_recv()

    @pl.when(inner == 1)
    def _():
        loop(0, here, attend_own)
        c_text(near, 1).wait_recv()
        m_text(across, 1).start()
        x_k(0).wait_recv()
        c_k(here).start()
        for sub in range(2):
            c_text(outer, sub).wait_recv()
            m_text(far, sub).start()
        x_v(0).wait_recv()
        c_v(here).start()

    @pl.when(inner == 0)
    def _():
        m_q(1).start()
        m_v(group).start()
        for j in range(1, here):
            m_k(group + j).start()
            m_v(group + j).start()
        loop(group, group + here, attend_own)
        for j in range(here):
            x_k(j).wait_recv()
            m_k(group + here + j).start()
            x_v(j).wait_recv()
            m_v(group + here + j).start()
        for kind in (near, across, far):
            for sub in range(2):
                m_text(kind, sub).wait_recv()

    count = 8 * rows
    key_lane = lax.broadcasted_iota(jnp.int32, (rows, count), 1)
    key_row = lax.broadcasted_iota(jnp.int32, (rows, count), 0)
    key_pos = key_lane % rows
    for kind in range(4):
        for sub in range(2):
            b = kind * 2 + sub
            inside = (key_lane >= b * rows) & (key_lane < (b + 1) * rows)
            key_pos = key_pos + jnp.where(inside, offsets[device(kind, sub)], 0)
    place = [offsets[me], offsets[side]]
    biases = [jnp.where(key_pos <= key_row + p, 0.0, NEG) for p in place]

    def text_step(s):
        q = q_own[s].reshape(2, GROUP * rows, DH)
        k = tkv[:, :, 0, s].reshape(count, DH)
        v = tkv[:, :, 1, s].reshape(count, DH)
        v = jnp.concatenate([v, jnp.ones_like(v)], axis=1)
        for b in range(2):
            scores = scores_of(q[b], k).reshape(GROUP, rows, count) + biases[b][None]
            peak, expd = softmax(scores.reshape(GROUP * rows, count))
            num = jnp.dot(expd, v, preferred_element_type=jnp.float32)
            out = (num[:, :DH] * (1.0 / num[:, DH:])).reshape(GROUP, rows, DH)
            if b == 0:
                t_own[0, s] = out
            else:
                t_send[s] = out.astype(jnp.bfloat16)

    loop(0, seqs, text_step)
    x_t.start()

    @pl.when(inner == 1)
    def _():
        for j in range(1, here):
            x_k(j).wait_recv()
            c_k(here + j).start()
            x_v(j).wait_recv()
            c_v(here + j).start()

    for piece in gates:
        piece.wait_recv()
    for s in range(seqs):
        logits = gate_own[s]
        for k in range(len(twins)):
            logits = logits + gate_recv[k, s]
        heads = 2 * GROUP
        mix = logits[:, :heads]
        for c in range(1, heads_split):
            mix = jnp.where(core == c, logits[:, c * heads:(c + 1) * heads], mix)
        mix = jax.nn.sigmoid(mix)
        for g in range(2):
            gate_buf[s, g, :, :GROUP] = mix[:, g * GROUP:(g + 1) * GROUP]

    @pl.when(inner == 1)
    def _():
        for sub in range(2):
            m_q(sub).wait_recv()

        def own_step(i):
            attend_mate(i)
            attend_own(i)

        loop(here, group, own_step)

    owners = [image_sequence[image_of(jnp.int32(i))] for i in range(slots)]
    positions = [image_position[image_of(jnp.int32(i))] for i in range(slots)]

    def table(late):
        at, thresholds = [], []
        for s in range(seqs):
            slot_here = [jnp.int32(0)] * per_seq
            threshold_here = [jnp.int32(FAR)] * per_seq
            found = jnp.int32(0)
            for slot, (owner, position) in enumerate(zip(owners, positions)):
                if slot == late:
                    continue
                hit = owner == s
                for j in range(per_seq):
                    take = hit & (found == j)
                    slot_here[j] = jnp.where(take, slot, slot_here[j])
                    threshold_here[j] = jnp.where(take, position, threshold_here[j])
                found = found + jnp.where(hit, 1, 0)
            at += slot_here
            thresholds += threshold_here
        return at, thresholds

    tables = [table(late) for late in lates]

    @pl.when(inner == 1)
    def _():
        def stream_step(c):
            @pl.when((c >= here) & (c < here + group))
            def _():
                o = group + c - here
                m_k(o).wait_recv()
                c_k(o).start()
                m_v(o).wait_recv()
                c_v(o).start()

            c_k(c).wait_recv()
            c_v(c).wait_recv()
            attend_mate(2 * group + c)
            attend_own(2 * group + c)

            @pl.when((c >= here) & (c < here + group))
            def _():
                attend_own(group + c - here)

        loop(0, 2 * group - 1, stream_step)

    @pl.when(inner == 0)
    def _():
        loop(group + here, 2 * group, attend_own)
        for j in range(here):
            m_k(j).wait_recv()
            m_v(j).wait_recv()
        loop(0, here, attend_own)

        def forward(i):
            m_part(i).wait_recv()
            m_stat(i).wait_recv()
            x_part(i).start()
            x_stat(i).start()

        loop(here, group, forward)
        loop(2 * group, edge, forward)
        for piece in edge_to_mate:
            piece.wait_recv()


    row_pos = lax.broadcasted_iota(jnp.int32, (rows, LANES), 0) + place[0]
    real = lane % 8 < GROUP

    def spread(values, join):
        stride = 8
        while stride < 8 * per_seq:
            up = pltpu.roll(values, LANES - stride, 1)
            down = pltpu.roll(values, stride, 1)
            values = join(values, jnp.where(lane // stride % 2 == 0, up, down))
            stride *= 2
        return values

    def lanes_of(choices, size):
        limits = jnp.full((rows, LANES), FAR, jnp.int32)
        for i, threshold in enumerate(choices):
            limits = jnp.where(lane // size == i, threshold, limits)
        return (limits <= row_pos) & real

    def early_merge(g):
        absolute = x if g == 0 else 1 - x
        at, thresholds = tables[g]
        if g == 1:
            at = [i + here * (1 - 2 * (i // here % 2)) for i in at]
        seen = lanes_of(thresholds, 8)
        gathered = jnp.concatenate([(stat, side_stat)[g][i] for i in at], axis=0).T
        lse = jnp.where(seen, gathered[g * rows:(g + 1) * rows], NEG)
        overall = spread(lse, jnp.maximum)
        weight = jnp.where(seen, jnp.exp(lse - overall), 0.0)
        total = spread(weight, jnp.add)
        gate = 0.0
        for s in range(seqs):
            here_gate = jnp.where(lane < GROUP, gate_buf[s, absolute], 0.0)
            gate = gate + (pltpu.roll(here_gate, s * per_seq * 8, 1) if s else here_gate)
        gate = spread(gate, jnp.add)
        weights[g, 0] = overall
        weights[g, 1] = total
        weights[g, 2] = gate
        weights[g, 3] = weight * (gate / jnp.where(total > 0.0, total, 1.0))
        for s in range(seqs):
            for h in range(GROUP):
                visual = 0.0
                for j in range(per_seq):
                    i = at[s * per_seq + j]
                    piece = part[i, 0, h] if g == 0 else side_part[i, h]
                    k = (s * per_seq + j) * 8 + h
                    visual = visual + weights[g, 3, :, k:k + 1] * piece.astype(jnp.float32)
                early[g, s, h] = visual
                k = s * per_seq * 8 + h
                text = t_own[g, s, h] if g == 0 else t_recv[s, h].astype(jnp.float32)
                t_own[g, s, h] = (1.0 - weights[g, 2, :, k:k + 1]) * text

    def late_weights(g):
        late = image_of(jnp.int32(lates[g]))
        limits = [jnp.where(image_sequence[late] == s, image_position[late], FAR) for s in range(seqs)]
        seen = lanes_of(limits, 8 * per_seq)
        source = (late_stat, late_side_stat)[g][...]
        gathered = jnp.concatenate([source] * (LANES // 8), axis=0).T
        lse = jnp.where(seen, gathered[g * rows:(g + 1) * rows], NEG)
        before = weights[g, 0]
        overall = jnp.maximum(before, lse)
        weight_a = jnp.where(weights[g, 1] > 0.0, weights[g, 1] * jnp.exp(before - overall), 0.0)
        weight_b = jnp.where(seen, jnp.exp(lse - overall), 0.0)
        total = weight_a + weight_b
        inverse = 1.0 / jnp.where(total > 0.0, total, 1.0)
        weights[g, 0] = weight_a * inverse
        weights[g, 1] = weight_b * inverse * weights[g, 2]
        for s in range(seqs):
            for h in range(GROUP):
                k = s * per_seq * 8 + h
                early[g, s, h] = t_own[g, s, h] + weights[g, 0, :, k:k + 1] * early[g, s, h]

    def late_apply(g):
        absolute = x if g == 0 else 1 - x
        for h in range(GROUP):
            piece = (late_part[0, h] if g == 0 else late_side[h]).astype(jnp.float32)
            cut = pl.ds(pl.multiple_of(absolute * width + h * DH, DH), DH)
            for s in range(seqs):
                k = s * per_seq * 8 + h
                out_ref[s, :, cut] = (
                    early[g, s, h] + weights[g, 1, :, k:k + 1] * piece
                ).astype(jnp.bfloat16)

    def receive(i):
        x_part(i).wait_recv()
        x_stat(i).wait_recv()

    early_merge(0)

    @pl.when(inner == 1)
    def _():
        c_k(2 * group - 1).wait_recv()
        mate_halves = apply_keys(last, q_mate)
        own_halves = apply_keys(last, q_own)
        c_v(2 * group - 1).wait_recv()
        apply_values(last, mate_halves, late_mate, late_mate_stat)
        for piece in (late_to_mate[0], late_to_diag[0], late_to_mate[1], late_to_diag[1]):
            piece.start()
        apply_values(last, own_halves, late_part, late_stat)
        for piece in late_own:
            piece.start()

    loop(0, edge, receive)

    @pl.when(inner == 1)
    def _():
        receive(edge)

    @pl.when(inner == 0)
    def _():
        for piece in edge_to_diag:
            piece.wait_recv()

    x_t.wait_recv()
    early_merge(1)

    def arrive(index):
        @pl.when(inner == 0)
        def _():
            late_to_diag[index].wait_recv()

        @pl.when(inner == 1)
        def _():
            late_own[index].wait_recv()

    @pl.when(inner == 0)
    def _():
        late_to_mate[0].wait_recv()

    late_weights(0)
    arrive(0)
    late_weights(1)

    @pl.when(inner == 0)
    def _():
        late_to_mate[1].wait_recv()

    late_apply(0)
    arrive(1)
    late_apply(1)

    def sent(piece):
        piece.wait_send()

    sent(x_text)
    sent(x_q)
    sent(x_t)
    for j in range(here):
        sent(x_k(j))
        sent(x_v(j))
    for piece in gates:
        sent(piece)

    def all_sent(i):
        sent(x_part(i))
        sent(x_stat(i))

    loop(0, edge, all_sent)

    @pl.when(inner == 1)
    def _():
        for sub in range(2):
            for kind in (near, outer):
                sent(c_text(kind, sub))
            for kind in (near, across, far):
                sent(m_text(kind, sub))
        for j in range(here):
            sent(m_k(j))
            sent(m_v(j))

        def stream_sent(i):
            sent(c_k(i))
            sent(c_v(i))

        def mate_sent(i):
            sent(m_part(i))
            sent(m_stat(i))

        loop(0, 2 * group, stream_sent)
        loop(here, group, mate_sent)
        loop(2 * group, edge, mate_sent)
        all_sent(edge)
        for piece in (*edge_to_mate, *edge_to_diag, *late_to_mate, *late_to_diag, *late_own):
            sent(piece)

    @pl.when(inner == 0)
    def _():
        for sub in range(2):
            sent(m_text(outer, sub))
            sent(m_q(sub))

        def stream_sent(i):
            sent(m_k(i))
            sent(m_v(i))

        loop(group, 2 * group, stream_sent)


def line_plan(heads_split, queries, text_keys, text_values, visual_keys, visual_values,
              gate_weight, text_offsets, image_sequence, image_position):
    seqs, rows, columns = queries.shape
    here, tokens, _ = visual_keys.shape
    slots = image_sequence.shape[0]
    per_seq = slots // seqs
    smem = pl.BlockSpec(memory_space=pltpu.SMEM)
    vmem = pl.BlockSpec(memory_space=pltpu.VMEM)
    bf16, f32 = jnp.bfloat16, jnp.float32
    stacked = (seqs, 2, GROUP, rows, DH)
    one = (seqs, GROUP, rows, DH)
    gate_shape = (seqs, rows, gate_weight.shape[-1])
    count = 2 + 2 * here + 1 + 2 * slots + 6 + 3 + 10 + 4 * slots + 8 + 2 * slots + heads_split
    pairs = 2 * rows * GROUP * (2 * slots * tokens + seqs * 8 * rows)
    mixed = pl.pallas_call(
        functools.partial(line_kernel, seqs, rows, here, per_seq, heads_split),
        in_specs=[smem] * 3 + [vmem] * 6,
        out_specs=vmem,
        out_shape=jax.ShapeDtypeStruct(queries.shape, bf16),
        scratch_shapes=[
            pltpu.VMEM(stacked, bf16),
            pltpu.VMEM(stacked, bf16),
            pltpu.VMEM(one, bf16),
            pltpu.VMEM((4, 2, 2, seqs, rows, DH), bf16),
            pltpu.VMEM((2, seqs, rows, DH), bf16),
            pltpu.VMEM((slots, tokens, DH), bf16),
            pltpu.VMEM((slots, tokens, DH), bf16),
            pltpu.VMEM((here, tokens, DH), bf16),
            pltpu.VMEM((here, tokens, DH), bf16),
            pltpu.VMEM((slots, 2, GROUP, rows, DH), bf16),
            pltpu.VMEM((slots, 2, GROUP, rows, DH), bf16),
            pltpu.VMEM((slots, 8, LANES), f32),
            pltpu.VMEM((slots, 8, LANES), f32),
            pltpu.VMEM((slots, GROUP, rows, DH), bf16),
            pltpu.VMEM((slots, 8, LANES), f32),
            pltpu.VMEM((2, GROUP, rows, DH), bf16),
            pltpu.VMEM((2, GROUP, rows, DH), bf16),
            pltpu.VMEM((8, LANES), f32),
            pltpu.VMEM((8, LANES), f32),
            pltpu.VMEM((GROUP, rows, DH), bf16),
            pltpu.VMEM((8, LANES), f32),
            pltpu.VMEM((2, *one), f32),
            pltpu.VMEM(one, bf16),
            pltpu.VMEM(one, bf16),
            pltpu.VMEM((2, *one), f32),
            pltpu.VMEM(gate_shape, f32),
            pltpu.VMEM((heads_split - 1, *gate_shape), f32),
            pltpu.VMEM((seqs, 2, rows, LANES), f32),
            pltpu.VMEM((2, 4, rows, LANES), f32),
            pltpu.SemaphoreType.DMA((count,)),
            pltpu.SemaphoreType.DMA((count,)),
        ],
        compiler_params=pltpu.CompilerParams(
            collective_id=1, has_side_effects=True, vmem_limit_bytes=60 << 20
        ),
        cost_estimate=pl.CostEstimate(
            flops=4 * pairs * DH, bytes_accessed=16 << 20, transcendentals=pairs
        ),
    )(
        text_offsets, image_sequence, image_position,
        queries, text_keys, text_values,
        visual_keys.transpose(1, 0, 2), visual_values.transpose(1, 0, 2), gate_weight.T,
    )

    def hand_over(source, out_ref):
        out_ref[...] = source[...]

    return pl.pallas_call(
        hand_over,
        in_specs=[vmem],
        out_specs=vmem,
        out_shape=jax.ShapeDtypeStruct(queries.shape, bf16),
    )(mixed)


def on_device(n, heads_split, queries, text_keys, *rest):
    groups = text_keys.shape[-1] // DH
    images = rest[-2].shape[0]
    line = n // 2
    if line - 2 == 2 and groups == 2 and images * 8 == LANES and 2 * queries.shape[1] == LANES:
        return line_plan(heads_split, queries, text_keys, *rest)
    return pair_plan(n, heads_split, queries, text_keys, *rest)


def solution(mesh):
    return jax.shard_map(
        functools.partial(on_device, mesh.shape["seq"], mesh.shape["kvh"]),
        mesh=mesh,
        in_specs=(
            P("batch", "seq", "kvh"),
            P("batch", "seq", "kvh"),
            P("batch", "seq", "kvh"),
            P(("batch", "seq"), None, "kvh"),
            P(("batch", "seq"), None, "kvh"),
            P("kvh", None),
            P("batch"),
            P("batch"),
            P("batch"),
        ),
        out_specs=P("batch", "seq", "kvh"),
        check_vma=False,
    )
```
